32 devices in a mesh: pages: 2 (over y), tile: 4 (over z), mp: 2 (over x), batch: 2 (over core).
Axes of the slice: x: 2, y: 2, z: 4, core: 2. Of those that a mesh axis runs over, the one named last changes fastest.
Arguments:
- page_cells: bfloat16 [4, 48, 24, 1024], P(('pages', 'batch'), 'tile'), parts along dimension 0, may hold values from -40 to 40
- text_states: bfloat16 [4, 1024, 1024], P(('pages', 'batch'), 'tile'), parts along dimension 0, may hold values from -40 to 40
- enc_query: bfloat16 [1024, 1024], P('batch', 'mp'), may hold values from -2.5 to 2.5
- enc_keyval: bfloat16 [1024, 2, 1024], P('batch', None, 'mp'), may hold values from -0.1875 to 0.1875
- enc_proj: bfloat16 [1024, 1024], P('mp', 'batch'), may hold values from -0.1875 to 0.1875
- dec_query: bfloat16 [1024, 1024], P('batch', 'mp'), may hold values from -2.5 to 2.5
- dec_keyval: bfloat16 [1024, 2, 1024], P('batch', None, 'mp'), may hold values from -0.1875 to 0.1875
- dec_out: bfloat16 [1024, 1024], P('mp', 'batch'), may hold values from -0.1875 to 0.1875
Outputs:
- encoded: bfloat16 [4, 48, 24, 1024], P(('pages', 'batch'), 'tile'), parts along dimension 0
- decoded: bfloat16 [4, 1024, 1024], P(('pages', 'batch'), ('tile', 'mp')), parts along dimension 0
The draws below stay inside these ranges and needn't reach their ends.
There are 2 independent parts, one for each index of `pages`. The reference program is written for one: setup_inputs(seed, part) draws one part's arguments, and reference() takes and returns one part's arrays. A program takes and returns all parts, laid end to end along the dimension named above; an argument that names none is the same for every part. Nothing has to cross between parts.
All inputs are finite; a program needn't handle non-finite values.
Results may differ from the reference program's by a relative error of at most 0.012.
Values may be sent and summed in bfloat16 or wider, within the bound.
No kernel may reach another device: no remote copies, remote signals or barrier semaphores. Data moves between devices by JAX's collectives and lax.ppermute only.
A program may use at most 64 MiB of HBM per device.

```python
import math
import jax
import jax.numpy as jnp
from jax import lax

D = 1024
HEADS_ENC = 32
HEAD_ENC = 32
HEADS_DEC = 16
HEAD_DEC = 64
WIN = 12
COLS = 24
SHIFT = 6
ROWS = 48
PAGES = 2
TEXT = 1024


def log_scales(key, shape, low, high):
    return jnp.exp(jax.random.uniform(key, shape, jnp.float32, math.log(low), math.log(high)))


def feature_draw(key, shape, width):
    base_key, row_key, col_key = jax.random.split(key, 3)
    values = jax.random.normal(base_key, shape, jnp.float32)
    row_scale = log_scales(row_key, shape[:-1] + (1,), 0.3, 3.0)
    col_scale = log_scales(col_key, (width,), 0.3, 3.0)
    return jnp.clip(values * row_scale * col_scale, -40.0, 40.0).astype(jnp.bfloat16)


def query_draw(key, heads, head_size, factor_base):
    base_key = jax.random.fold_in(key, 0)
    values = factor_base * jax.random.normal(base_key, (D, heads * head_size), jnp.float32) / math.sqrt(D)
    return jnp.clip(values, -2.5, 2.5).astype(jnp.bfloat16)


def draw_page_cells(key, part):
    return feature_draw(jax.random.fold_in(key, 101), (PAGES, ROWS, COLS, D), D)


def draw_text_states(key, part):
    return feature_draw(jax.random.fold_in(key, 202), (PAGES, TEXT, D), D)


def draw_enc_query(key, part):
    return query_draw(jax.random.fold_in(key, 303), HEADS_ENC, HEAD_ENC, 2.0)


def draw_dec_query(key, part):
    return query_draw(jax.random.fold_in(key, 404), HEADS_DEC, HEAD_DEC, 2.5)


def shard_levels(rng, shape, cuts, low, top_value):
    factor_of, own = 1.0, jax.random.fold_in(rng, 6)
    for dim, shards_of in cuts:
        draws = jnp.exp(jax.random.uniform(jax.random.fold_in(own, dim), (shards_of,), jnp.float32, low / len(cuts), top_value / len(cuts)))
        factor_of = factor_of * jnp.repeat(draws, shape[dim] // shards_of).reshape([-1 if axis == dim else 1 for axis in range(len(shape))])
    return factor_of


def noise(rng, dims, deviation, limit, shards=(), kind=jnp.bfloat16):
    array = deviation * jax.random.normal(rng, dims, jnp.float32)
    if shards:
        array = array * shard_levels(rng, dims, shards, -0.22, 0.18)
    return jnp.clip(array, -limit, limit).astype(kind)


def setup_inputs(seed: int = 0, part: int = 0) -> dict:
    seeds = jax.random.split(jax.random.key(seed), 9)
    part_splits = jax.random.split(jax.random.fold_in(seeds[8], part), 9)
    page_cells = draw_page_cells(jax.random.fold_in(jax.random.fold_in(seeds[8], part), 71), part)
    text_states = draw_text_states(jax.random.fold_in(jax.random.fold_in(seeds[8], part), 71), part)
    enc_query = draw_enc_query(jax.random.fold_in(seeds[8], 71), part)
    enc_keyval = noise(seeds[3], (D, 2, HEADS_ENC * HEAD_ENC), D ** -0.5, 0.1875, ((0, 2), (2, 2)))
    enc_proj = noise(seeds[4], (HEADS_ENC * HEAD_ENC, D), (HEADS_ENC * HEAD_ENC) ** -0.5, 0.1875, ((0, 2), (1, 2)))
    dec_query = draw_dec_query(jax.random.fold_in(seeds[8], 71), part)
    dec_keyval = noise(seeds[6], (D, 2, HEADS_DEC * HEAD_DEC), D ** -0.5, 0.1875, ((0, 2), (2, 2)))
    dec_out = noise(seeds[7], (HEADS_DEC * HEAD_DEC, D), (HEADS_DEC * HEAD_DEC) ** -0.5, 0.1875, ((0, 2), (1, 2)))
    return {"page_cells": page_cells, "text_states": text_states, "enc_query": enc_query, "enc_keyval": enc_keyval, "enc_proj": enc_proj, "dec_query": dec_query, "dec_keyval": dec_keyval, "dec_out": dec_out}


def layer_norm(values):
    center = values - lax.optimization_barrier(jnp.mean(values, axis=-1, keepdims=True))
    variance = lax.optimization_barrier(jnp.mean(center * center, axis=-1, keepdims=True))
    return center / jnp.sqrt(variance + 1e-05)

def region_of(index_count, length):
    index_row = jnp.arange(length, dtype=jnp.int32)
    return jnp.where(index_row < length - WIN, 0, jnp.where(index_row < length - SHIFT, 1, 2)).astype(jnp.int32)

def to_windows(grid):
    extra = grid.shape[3:]
    shaped = grid.reshape((grid.shape[0], ROWS // WIN, WIN, COLS // WIN, WIN) + extra)
    shaped = jnp.swapaxes(shaped, 2, 3)
    return shaped.reshape((grid.shape[0], ROWS // WIN * (COLS // WIN), WIN * WIN) + extra)

def reference(page_cells, text_states, enc_query, enc_keyval, enc_proj, dec_query, dec_keyval, dec_out):
    hq_enc = HEADS_ENC * HEAD_ENC
    hq_dec = HEADS_DEC * HEAD_DEC
    rolled = jnp.roll(page_cells, (-SHIFT, -SHIFT), axis=(1, 2))
    normed = layer_norm(rolled.astype(jnp.float32)).astype(jnp.bfloat16).reshape(-1, D)
    enc_q = jnp.dot(normed, enc_query, preferred_element_type=jnp.float32).astype(jnp.bfloat16)
    enc_kv = jnp.dot(normed, enc_keyval.reshape(D, 2 * hq_enc), preferred_element_type=jnp.float32).astype(jnp.bfloat16)
    grid_q = enc_q.reshape(PAGES, ROWS, COLS, HEADS_ENC, HEAD_ENC)
    grid_k = enc_kv[:, :hq_enc].reshape(PAGES, ROWS, COLS, HEADS_ENC, HEAD_ENC)
    grid_v = enc_kv[:, hq_enc:].reshape(PAGES, ROWS, COLS, HEADS_ENC, HEAD_ENC)
    win_q = to_windows(grid_q).astype(jnp.float32)
    win_k = to_windows(grid_k).astype(jnp.float32)
    win_v = to_windows(grid_v).astype(jnp.float32)
    labels = region_of(0, ROWS)[:, None] * 3 + region_of(0, COLS)[None, :]
    win_labels = to_windows(labels[None])[0]
    allowed = win_labels[:, :, None] == win_labels[:, None, :]
    win_scores = jnp.einsum('pnqhd,pnkhd->pnhqk', win_q, win_k, precision=lax.Precision.HIGHEST) / math.sqrt(HEAD_ENC)
    win_scores = jnp.where(allowed[None, :, None], win_scores, -jnp.inf)
    top = lax.optimization_barrier(jnp.max(win_scores, axis=-1, keepdims=True))
    expd = jnp.exp(win_scores - top)
    win_weights = (expd / lax.optimization_barrier(jnp.sum(expd, axis=-1, keepdims=True))).astype(jnp.bfloat16)
    win_out = jnp.einsum('pnhqk,pnkhd->pnqhd', win_weights.astype(jnp.float32), win_v, precision=lax.Precision.HIGHEST).astype(jnp.bfloat16)
    win_out = win_out.reshape(PAGES, ROWS // WIN, COLS // WIN, WIN, WIN, hq_enc)
    win_out = jnp.swapaxes(win_out, 2, 3).reshape(PAGES, ROWS, COLS, hq_enc)
    unrolled = jnp.roll(win_out, (SHIFT, SHIFT), axis=(1, 2))
    attended = jnp.dot(unrolled.reshape(-1, hq_enc), enc_proj, preferred_element_type=jnp.float32)
    encoded = (page_cells.reshape(-1, D).astype(jnp.float32) + attended).astype(jnp.bfloat16)
    page_normed = layer_norm(encoded.astype(jnp.float32)).astype(jnp.bfloat16)
    page_kv = jnp.dot(page_normed, dec_keyval.reshape(D, 2 * hq_dec), preferred_element_type=jnp.float32).astype(jnp.bfloat16)
    keys = page_kv[:, :hq_dec].reshape(PAGES, ROWS * COLS, HEADS_DEC, HEAD_DEC)
    values = page_kv[:, hq_dec:].reshape(PAGES, ROWS * COLS, HEADS_DEC, HEAD_DEC)
    text_normed = layer_norm(text_states.astype(jnp.float32)).astype(jnp.bfloat16).reshape(-1, D)
    queries = jnp.dot(text_normed, dec_query, preferred_element_type=jnp.float32).astype(jnp.bfloat16)
    queries = queries.reshape(PAGES, TEXT, HEADS_DEC, HEAD_DEC)

    def head_attention(operands):
        head_q, head_k, head_v = operands
        cross_scores = jnp.einsum('ptd,pkd->ptk', head_q.astype(jnp.float32), head_k.astype(jnp.float32), precision=lax.Precision.HIGHEST) / math.sqrt(HEAD_DEC)
        row_top = lax.optimization_barrier(jnp.max(cross_scores, axis=-1, keepdims=True))
        expo = jnp.exp(cross_scores - row_top)
        totals = lax.optimization_barrier(jnp.sum(expo, axis=-1, keepdims=True))
        cross_weights = lax.optimization_barrier(expo.astype(jnp.bfloat16)).astype(jnp.float32)
        accum = jnp.einsum('ptk,pkd->ptd', cross_weights, head_v.astype(jnp.float32), precision=lax.Precision.HIGHEST)
        return accum / totals
    per_head = lax.map(head_attention, (jnp.transpose(queries, (2, 0, 1, 3)), jnp.transpose(keys, (2, 0, 1, 3)), jnp.transpose(values, (2, 0, 1, 3))))
    context = jnp.transpose(per_head, (1, 2, 0, 3)).reshape(PAGES * TEXT, hq_dec).astype(jnp.bfloat16)
    mixed = jnp.dot(context, dec_out, preferred_element_type=jnp.float32)
    decoded = (text_states.reshape(-1, D).astype(jnp.float32) + mixed).astype(jnp.bfloat16)
    return (encoded.reshape(PAGES, ROWS, COLS, D), decoded.reshape(PAGES, TEXT, D))
```

```python
import functools
import math

import jax
import jax.numpy as jnp
from jax import lax
from jax.experimental import pallas as pl
from jax.experimental.pallas import tpu as pltpu
from jax.sharding import PartitionSpec as P

HEAD_ENC = 32
HEAD_DEC = 64
LANES = 128
VMEM_LIMIT = 48 << 20
F32 = jnp.float32
BF16 = jnp.bfloat16


def from_behind(value, axis, by):
    devices = lax.axis_size(axis)
    return lax.ppermute(value, axis, [(i, (i + by) % devices) for i in range(devices)])


def layer_norm(values):
    center = values - jnp.mean(values, axis=-1, keepdims=True)
    variance = jnp.mean(center * center, axis=-1, keepdims=True)
    return center / jnp.sqrt(variance + 1e-05)


def regions(length, window, offset):
    index_row = jnp.arange(length, dtype=jnp.int32)
    return jnp.where(
        index_row < length - window, 0, jnp.where(index_row < length - offset, 1, 2)
    ).astype(jnp.int32)


def general_body(
    page_cells, text_states, enc_query, enc_keyval, enc_proj, dec_query, dec_keyval, dec_out
):
    wq_enc, wkv_enc, wproj_enc, wq_dec, wkv_dec, wout_dec = (
        lax.all_gather(enc_query, "batch", axis=0, tiled=True),
        lax.all_gather(enc_keyval, "batch", axis=0, tiled=True),
        lax.all_gather(enc_proj, "batch", axis=1, tiled=True),
        lax.all_gather(dec_query, "batch", axis=0, tiled=True),
        lax.all_gather(dec_keyval, "batch", axis=0, tiled=True),
        lax.all_gather(dec_out, "batch", axis=1, tiled=True),
    )
    pages_here, window, columns, width = page_cells.shape
    offset = window // 2
    own_rows = window * columns
    hq_enc = wq_enc.shape[1]
    heads_enc = hq_enc // HEAD_ENC
    joined = jnp.concatenate([wq_enc, wkv_enc.reshape(width, 2 * hq_enc)], axis=1)
    rows_below = from_behind(page_cells[:, :offset], "tile", -1)
    normed = layer_norm(
        jnp.concatenate([page_cells[:, offset:], rows_below], axis=1).astype(F32)
    ).astype(BF16)
    projected = jnp.einsum("prcd,de->prce", normed, joined, preferred_element_type=F32).astype(BF16)
    projected = jnp.roll(projected, -offset, axis=2)
    per_row = columns // window
    shaped = projected.reshape(pages_here, window, per_row, window, 3, heads_enc, HEAD_ENC)
    shaped = jnp.swapaxes(shaped, 1, 2).reshape(
        pages_here, per_row, window * window, 3, heads_enc, HEAD_ENC
    )
    win_q = shaped[:, :, :, 0]
    win_k = shaped[:, :, :, 1]
    win_v = shaped[:, :, :, 2]
    is_last = lax.axis_index("tile") == lax.axis_size("tile") - 1
    local_rows = jnp.arange(window, dtype=jnp.int32)
    row_region = jnp.where(is_last, jnp.where(local_rows < window - offset, 1, 2), 0).astype(
        jnp.int32
    )
    labels = row_region[:, None] * 3 + regions(columns, window, offset)[None, :]
    labels = jnp.swapaxes(labels.reshape(window, per_row, window), 0, 1).reshape(
        per_row, window * window
    )
    allowed = labels[:, :, None] == labels[:, None, :]
    win_scores = jnp.einsum(
        "pnqhd,pnkhd->pnhqk", win_q, win_k, preferred_element_type=F32
    ) / math.sqrt(HEAD_ENC)
    win_scores = jnp.where(allowed[None, :, None], win_scores, -jnp.inf)
    top = jnp.max(win_scores, axis=-1, keepdims=True)
    expd = jnp.exp(win_scores - top)
    win_weights = (expd / jnp.sum(expd, axis=-1, keepdims=True)).astype(BF16)
    win_out = jnp.einsum(
        "pnhqk,pnkhd->pnqhd", win_weights, win_v, preferred_element_type=F32
    ).astype(BF16)
    win_out = win_out.reshape(pages_here, per_row, window, window, hq_enc)
    win_out = jnp.swapaxes(win_out, 1, 2).reshape(pages_here, window, columns, hq_enc)
    win_out = jnp.roll(win_out, offset, axis=2)
    rows_above = from_behind(win_out[:, window - offset :], "tile", 1)
    unrolled = jnp.concatenate([rows_above, win_out[:, : window - offset]], axis=1)
    partial_proj = jnp.einsum("prce,ed->prcd", unrolled, wproj_enc, preferred_element_type=F32)
    summed = lax.psum(partial_proj.astype(BF16), "mp").astype(F32)
    encoded = (page_cells.astype(F32) + summed).astype(BF16)
    hq_dec = wq_dec.shape[1]
    heads_dec = hq_dec // HEAD_DEC
    page_normed = (
        layer_norm(encoded.astype(F32)).astype(BF16).reshape(pages_here, own_rows, width)
    )
    page_kv = jnp.einsum(
        "pnd,de->pne", page_normed, wkv_dec.reshape(width, 2 * hq_dec), preferred_element_type=F32
    ).astype(BF16)
    text_normed = layer_norm(text_states.astype(F32)).astype(BF16)
    queries = jnp.einsum("ptd,de->pte", text_normed, wq_dec, preferred_element_type=F32).astype(
        BF16
    )
    text_len = text_states.shape[1]
    query_heads = queries.reshape(pages_here, text_len, heads_dec, HEAD_DEC)
    carried = (
        jnp.full((pages_here, heads_dec, text_len), -jnp.inf, F32),
        jnp.zeros((pages_here, heads_dec, text_len), F32),
        jnp.zeros((pages_here, heads_dec, text_len, HEAD_DEC), F32),
    )
    shard_rows = lax.all_gather(page_kv, "tile", axis=1, tiled=True)
    count = shard_rows.shape[1] // own_rows
    grouped = max(
        (
            factor
            for factor in range(1, count + 1)
            if count % factor == 0 and factor * own_rows <= 2048
        )
    )
    blocks = jnp.moveaxis(
        shard_rows.reshape(pages_here, count // grouped, grouped * own_rows, 2 * hq_dec), 1, 0
    )

    def advance(running, block_kv):
        maxima, totals, accum = running
        span = block_kv.shape[1]
        block_keys = block_kv[..., :hq_dec].reshape(pages_here, span, heads_dec, HEAD_DEC)
        block_vals = block_kv[..., hq_dec:].reshape(pages_here, span, heads_dec, HEAD_DEC)
        cross_scores = jnp.einsum(
            "pqhd,pkhd->phqk", query_heads, block_keys, preferred_element_type=F32
        ) / math.sqrt(HEAD_DEC)
        newest = jnp.maximum(maxima, jnp.max(cross_scores, axis=-1))
        rescale = jnp.exp(maxima - newest)
        expo = jnp.exp(cross_scores - newest[..., None])
        totals = totals * rescale + jnp.sum(expo, axis=-1)
        accum = accum * rescale[..., None] + jnp.einsum(
            "phqk,pkhd->phqd", expo.astype(BF16), block_vals, preferred_element_type=F32
        )
        return ((newest, totals, accum), None)

    carried, unused = lax.scan(advance, carried, blocks)
    maxima, totals, accum = carried
    context = (
        jnp.transpose(accum / totals[..., None], (0, 2, 1, 3))
        .reshape(pages_here, text_len, hq_dec)
        .astype(BF16)
    )
    share = text_len // lax.axis_size("mp")
    mixed = lax.psum_scatter(
        jnp.einsum("pte,ed->tpd", context, wout_dec, preferred_element_type=F32).astype(BF16),
        "mp",
        scatter_dimension=0,
        tiled=True,
    ).astype(F32)
    own_text = lax.dynamic_slice_in_dim(text_states, lax.axis_index("mp") * share, share, 1)
    decoded = (own_text.astype(F32) + jnp.moveaxis(mixed, 0, 1)).astype(BF16)
    return (encoded, decoded)


def swapped(value, axis):
    return lax.ppermute(value, axis, [(0, 1), (1, 0)])


def norm_rows(ref):
    v = ref[...].astype(F32)
    center = v - jnp.mean(v, axis=-1, keepdims=True)
    variance = jnp.mean(center * center, axis=-1, keepdims=True)
    return (center / jnp.sqrt(variance + 1e-05)).astype(BF16)


def halves(width):
    b = lax.axis_index("batch")
    half = width // 2
    own = pl.multiple_of(b * half, half)
    other = pl.multiple_of((1 - b) * half, half)
    return pl.ds(own, half), pl.ds(other, half)


def dot(a, b):
    return jnp.dot(a, b, preferred_element_type=F32)


def dot_t(a, b):
    return lax.dot_general(a, b, (((1,), (1,)), ((), ())), preferred_element_type=F32)


def lane_head(shape, size):
    return lax.broadcasted_iota(jnp.int32, shape, 1) // size


def enc_kernel(
    columns, page, above, below, wq_o, wq_x, wkv_o, wkv_x, wp_o, wp_x, part, xn, qs, kvs, wo, bias
):
    rows, width = page.shape
    part_rows = rows // 2
    offset = part_rows // columns
    window = 2 * offset
    hq = wq_o.shape[1]
    own, other = halves(width)
    xn[:part_rows] = norm_rows(above)
    xn[part_rows : part_rows + rows] = norm_rows(page)
    xn[part_rows + rows :] = norm_rows(below)
    kvs[...] = (dot(xn[:, own], wkv_o[...]) + dot(xn[:, other], wkv_x[...])).astype(BF16)
    mine = slice(part_rows, part_rows + rows)
    qs[...] = (dot(xn[mine, own], wq_o[...]) + dot(xn[mine, other], wq_x[...])).astype(BF16)

    tile = lax.axis_index("tile")
    edge = (tile == 0, tile == lax.axis_size("tile") - 1)
    shape = (part_rows, rows)
    q_col = lax.broadcasted_iota(jnp.int32, shape, 0) % columns
    key = lax.broadcasted_iota(jnp.int32, shape, 1)
    k_col = key % columns

    def group(col):
        return jnp.where(col < offset, 0, 1 + (col - offset + window) // window)

    same = group(q_col) == group(k_col)
    outside = (key < part_rows, key >= part_rows)
    for half in range(2):
        cut = jnp.logical_and(outside[half], edge[half])
        allowed = jnp.logical_and(same, jnp.logical_not(cut))
        bias[half] = jnp.where(allowed, 0.0, -jnp.inf).astype(F32)

    scale = 1.0 / math.sqrt(HEAD_ENC)
    q_head = lane_head((part_rows, LANES), HEAD_ENC)
    k_head = lane_head((rows, LANES), HEAD_ENC)
    for half in range(2):
        q_rows = slice(half * part_rows, (half + 1) * part_rows)
        k_rows = slice(half * rows, (half + 1) * rows)
        for lanes in range(hq // LANES):
            cols = slice(lanes * LANES, (lanes + 1) * LANES)
            v_cols = slice(hq + lanes * LANES, hq + (lanes + 1) * LANES)
            q = qs[q_rows, cols]
            k = kvs[k_rows, cols]
            v = kvs[k_rows, v_cols]
            acc = jnp.zeros((part_rows, LANES), F32)
            for head in range(LANES // HEAD_ENC):
                s = dot_t(jnp.where(q_head == head, q, jnp.zeros_like(q)), k) * scale
                s = s + bias[half]
                e = jnp.exp(s - jnp.max(s, axis=-1, keepdims=True))
                w = (e / jnp.sum(e, axis=-1, keepdims=True)).astype(BF16)
                acc = acc + dot(w, jnp.where(k_head == head, v, jnp.zeros_like(v)))
            wo[q_rows, cols] = acc.astype(BF16)
    part[:, own] = dot(wo[...], wp_o[...]).astype(BF16)
    part[:, other] = dot(wo[...], wp_x[...]).astype(BF16)


def pieces(scratch, first_col, outs, out_col):
    tiles = len(outs)
    tile = lax.axis_index("tile")
    for s in range(tiles):
        dest = lax.rem(tile + s, tiles)
        start = pl.multiple_of(dest * LANES + first_col, LANES)
        outs[s][:, out_col : out_col + LANES] = scratch[:, pl.ds(start, LANES)]


def kv_kernel(page, mine, theirs, wkv_o, wkv_x, encoded, *rest):
    outs, (xn, kvs) = rest[:-2], rest[-2:]
    width = page.shape[1]
    own, other = halves(width)
    total = mine[...].astype(F32) + theirs[...].astype(F32)
    encoded[...] = (page[...].astype(F32) + total).astype(BF16)
    xn[...] = norm_rows(encoded)
    kvs[...] = (dot(xn[:, own], wkv_o[...]) + dot(xn[:, other], wkv_x[...])).astype(BF16)
    pieces(kvs, 0, outs, 0)
    pieces(kvs, kvs.shape[1] // 2, outs, LANES)


def query_kernel(text, wq_o, wq_x, *rest):
    outs, (xn, qs) = rest[:-2], rest[-2:]
    own, other = halves(text.shape[1])
    xn[...] = norm_rows(text)
    qs[...] = (dot(xn[:, own], wq_o[...]) + dot(xn[:, other], wq_x[...])).astype(BF16)
    pieces(qs, 0, outs, 0)


def cross_kernel(tiles, *refs):
    q_in = refs[:tiles]
    kv_in = refs[tiles : 2 * tiles]
    outs = refs[2 * tiles : 3 * tiles]
    kv, sem = refs[3 * tiles :]
    rows = kv_in[0].shape[0]
    copies = [
        pltpu.make_async_copy(kv_in[s], kv.at[pl.ds(s * rows, rows)], sem.at[s])
        for s in range(tiles)
    ]
    for copy in copies:
        copy.start()
    for copy in copies:
        copy.wait()
    scale = 1.0 / math.sqrt(HEAD_DEC)
    q_head = lane_head(q_in[0].shape, HEAD_DEC)
    for s in range(tiles):
        q = q_in[s][...]
        acc = None
        for head in range(LANES // HEAD_DEC):
            sc = dot_t(jnp.where(q_head == head, q, jnp.zeros_like(q)), kv[:, :LANES]) * scale
            e = jnp.exp(sc - jnp.max(sc, axis=-1, keepdims=True))
            total = jnp.sum(e, axis=-1, keepdims=True)
            out = dot(e.astype(BF16), kv[:, LANES:]) / total
            acc = out if acc is None else jnp.where(q_head == head, out, acc)
        outs[s][...] = acc.astype(BF16)


def out_kernel(tiles, *refs):
    ctx_in = refs[:tiles]
    wo_o, wo_x, text, keep, send, ctx, acc = refs[tiles:]
    tokens = ctx.shape[0]
    own, other = halves(acc.shape[1])
    tile = lax.axis_index("tile")
    for s in range(tiles):
        start = pl.multiple_of(lax.rem(tile + s, tiles) * LANES, LANES)
        ctx[:, pl.ds(start, LANES)] = ctx_in[s][...]
    acc[:, own] = dot(ctx[...], wo_o[...])
    acc[:, other] = dot(ctx[...], wo_x[...])
    half = tokens // 2
    m = lax.axis_index("mp")
    own_rows = pl.ds(pl.multiple_of(m * half, half), half)
    send_rows = pl.ds(pl.multiple_of((1 - m) * half, half), half)
    keep[...] = text[own_rows, :].astype(F32) + acc[own_rows, :]
    send[...] = acc[send_rows, :].astype(BF16)


VM = pl.BlockSpec(memory_space=pltpu.VMEM)
ANY = pl.BlockSpec(memory_space=pl.ANY)


def call(kernel, outs, scratch, *args, specs=None):
    return pl.pallas_call(
        kernel,
        out_shape=[jax.ShapeDtypeStruct(shape, dtype) for shape, dtype in outs],
        in_specs=specs or [VM] * len(args),
        out_specs=[VM] * len(outs),
        scratch_shapes=scratch,
        compiler_params=pltpu.CompilerParams(vmem_limit_bytes=VMEM_LIMIT),
    )(*args)


def body(page_cells, text_states, enc_query, enc_keyval, enc_proj, dec_query, dec_keyval, dec_out):
    tiles = lax.axis_size("tile")
    pages_here, window, columns, width = page_cells.shape
    hq_enc = enc_query.shape[1]
    hq_dec = dec_query.shape[1]
    if (
        pages_here != 1
        or lax.axis_size("batch") != 2
        or lax.axis_size("mp") != 2
        or hq_dec != tiles * LANES
        or hq_enc % LANES
    ):
        return general_body(
            page_cells, text_states, enc_query, enc_keyval, enc_proj, dec_query, dec_keyval, dec_out
        )
    rows = window * columns
    half_rows = rows // 2
    page = page_cells.reshape(rows, width)
    text = text_states.reshape(-1, width)
    tokens = text.shape[0]
    wkv_enc = enc_keyval.reshape(width // 2, 2 * hq_enc)
    wkv_dec = dec_keyval.reshape(width // 2, 2 * hq_dec)
    up = [(i, i + 1) for i in range(tiles - 1)]
    down = [(i + 1, i) for i in range(tiles - 1)]
    wq_x = swapped(enc_query, "batch")
    wkv_x = swapped(wkv_enc, "batch")
    above = lax.ppermute(page[half_rows:], "tile", up)
    below = lax.ppermute(page[:half_rows], "tile", down)
    wp_x = swapped(enc_proj, "batch")
    dq_x = swapped(dec_query, "batch")
    dkv_x = swapped(wkv_dec, "batch")
    do_x = swapped(dec_out, "batch")

    (part,) = call(
        functools.partial(enc_kernel, columns),
        [((rows, width), BF16)],
        [
            pltpu.VMEM((2 * rows, width), BF16),
            pltpu.VMEM((rows, hq_enc), BF16),
            pltpu.VMEM((2 * rows, 2 * hq_enc), BF16),
            pltpu.VMEM((rows, hq_enc), BF16),
            pltpu.VMEM((2, half_rows, rows), F32),
        ],
        page,
        above,
        below,
        enc_query,
        wq_x,
        wkv_enc,
        wkv_x,
        enc_proj,
        wp_x,
    )
    theirs = swapped(part, "mp")

    q_out = call(
        query_kernel,
        [((tokens, LANES), BF16)] * tiles,
        [pltpu.VMEM((tokens, width), BF16), pltpu.VMEM((tokens, hq_dec), BF16)],
        text,
        dec_query,
        dq_x,
    )
    q_in = [q_out[0]] + [from_behind(q_out[s], "tile", s) for s in range(1, tiles)]

    encoded, *kv_out = call(
        kv_kernel,
        [((rows, width), BF16)] + [((rows, 2 * LANES), BF16)] * tiles,
        [pltpu.VMEM((rows, width), BF16), pltpu.VMEM((rows, 2 * hq_dec), BF16)],
        page,
        part,
        theirs,
        wkv_dec,
        dkv_x,
    )
    kv_in = [kv_out[0]] + [from_behind(kv_out[s], "tile", s) for s in range(1, tiles)]

    ctx_out = call(
        functools.partial(cross_kernel, tiles),
        [((tokens, LANES), BF16)] * tiles,
        [pltpu.VMEM((tiles * rows, 2 * LANES), BF16), pltpu.SemaphoreType.DMA((tiles,))],
        *q_in,
        *kv_in,
        specs=[VM] * tiles + [ANY] * tiles,
    )
    ctx_in = [ctx_out[0]] + [from_behind(ctx_out[s], "tile", -s) for s in range(1, tiles)]

    keep, send = call(
        functools.partial(out_kernel, tiles),
        [((tokens // 2, width), F32), ((tokens // 2, width), BF16)],
        [pltpu.VMEM((tokens, hq_dec), BF16), pltpu.VMEM((tokens, width), F32)],
        *ctx_in,
        dec_out,
        do_x,
        text,
    )
    received = swapped(send, "mp")
    decoded = (keep + received.astype(F32)).astype(BF16)
    return (
        encoded.reshape(page_cells.shape),
        decoded.reshape(1, tokens // 2, width),
    )


def solution(mesh):
    placed = (
        P(("pages", "batch"), "tile", None, None),
        P(("pages", "batch"), "tile", None),
        P("batch", "mp"),
        P("batch", None, "mp"),
        P("mp", "batch"),
        P("batch", "mp"),
        P("batch", None, "mp"),
        P("mp", "batch"),
    )
    return jax.shard_map(
        body,
        mesh=mesh,
        in_specs=placed,
        out_specs=(
            P(("pages", "batch"), "tile", None, None),
            P(("pages", "batch"), ("tile", "mp"), None),
        ),
        check_vma=False,
    )
```

```python
import functools
import math

import jax
import jax.numpy as jnp
from jax import lax
from jax.experimental import pallas as pl
from jax.experimental.pallas import tpu as pltpu
from jax.sharding import PartitionSpec as P

HEAD_ENC = 32
HEAD_DEC = 64
LANES = 128
VMEM_LIMIT = 48 << 20
F32 = jnp.float32
BF16 = jnp.bfloat16


def from_behind(value, axis, by):
    devices = lax.axis_size(axis)
    return lax.ppermute(value, axis, [(i, (i + by) % devices) for i in range(devices)])


def layer_norm(values):
    center = values - jnp.mean(values, axis=-1, keepdims=True)
    variance = jnp.mean(center * center, axis=-1, keepdims=True)
    return center / jnp.sqrt(variance + 1e-05)


def regions(length, window, offset):
    index_row = jnp.arange(length, dtype=jnp.int32)
    return jnp.where(
        index_row < length - window, 0, jnp.where(index_row < length - offset, 1, 2)
    ).astype(jnp.int32)


def general_body(
    page_cells, text_states, enc_query, enc_keyval, enc_proj, dec_query, dec_keyval, dec_out
):
    wq_enc, wkv_enc, wproj_enc, wq_dec, wkv_dec, wout_dec = (
        lax.all_gather(enc_query, "batch", axis=0, tiled=True),
        lax.all_gather(enc_keyval, "batch", axis=0, tiled=True),
        lax.all_gather(enc_proj, "batch", axis=1, tiled=True),
        lax.all_gather(dec_query, "batch", axis=0, tiled=True),
        lax.all_gather(dec_keyval, "batch", axis=0, tiled=True),
        lax.all_gather(dec_out, "batch", axis=1, tiled=True),
    )
    pages_here, window, columns, width = page_cells.shape
    offset = window // 2
    own_rows = window * columns
    hq_enc = wq_enc.shape[1]
    heads_enc = hq_enc // HEAD_ENC
    joined = jnp.concatenate([wq_enc, wkv_enc.reshape(width, 2 * hq_enc)], axis=1)
    rows_below = from_behind(page_cells[:, :offset], "tile", -1)
    normed = layer_norm(
        jnp.concatenate([page_cells[:, offset:], rows_below], axis=1).astype(F32)
    ).astype(BF16)
    projected = jnp.einsum("prcd,de->prce", normed, joined, preferred_element_type=F32).astype(BF16)
    projected = jnp.roll(projected, -offset, axis=2)
    per_row = columns // window
    shaped = projected.reshape(pages_here, window, per_row, window, 3, heads_enc, HEAD_ENC)
    shaped = jnp.swapaxes(shaped, 1, 2).reshape(
        pages_here, per_row, window * window, 3, heads_enc, HEAD_ENC
    )
    win_q = shaped[:, :, :, 0]
    win_k = shaped[:, :, :, 1]
    win_v = shaped[:, :, :, 2]
    is_last = lax.axis_index("tile") == lax.axis_size("tile") - 1
    local_rows = jnp.arange(window, dtype=jnp.int32)
    row_region = jnp.where(is_last, jnp.where(local_rows < window - offset, 1, 2), 0).astype(
        jnp.int32
    )
    labels = row_region[:, None] * 3 + regions(columns, window, offset)[None, :]
    labels = jnp.swapaxes(labels.reshape(window, per_row, window), 0, 1).reshape(
        per_row, window * window
    )
    allowed = labels[:, :, None] == labels[:, None, :]
    win_scores = jnp.einsum(
        "pnqhd,pnkhd->pnhqk", win_q, win_k, preferred_element_type=F32
    ) / math.sqrt(HEAD_ENC)
    win_scores = jnp.where(allowed[None, :, None], win_scores, -jnp.inf)
    top = jnp.max(win_scores, axis=-1, keepdims=True)
    expd = jnp.exp(win_scores - top)
    win_weights = (expd / jnp.sum(expd, axis=-1, keepdims=True)).astype(BF16)
    win_out = jnp.einsum(
        "pnhqk,pnkhd->pnqhd", win_weights, win_v, preferred_element_type=F32
    ).astype(BF16)
    win_out = win_out.reshape(pages_here, per_row, window, window, hq_enc)
    win_out = jnp.swapaxes(win_out, 1, 2).reshape(pages_here, window, columns, hq_enc)
    win_out = jnp.roll(win_out, offset, axis=2)
    rows_above = from_behind(win_out[:, window - offset :], "tile", 1)
    unrolled = jnp.concatenate([rows_above, win_out[:, : window - offset]], axis=1)
    partial_proj = jnp.einsum("prce,ed->prcd", unrolled, wproj_enc, preferred_element_type=F32)
    summed = lax.psum(partial_proj.astype(BF16), "mp").astype(F32)
    encoded = (page_cells.astype(F32) + summed).astype(BF16)
    hq_dec = wq_dec.shape[1]
    heads_dec = hq_dec // HEAD_DEC
    page_normed = (
        layer_norm(encoded.astype(F32)).astype(BF16).reshape(pages_here, own_rows, width)
    )
    page_kv = jnp.einsum(
        "pnd,de->pne", page_normed, wkv_dec.reshape(width, 2 * hq_dec), preferred_element_type=F32
    ).astype(BF16)
    text_normed = layer_norm(text_states.astype(F32)).astype(BF16)
    queries = jnp.einsum("ptd,de->pte", text_normed, wq_dec, preferred_element_type=F32).astype(
        BF16
    )
    text_len = text_states.shape[1]
    query_heads = queries.reshape(pages_here, text_len, heads_dec, HEAD_DEC)
    carried = (
        jnp.full((pages_here, heads_dec, text_len), -jnp.inf, F32),
        jnp.zeros((pages_here, heads_dec, text_len), F32),
        jnp.zeros((pages_here, heads_dec, text_len, HEAD_DEC), F32),
    )
    shard_rows = lax.all_gather(page_kv, "tile", axis=1, tiled=True)
    count = shard_rows.shape[1] // own_rows
    grouped = max(
        (
            factor
            for factor in range(1, count + 1)
            if count % factor == 0 and factor * own_rows <= 2048
        )
    )
    blocks = jnp.moveaxis(
        shard_rows.reshape(pages_here, count // grouped, grouped * own_rows, 2 * hq_dec), 1, 0
    )

    def advance(running, block_kv):
        maxima, totals, accum = running
        span = block_kv.shape[1]
        block_keys = block_kv[..., :hq_dec].reshape(pages_here, span, heads_dec, HEAD_DEC)
        block_vals = block_kv[..., hq_dec:].reshape(pages_here, span, heads_dec, HEAD_DEC)
        cross_scores = jnp.einsum(
            "pqhd,pkhd->phqk", query_heads, block_keys, preferred_element_type=F32
        ) / math.sqrt(HEAD_DEC)
        newest = jnp.maximum(maxima, jnp.max(cross_scores, axis=-1))
        rescale = jnp.exp(maxima - newest)
        expo = jnp.exp(cross_scores - newest[..., None])
        totals = totals * rescale + jnp.sum(expo, axis=-1)
        accum = accum * rescale[..., None] + jnp.einsum(
            "phqk,pkhd->phqd", expo.astype(BF16), block_vals, preferred_element_type=F32
        )
        return ((newest, totals, accum), None)

    carried, unused = lax.scan(advance, carried, blocks)
    maxima, totals, accum = carried
    context = (
        jnp.transpose(accum / totals[..., None], (0, 2, 1, 3))
        .reshape(pages_here, text_len, hq_dec)
        .astype(BF16)
    )
    share = text_len // lax.axis_size("mp")
    mixed = lax.psum_scatter(
        jnp.einsum("pte,ed->tpd", context, wout_dec, preferred_element_type=F32).astype(BF16),
        "mp",
        scatter_dimension=0,
        tiled=True,
    ).astype(F32)
    own_text = lax.dynamic_slice_in_dim(text_states, lax.axis_index("mp") * share, share, 1)
    decoded = (own_text.astype(F32) + jnp.moveaxis(mixed, 0, 1)).astype(BF16)
    return (encoded, decoded)


def swapped(value, axis):
    return lax.ppermute(value, axis, [(0, 1), (1, 0)])


def norm_rows(ref):
    v = ref[...].astype(F32)
    center = v - jnp.mean(v, axis=-1, keepdims=True)
    variance = jnp.mean(center * center, axis=-1, keepdims=True)
    return (center / jnp.sqrt(variance + 1e-05)).astype(BF16)


def halves(width):
    b = lax.axis_index("batch")
    half = width // 2
    own = pl.multiple_of(b * half, half)
    other = pl.multiple_of((1 - b) * half, half)
    return pl.ds(own, half), pl.ds(other, half)


def dot(a, b):
    return jnp.dot(a, b, preferred_element_type=F32)


def dot_t(a, b):
    return lax.dot_general(a, b, (((1,), (1,)), ((), ())), preferred_element_type=F32)


def lane_head(shape, size):
    return lax.broadcasted_iota(jnp.int32, shape, 1) // size


LOG2E = math.log2(math.e)
EXCLUDED = -1e30


def own_kernel(page, wq_o, wq_x, wkv_o, wkv_x, q_out, kv_out, xn):
    own, other = halves(page.shape[1])
    xn[...] = norm_rows(page)
    q_out[...] = (dot(xn[:, own], wq_o[...]) + dot(xn[:, other], wq_x[...])).astype(BF16)
    kv_out[...] = (dot(xn[:, own], wkv_o[...]) + dot(xn[:, other], wkv_x[...])).astype(BF16)


def col_group(col, offset):
    window = 2 * offset
    return jnp.where(col < offset, 0, 1 + jnp.maximum(col - offset, 0) // window)


def win_kernel(
    columns, half, q_own, kv_own, halo, wkv_o, wkv_x, wp_o, wp_x, part, xn, kx, vx, ql, wo
):
    rows, width = halo.shape
    hq = q_own.shape[1]
    offset = rows // columns
    groups = columns // (2 * offset) + 1
    own, other = halves(width)
    xn[...] = norm_rows(halo)
    kv_halo = (dot(xn[:, own], wkv_o[...]) + dot(xn[:, other], wkv_x[...])).astype(BF16)
    kv_here = kv_own[half * rows : (half + 1) * rows, :]

    tile = lax.axis_index("tile")
    edge = tile == (0 if half == 0 else lax.axis_size("tile") - 1)
    lane = lax.broadcasted_iota(jnp.int32, (rows, LANES), 1)
    group = col_group(lax.broadcasted_iota(jnp.int32, (rows, LANES), 0) % columns, offset)
    unlike = jnp.logical_and(lane < groups, lane != group)
    cut = jnp.logical_and(lane == groups, edge)
    off = jnp.full((rows, LANES), EXCLUDED, F32)
    here_marks = jnp.where(unlike, off, 0.0).astype(BF16)
    halo_marks = jnp.where(jnp.logical_or(unlike, cut), off, 0.0).astype(BF16)
    q_marks = jnp.where(jnp.logical_or(lane == group, lane == groups), 1.0, 0.0).astype(BF16)
    ones = jnp.ones((2 * rows, LANES), BF16)
    heads = LANES // HEAD_ENC
    for h in range(heads):
        ql[h * rows : (h + 1) * rows, LANES:] = q_marks
    for g in range(hq // LANES):
        k_cols = slice(g * LANES, (g + 1) * LANES)
        v_cols = slice(hq + g * LANES, hq + (g + 1) * LANES)
        wide = slice(2 * g * LANES, (2 * g + 1) * LANES)
        extra = slice((2 * g + 1) * LANES, (2 * g + 2) * LANES)
        kx[:rows, wide] = kv_here[:, k_cols]
        kx[rows:, wide] = kv_halo[:, k_cols]
        kx[:rows, extra] = here_marks
        kx[rows:, extra] = halo_marks
        vx[:rows, wide] = kv_here[:, v_cols]
        vx[rows:, wide] = kv_halo[:, v_cols]
        vx[:, extra] = ones
    scale = LOG2E / math.sqrt(HEAD_ENC)
    q_head = lane // HEAD_ENC
    for g in range(hq // LANES):
        q = q_own[half * rows : (half + 1) * rows, g * LANES : (g + 1) * LANES]
        both = slice(2 * g * LANES, (2 * g + 2) * LANES)
        for h in range(heads):
            ql[h * rows : (h + 1) * rows, :LANES] = jnp.where(q_head == h, q, jnp.zeros_like(q))
        s = dot_t(ql[...], kx[:, both])
        e = jnp.exp2((s - jnp.max(s, axis=-1, keepdims=True)) * scale).astype(BF16)
        o = dot(e, vx[:, both])
        acc = None
        for h in range(heads):
            block = slice(h * rows, (h + 1) * rows)
            one = o[block, :LANES] / o[block, LANES:]
            acc = one if acc is None else jnp.where(q_head == h, one, acc)
        wo[:, g * LANES : (g + 1) * LANES] = acc.astype(BF16)
    part[:, own] = dot(wo[...], wp_o[...]).astype(BF16)
    part[:, other] = dot(wo[...], wp_x[...]).astype(BF16)


def pieces(scratch, first_col, outs, out_col):
    tiles = len(outs)
    tile = lax.axis_index("tile")
    for s in range(tiles):
        dest = lax.rem(tile + s, tiles)
        start = pl.multiple_of(dest * LANES + first_col, LANES)
        outs[s][:, out_col : out_col + LANES] = scratch[:, pl.ds(start, LANES)]


def kv_kernel(half, page, mine, theirs, wkv_o, wkv_x, encoded, *rest):
    outs, (xn, kvs) = rest[:-2], rest[-2:]
    rows, width = mine.shape
    own, other = halves(width)
    total = mine[...].astype(F32) + theirs[...].astype(F32)
    here = page[half * rows : (half + 1) * rows, :]
    encoded[...] = (here.astype(F32) + total).astype(BF16)
    xn[...] = norm_rows(encoded)
    kvs[...] = (dot(xn[:, own], wkv_o[...]) + dot(xn[:, other], wkv_x[...])).astype(BF16)
    pieces(kvs, 0, outs, 0)
    pieces(kvs, kvs.shape[1] // 2, outs, LANES)


def query_kernel(text, wq_o, wq_x, *rest):
    outs, (xn, qs) = rest[:-2], rest[-2:]
    own, other = halves(text.shape[1])
    xn[...] = norm_rows(text)
    qs[...] = (dot(xn[:, own], wq_o[...]) + dot(xn[:, other], wq_x[...])).astype(BF16)
    pieces(qs, 0, outs, 0)


def cross_kernel(tiles, *refs):
    q_in = refs[:tiles]
    kv_in = refs[tiles : 3 * tiles]
    outs = refs[3 * tiles : 4 * tiles]
    kv, ql, sem = refs[4 * tiles :]
    rows = kv_in[0].shape[0]
    copies = [
        pltpu.make_async_copy(
            kv_in[s], kv.at[pl.ds(s * rows, rows), pl.ds(0, 2 * LANES)], sem.at[s]
        )
        for s in range(2 * tiles)
    ]
    for copy in copies:
        copy.start()
    kv[:, 2 * LANES :] = jnp.ones((kv.shape[0], LANES), BF16)
    tokens = q_in[0].shape[0]
    q_head = lane_head(q_in[0].shape, HEAD_DEC)
    scale = LOG2E / math.sqrt(HEAD_DEC)
    for copy in copies:
        copy.wait()
    for s in range(tiles):
        q = q_in[s][...]
        for h in range(LANES // HEAD_DEC):
            ql[h * tokens : (h + 1) * tokens] = jnp.where(q_head == h, q, jnp.zeros_like(q))
        sc = dot_t(ql[...], kv[:, :LANES])
        e = jnp.exp2((sc - jnp.max(sc, axis=-1, keepdims=True)) * scale).astype(BF16)
        o = dot(e, kv[:, LANES:])
        o = o[:, :LANES] / o[:, LANES:]
        outs[s][...] = jnp.where(q_head == 0, o[:tokens], o[tokens:]).astype(BF16)


def out_kernel(tiles, *refs):
    ctx_in = refs[:tiles]
    wo_o, wo_x, text, keep, send, ctx, acc = refs[tiles:]
    tokens = ctx.shape[0]
    own, other = halves(acc.shape[1])
    tile = lax.axis_index("tile")
    for s in range(tiles):
        start = pl.multiple_of(lax.rem(tile + s, tiles) * LANES, LANES)
        ctx[:, pl.ds(start, LANES)] = ctx_in[s][...]
    acc[:, own] = dot(ctx[...], wo_o[...])
    acc[:, other] = dot(ctx[...], wo_x[...])
    half = tokens // 2
    m = lax.axis_index("mp")
    own_rows = pl.ds(pl.multiple_of(m * half, half), half)
    send_rows = pl.ds(pl.multiple_of((1 - m) * half, half), half)
    keep[...] = text[own_rows, :].astype(F32) + acc[own_rows, :]
    send[...] = acc[send_rows, :].astype(BF16)


VM = pl.BlockSpec(memory_space=pltpu.VMEM)
ANY = pl.BlockSpec(memory_space=pl.ANY)


def call(kernel, flops, outs, scratch, *args, specs=None):
    moved = sum(math.prod(a.shape) * 2 for a in args) + sum(math.prod(s) * 2 for s, _ in outs)
    return pl.pallas_call(
        kernel,
        out_shape=[jax.ShapeDtypeStruct(shape, dtype) for shape, dtype in outs],
        in_specs=specs or [VM] * len(args),
        out_specs=[VM] * len(outs),
        scratch_shapes=scratch,
        cost_estimate=pl.CostEstimate(flops=flops, transcendentals=0, bytes_accessed=moved)
        if flops
        else None,
        compiler_params=pltpu.CompilerParams(vmem_limit_bytes=VMEM_LIMIT),
    )(*args)


def after(value, *earlier):
    return lax.optimization_barrier((value,) + earlier)[0]


def body(page_cells, text_states, enc_query, enc_keyval, enc_proj, dec_query, dec_keyval, dec_out):
    tiles = lax.axis_size("tile")
    pages_here, window, columns, width = page_cells.shape
    hq_enc = enc_query.shape[1]
    hq_dec = dec_query.shape[1]
    if (
        pages_here != 1
        or lax.axis_size("batch") != 2
        or lax.axis_size("mp") != 2
        or hq_dec != tiles * LANES
        or hq_enc % LANES
    ):
        return general_body(
            page_cells, text_states, enc_query, enc_keyval, enc_proj, dec_query, dec_keyval, dec_out
        )
    rows = window * columns
    half_rows = rows // 2
    page = page_cells.reshape(rows, width)
    text = text_states.reshape(-1, width)
    tokens = text.shape[0]
    up = [(i, i + 1) for i in range(tiles - 1)]
    down = [(i + 1, i) for i in range(tiles - 1)]
    upper, lower = page[:half_rows], page[half_rows:]
    above = lax.ppermute(lower, "tile", up)
    below = lax.ppermute(upper, "tile", down)
    wkv_enc = enc_keyval.reshape(width // 2, 2 * hq_enc)
    wkv_x = swapped(wkv_enc, "batch")
    wq_x = swapped(enc_query, "batch")
    wp_x = swapped(enc_proj, "batch")
    dq_x = swapped(after(dec_query, wkv_x), "batch")

    q_own, kv_own = call(
        own_kernel,
        1,
        [((rows, hq_enc), BF16), ((rows, 2 * hq_enc), BF16)],
        [pltpu.VMEM((rows, width), BF16)],
        page,
        enc_query,
        wq_x,
        wkv_enc,
        wkv_x,
    )
    q_out = call(
        query_kernel,
        1,
        [((tokens, LANES), BF16)] * tiles,
        [pltpu.VMEM((tokens, width), BF16), pltpu.VMEM((tokens, hq_dec), BF16)],
        text,
        dec_query,
        dq_x,
    )
    q_in = [q_out[0]] + [from_behind(q_out[s], "tile", s) for s in range(1, tiles)]

    def window_half(half, halo):
        (part,) = call(
            functools.partial(win_kernel, columns, half),
            2 * half_rows * width * 3 * hq_enc + 8 * half_rows * rows * LANES * hq_enc // HEAD_ENC,
            [((half_rows, width), BF16)],
            [
                pltpu.VMEM((half_rows, width), BF16),
                pltpu.VMEM((rows, 2 * hq_enc), BF16),
                pltpu.VMEM((rows, 2 * hq_enc), BF16),
                pltpu.VMEM((LANES // HEAD_ENC * half_rows, 2 * LANES), BF16),
                pltpu.VMEM((half_rows, hq_enc), BF16),
            ],
            q_own,
            kv_own,
            halo,
            wkv_enc,
            wkv_x,
            enc_proj,
            wp_x,
        )
        return part

    def key_values(half, part, theirs):
        return call(
            functools.partial(kv_kernel, half),
            2 * half_rows * width * 2 * hq_dec,
            [((half_rows, width), BF16)] + [((half_rows, 2 * LANES), BF16)] * tiles,
            [pltpu.VMEM((half_rows, width), BF16), pltpu.VMEM((half_rows, 2 * hq_dec), BF16)],
            page,
            part,
            theirs,
            wkv_dec,
            dkv_x,
        )

    above, below = lax.optimization_barrier((above, below, *q_out))[:2]
    part_a = window_half(0, above)
    theirs_a = swapped(part_a, "mp")
    part_b = window_half(1, after(below, part_a))
    wkv_dec = after(dec_keyval, part_b).reshape(width // 2, 2 * hq_dec)
    dkv_x = swapped(wkv_dec, "batch")
    theirs_b = swapped(part_b, "mp")
    theirs_a, *q_in = lax.optimization_barrier((theirs_a, *q_in))
    encoded_a, *kv_a = key_values(0, part_a, theirs_a)
    kv_first = kv_a
    kv_a = [kv_a[0]] + [from_behind(kv_a[s], "tile", s) for s in range(1, tiles)]
    encoded_b, *kv_b = key_values(1, part_b, after(theirs_b, *kv_first))
    kv_b = [kv_b[0]] + [from_behind(kv_b[s], "tile", s) for s in range(1, tiles)]
    do_x = swapped(after(dec_out, encoded_b), "batch")
    encoded = jnp.concatenate([encoded_a, encoded_b], axis=0)

    ctx_out = call(
        functools.partial(cross_kernel, tiles),
        8 * tiles * tokens * tiles * rows * LANES,
        [((tokens, LANES), BF16)] * tiles,
        [
            pltpu.VMEM((tiles * rows, 3 * LANES), BF16),
            pltpu.VMEM((LANES // HEAD_DEC * tokens, LANES), BF16),
            pltpu.SemaphoreType.DMA((2 * tiles,)),
        ],
        *q_in,
        *kv_a,
        *kv_b,
        specs=[VM] * tiles + [ANY] * (2 * tiles),
    )
    ctx_in = [ctx_out[0]] + [from_behind(ctx_out[s], "tile", -s) for s in range(1, tiles)]

    keep, send = call(
        functools.partial(out_kernel, tiles),
        2 * tokens * hq_dec * width,
        [((tokens // 2, width), F32), ((tokens // 2, width), BF16)],
        [pltpu.VMEM((tokens, hq_dec), BF16), pltpu.VMEM((tokens, width), F32)],
        *ctx_in,
        dec_out,
        do_x,
        text,
    )
    received = swapped(send, "mp")
    decoded = (keep + received.astype(F32)).astype(BF16)
    return (
        encoded.reshape(page_cells.shape),
        decoded.reshape(1, tokens // 2, width),
    )


def solution(mesh):
    placed = (
        P(("pages", "batch"), "tile", None, None),
        P(("pages", "batch"), "tile", None),
        P("batch", "mp"),
        P("batch", None, "mp"),
        P("mp", "batch"),
        P("batch", "mp"),
        P("batch", None, "mp"),
        P("mp", "batch"),
    )
    return jax.shard_map(
        body,
        mesh=mesh,
        in_specs=placed,
        out_specs=(
            P(("pages", "batch"), "tile", None, None),
            P(("pages", "batch"), ("tile", "mp"), None),
        ),
        check_vma=False,
    )
```

```python
import functools
import math

import jax
import jax.numpy as jnp
from jax import lax
from jax.experimental import pallas as pl
from jax.experimental.pallas import tpu as pltpu
from jax.sharding import PartitionSpec as P

HEAD_ENC = 32
HEAD_DEC = 64
LANES = 128
VMEM_LIMIT = 48 << 20
F32 = jnp.float32
BF16 = jnp.bfloat16


def from_behind(value, axis, by):
    devices = lax.axis_size(axis)
    return lax.ppermute(value, axis, [(i, (i + by) % devices) for i in range(devices)])


def layer_norm(values):
    center = values - jnp.mean(values, axis=-1, keepdims=True)
    variance = jnp.mean(center * center, axis=-1, keepdims=True)
    return center / jnp.sqrt(variance + 1e-05)


def regions(length, window, offset):
    index_row = jnp.arange(length, dtype=jnp.int32)
    return jnp.where(
        index_row < length - window, 0, jnp.where(index_row < length - offset, 1, 2)
    ).astype(jnp.int32)


def general_body(
    page_cells, text_states, enc_query, enc_keyval, enc_proj, dec_query, dec_keyval, dec_out
):
    wq_enc, wkv_enc, wproj_enc, wq_dec, wkv_dec, wout_dec = (
        lax.all_gather(enc_query, "batch", axis=0, tiled=True),
        lax.all_gather(enc_keyval, "batch", axis=0, tiled=True),
        lax.all_gather(enc_proj, "batch", axis=1, tiled=True),
        lax.all_gather(dec_query, "batch", axis=0, tiled=True),
        lax.all_gather(dec_keyval, "batch", axis=0, tiled=True),
        lax.all_gather(dec_out, "batch", axis=1, tiled=True),
    )
    pages_here, window, columns, width = page_cells.shape
    offset = window // 2
    own_rows = window * columns
    hq_enc = wq_enc.shape[1]
    heads_enc = hq_enc // HEAD_ENC
    joined = jnp.concatenate([wq_enc, wkv_enc.reshape(width, 2 * hq_enc)], axis=1)
    rows_below = from_behind(page_cells[:, :offset], "tile", -1)
    normed = layer_norm(
        jnp.concatenate([page_cells[:, offset:], rows_below], axis=1).astype(F32)
    ).astype(BF16)
    projected = jnp.einsum("prcd,de->prce", normed, joined, preferred_element_type=F32).astype(BF16)
    projected = jnp.roll(projected, -offset, axis=2)
    per_row = columns // window
    shaped = projected.reshape(pages_here, window, per_row, window, 3, heads_enc, HEAD_ENC)
    shaped = jnp.swapaxes(shaped, 1, 2).reshape(
        pages_here, per_row, window * window, 3, heads_enc, HEAD_ENC
    )
    win_q = shaped[:, :, :, 0]
    win_k = shaped[:, :, :, 1]
    win_v = shaped[:, :, :, 2]
    is_last = lax.axis_index("tile") == lax.axis_size("tile") - 1
    local_rows = jnp.arange(window, dtype=jnp.int32)
    row_region = jnp.where(is_last, jnp.where(local_rows < window - offset, 1, 2), 0).astype(
        jnp.int32
    )
    labels = row_region[:, None] * 3 + regions(columns, window, offset)[None, :]
    labels = jnp.swapaxes(labels.reshape(window, per_row, window), 0, 1).reshape(
        per_row, window * window
    )
    allowed = labels[:, :, None] == labels[:, None, :]
    win_scores = jnp.einsum(
        "pnqhd,pnkhd->pnhqk", win_q, win_k, preferred_element_type=F32
    ) / math.sqrt(HEAD_ENC)
    win_scores = jnp.where(allowed[None, :, None], win_scores, -jnp.inf)
    top = jnp.max(win_scores, axis=-1, keepdims=True)
    expd = jnp.exp(win_scores - top)
    win_weights = (expd / jnp.sum(expd, axis=-1, keepdims=True)).astype(BF16)
    win_out = jnp.einsum(
        "pnhqk,pnkhd->pnqhd", win_weights, win_v, preferred_element_type=F32
    ).astype(BF16)
    win_out = win_out.reshape(pages_here, per_row, window, window, hq_enc)
    win_out = jnp.swapaxes(win_out, 1, 2).reshape(pages_here, window, columns, hq_enc)
    win_out = jnp.roll(win_out, offset, axis=2)
    rows_above = from_behind(win_out[:, window - offset :], "tile", 1)
    unrolled = jnp.concatenate([rows_above, win_out[:, : window - offset]], axis=1)
    partial_proj = jnp.einsum("prce,ed->prcd", unrolled, wproj_enc, preferred_element_type=F32)
    summed = lax.psum(partial_proj.astype(BF16), "mp").astype(F32)
    encoded = (page_cells.astype(F32) + summed).astype(BF16)
    hq_dec = wq_dec.shape[1]
    heads_dec = hq_dec // HEAD_DEC
    page_normed = (
        layer_norm(encoded.astype(F32)).astype(BF16).reshape(pages_here, own_rows, width)
    )
    page_kv = jnp.einsum(
        "pnd,de->pne", page_normed, wkv_dec.reshape(width, 2 * hq_dec), preferred_element_type=F32
    ).astype(BF16)
    text_normed = layer_norm(text_states.astype(F32)).astype(BF16)
    queries = jnp.einsum("ptd,de->pte", text_normed, wq_dec, preferred_element_type=F32).astype(
        BF16
    )
    text_len = text_states.shape[1]
    query_heads = queries.reshape(pages_here, text_len, heads_dec, HEAD_DEC)
    carried = (
        jnp.full((pages_here, heads_dec, text_len), -jnp.inf, F32),
        jnp.zeros((pages_here, heads_dec, text_len), F32),
        jnp.zeros((pages_here, heads_dec, text_len, HEAD_DEC), F32),
    )
    shard_rows = lax.all_gather(page_kv, "tile", axis=1, tiled=True)
    count = shard_rows.shape[1] // own_rows
    grouped = max(
        (
            factor
            for factor in range(1, count + 1)
            if count % factor == 0 and factor * own_rows <= 2048
        )
    )
    blocks = jnp.moveaxis(
        shard_rows.reshape(pages_here, count // grouped, grouped * own_rows, 2 * hq_dec), 1, 0
    )

    def advance(running, block_kv):
        maxima, totals, accum = running
        span = block_kv.shape[1]
        block_keys = block_kv[..., :hq_dec].reshape(pages_here, span, heads_dec, HEAD_DEC)
        block_vals = block_kv[..., hq_dec:].reshape(pages_here, span, heads_dec, HEAD_DEC)
        cross_scores = jnp.einsum(
            "pqhd,pkhd->phqk", query_heads, block_keys, preferred_element_type=F32
        ) / math.sqrt(HEAD_DEC)
        newest = jnp.maximum(maxima, jnp.max(cross_scores, axis=-1))
        rescale = jnp.exp(maxima - newest)
        expo = jnp.exp(cross_scores - newest[..., None])
        totals = totals * rescale + jnp.sum(expo, axis=-1)
        accum = accum * rescale[..., None] + jnp.einsum(
            "phqk,pkhd->phqd", expo.astype(BF16), block_vals, preferred_element_type=F32
        )
        return ((newest, totals, accum), None)

    carried, unused = lax.scan(advance, carried, blocks)
    maxima, totals, accum = carried
    context = (
        jnp.transpose(accum / totals[..., None], (0, 2, 1, 3))
        .reshape(pages_here, text_len, hq_dec)
        .astype(BF16)
    )
    share = text_len // lax.axis_size("mp")
    mixed = lax.psum_scatter(
        jnp.einsum("pte,ed->tpd", context, wout_dec, preferred_element_type=F32).astype(BF16),
        "mp",
        scatter_dimension=0,
        tiled=True,
    ).astype(F32)
    own_text = lax.dynamic_slice_in_dim(text_states, lax.axis_index("mp") * share, share, 1)
    decoded = (own_text.astype(F32) + jnp.moveaxis(mixed, 0, 1)).astype(BF16)
    return (encoded, decoded)


def swapped(value, axis):
    return lax.ppermute(value, axis, [(0, 1), (1, 0)])


def norm_rows(ref):
    v = ref[...].astype(F32)
    center = v - jnp.mean(v, axis=-1, keepdims=True)
    variance = jnp.mean(center * center, axis=-1, keepdims=True)
    return (center / jnp.sqrt(variance + 1e-05)).astype(BF16)


def halves(width):
    b = lax.axis_index("batch")
    half = width // 2
    own = pl.multiple_of(b * half, half)
    other = pl.multiple_of((1 - b) * half, half)
    return pl.ds(own, half), pl.ds(other, half)


def dot(a, b):
    return jnp.dot(a, b, preferred_element_type=F32)


def dot_t(a, b):
    return lax.dot_general(a, b, (((1,), (1,)), ((), ())), preferred_element_type=F32)


def lane_head(shape, size):
    return lax.broadcasted_iota(jnp.int32, shape, 1) // size


LOG2E = math.log2(math.e)
EXCLUDED = -1e30


def own_kernel(page, wq_o, wq_x, wkv_o, wkv_x, q_out, kv_out, xn):
    own, other = halves(page.shape[1])
    xn[...] = norm_rows(page)
    q_out[...] = (dot(xn[:, own], wq_o[...]) + dot(xn[:, other], wq_x[...])).astype(BF16)
    kv_out[...] = (dot(xn[:, own], wkv_o[...]) + dot(xn[:, other], wkv_x[...])).astype(BF16)


def col_group(col, offset):
    window = 2 * offset
    return jnp.where(col < offset, 0, 1 + jnp.maximum(col - offset, 0) // window)


def win_kernel(
    columns, half, q_own, kv_own, halo, wkv_o, wkv_x, wp_o, wp_x, part, xn, kx, vx, ql, wo
):
    rows, width = halo.shape
    hq = q_own.shape[1]
    offset = rows // columns
    groups = columns // (2 * offset) + 1
    own, other = halves(width)
    xn[...] = norm_rows(halo)
    kv_halo = (dot(xn[:, own], wkv_o[...]) + dot(xn[:, other], wkv_x[...])).astype(BF16)
    kv_here = kv_own[half * rows : (half + 1) * rows, :]

    tile = lax.axis_index("tile")
    edge = tile == (0 if half == 0 else lax.axis_size("tile") - 1)
    lane = lax.broadcasted_iota(jnp.int32, (rows, LANES), 1)
    group = col_group(lax.broadcasted_iota(jnp.int32, (rows, LANES), 0) % columns, offset)
    unlike = jnp.logical_and(lane < groups, lane != group)
    cut = jnp.logical_and(lane == groups, edge)
    off = jnp.full((rows, LANES), EXCLUDED, F32)
    here_marks = jnp.where(unlike, off, 0.0).astype(BF16)
    halo_marks = jnp.where(jnp.logical_or(unlike, cut), off, 0.0).astype(BF16)
    q_marks = jnp.where(jnp.logical_or(lane == group, lane == groups), 1.0, 0.0).astype(BF16)
    ones = jnp.ones((2 * rows, LANES), BF16)
    heads = LANES // HEAD_ENC
    for h in range(heads):
        ql[h * rows : (h + 1) * rows, LANES:] = q_marks
    for g in range(hq // LANES):
        k_cols = slice(g * LANES, (g + 1) * LANES)
        v_cols = slice(hq + g * LANES, hq + (g + 1) * LANES)
        wide = slice(2 * g * LANES, (2 * g + 1) * LANES)
        extra = slice((2 * g + 1) * LANES, (2 * g + 2) * LANES)
        kx[:rows, wide] = kv_here[:, k_cols]
        kx[rows:, wide] = kv_halo[:, k_cols]
        kx[:rows, extra] = here_marks
        kx[rows:, extra] = halo_marks
        vx[:rows, wide] = kv_here[:, v_cols]
        vx[rows:, wide] = kv_halo[:, v_cols]
        vx[:, extra] = ones
    scale = LOG2E / math.sqrt(HEAD_ENC)
    q_head = lane // HEAD_ENC
    for g in range(hq // LANES):
        q = q_own[half * rows : (half + 1) * rows, g * LANES : (g + 1) * LANES]
        both = slice(2 * g * LANES, (2 * g + 2) * LANES)
        for h in range(heads):
            ql[h * rows : (h + 1) * rows, :LANES] = jnp.where(q_head == h, q, jnp.zeros_like(q))
        s = dot_t(ql[...], kx[:, both])
        e = jnp.exp2((s - jnp.max(s, axis=-1, keepdims=True)) * scale).astype(BF16)
        o = dot(e, vx[:, both])
        acc = None
        for h in range(heads):
            block = slice(h * rows, (h + 1) * rows)
            one = o[block, :LANES] / o[block, LANES:]
            acc = one if acc is None else jnp.where(q_head == h, one, acc)
        wo[:, g * LANES : (g + 1) * LANES] = acc.astype(BF16)
    part[:, own] = dot(wo[...], wp_o[...]).astype(BF16)
    part[:, other] = dot(wo[...], wp_x[...]).astype(BF16)


def pieces(scratch, first_col, outs, out_col):
    tiles = len(outs)
    tile = lax.axis_index("tile")
    for s in range(tiles):
        dest = lax.rem(tile + s, tiles)
        start = pl.multiple_of(dest * LANES + first_col, LANES)
        outs[s][:, out_col : out_col + LANES] = scratch[:, pl.ds(start, LANES)]


def kv_kernel(half, page, mine, theirs, wkv_o, wkv_x, encoded, *rest):
    outs, (xn, kvs) = rest[:-2], rest[-2:]
    rows, width = mine.shape
    own, other = halves(width)
    total = mine[...].astype(F32) + theirs[...].astype(F32)
    here = page[half * rows : (half + 1) * rows, :]
    encoded[...] = (here.astype(F32) + total).astype(BF16)
    xn[...] = norm_rows(encoded)
    kvs[...] = (dot(xn[:, own], wkv_o[...]) + dot(xn[:, other], wkv_x[...])).astype(BF16)
    pieces(kvs, 0, outs, 0)
    pieces(kvs, kvs.shape[1] // 2, outs, LANES)


def query_kernel(text, wq_o, wq_x, *rest):
    outs, (xn, qs) = rest[:-2], rest[-2:]
    own, other = halves(text.shape[1])
    xn[...] = norm_rows(text)
    qs[...] = (dot(xn[:, own], wq_o[...]) + dot(xn[:, other], wq_x[...])).astype(BF16)
    pieces(qs, 0, outs, 0)


def cross_kernel(count, strips, *refs):
    q_in = refs[:count]
    kv_in = refs[count : count + strips]
    outs = refs[count + strips : 2 * count + strips]
    kv, ql, sem = refs[2 * count + strips :]
    rows = kv_in[0].shape[0]
    copies = [
        pltpu.make_async_copy(
            kv_in[s], kv.at[pl.ds(s * rows, rows), pl.ds(0, 2 * LANES)], sem.at[s]
        )
        for s in range(strips)
    ]
    for copy in copies:
        copy.start()
    kv[:, 2 * LANES :] = jnp.ones((kv.shape[0], LANES), BF16)
    tokens = q_in[0].shape[0]
    q_head = lane_head(q_in[0].shape, HEAD_DEC)
    scale = LOG2E / math.sqrt(HEAD_DEC)
    for copy in copies:
        copy.wait()
    for s in range(count):
        q = q_in[s][...]
        for h in range(LANES // HEAD_DEC):
            ql[h * tokens : (h + 1) * tokens] = jnp.where(q_head == h, q, jnp.zeros_like(q))
        sc = dot_t(ql[...], kv[:, :LANES])
        e = jnp.exp2((sc - jnp.max(sc, axis=-1, keepdims=True)) * scale).astype(BF16)
        o = dot(e, kv[:, LANES:])
        o = o[:, :LANES] / o[:, LANES:]
        outs[s][...] = jnp.where(q_head == 0, o[:tokens], o[tokens:]).astype(BF16)


def out_kernel(tiles, *refs):
    ctx_in = refs[:tiles]
    wo_o, wo_x, text, keep, send, ctx, acc = refs[tiles:]
    tokens = ctx.shape[0]
    own, other = halves(acc.shape[1])
    tile = lax.axis_index("tile")
    for s in range(tiles):
        start = pl.multiple_of(lax.rem(tile + s, tiles) * LANES, LANES)
        ctx[:, pl.ds(start, LANES)] = ctx_in[s][...]
    acc[:, own] = dot(ctx[...], wo_o[...])
    acc[:, other] = dot(ctx[...], wo_x[...])
    half = tokens // 2
    m = lax.axis_index("mp")
    own_rows = pl.ds(pl.multiple_of(m * half, half), half)
    send_rows = pl.ds(pl.multiple_of((1 - m) * half, half), half)
    keep[...] = text[own_rows, :].astype(F32) + acc[own_rows, :]
    send[...] = acc[send_rows, :].astype(BF16)


VM = pl.BlockSpec(memory_space=pltpu.VMEM)
ANY = pl.BlockSpec(memory_space=pl.ANY)


def call(kernel, flops, outs, scratch, *args, specs=None):
    moved = sum(math.prod(a.shape) * 2 for a in args) + sum(math.prod(s) * 2 for s, _ in outs)
    return pl.pallas_call(
        kernel,
        out_shape=[jax.ShapeDtypeStruct(shape, dtype) for shape, dtype in outs],
        in_specs=specs or [VM] * len(args),
        out_specs=[VM] * len(outs),
        scratch_shapes=scratch,
        cost_estimate=pl.CostEstimate(flops=flops, transcendentals=0, bytes_accessed=moved)
        if flops
        else None,
        compiler_params=pltpu.CompilerParams(vmem_limit_bytes=VMEM_LIMIT),
    )(*args)


def after(value, *earlier):
    return lax.optimization_barrier((value,) + earlier)[0]


def body(page_cells, text_states, enc_query, enc_keyval, enc_proj, dec_query, dec_keyval, dec_out):
    tiles = lax.axis_size("tile")
    pages_here, window, columns, width = page_cells.shape
    hq_enc = enc_query.shape[1]
    hq_dec = dec_query.shape[1]
    if (
        pages_here != 1
        or lax.axis_size("batch") != 2
        or lax.axis_size("mp") != 2
        or hq_dec != tiles * LANES
        or hq_enc % LANES
    ):
        return general_body(
            page_cells, text_states, enc_query, enc_keyval, enc_proj, dec_query, dec_keyval, dec_out
        )
    rows = window * columns
    half_rows = rows // 2
    page = page_cells.reshape(rows, width)
    text = text_states.reshape(-1, width)
    tokens = text.shape[0]
    up = [(i, i + 1) for i in range(tiles - 1)]
    down = [(i + 1, i) for i in range(tiles - 1)]
    upper, lower = page[:half_rows], page[half_rows:]
    above = lax.ppermute(lower, "tile", up)
    below = lax.ppermute(upper, "tile", down)
    wkv_x = swapped(enc_keyval, "batch").reshape(width // 2, 2 * hq_enc)
    wkv_enc = enc_keyval.reshape(width // 2, 2 * hq_enc)
    wq_x = swapped(enc_query, "batch")
    dq_x = swapped(dec_query, "batch")

    q_own, kv_own = call(
        own_kernel,
        1,
        [((rows, hq_enc), BF16), ((rows, 2 * hq_enc), BF16)],
        [pltpu.VMEM((rows, width), BF16)],
        page,
        enc_query,
        wq_x,
        wkv_enc,
        wkv_x,
    )
    q_out = call(
        query_kernel,
        1,
        [((tokens, LANES), BF16)] * tiles,
        [pltpu.VMEM((tokens, width), BF16), pltpu.VMEM((tokens, hq_dec), BF16)],
        after(text, q_own),
        dec_query,
        dq_x,
    )
    q_in = [q_out[0]] + [from_behind(q_out[s], "tile", s) for s in range(1, tiles)]

    wp_x = swapped(enc_proj, "batch")
    above, below, *q_in = lax.optimization_barrier((above, below, *q_in))

    def window_half(half, halo):
        (part,) = call(
            functools.partial(win_kernel, columns, half),
            2 * half_rows * width * 3 * hq_enc + 8 * half_rows * rows * LANES * hq_enc // HEAD_ENC,
            [((half_rows, width), BF16)],
            [
                pltpu.VMEM((half_rows, width), BF16),
                pltpu.VMEM((rows, 2 * hq_enc), BF16),
                pltpu.VMEM((rows, 2 * hq_enc), BF16),
                pltpu.VMEM((LANES // HEAD_ENC * half_rows, 2 * LANES), BF16),
                pltpu.VMEM((half_rows, hq_enc), BF16),
            ],
            q_own,
            kv_own,
            halo,
            wkv_enc,
            wkv_x,
            enc_proj,
            wp_x,
        )
        return part

    def key_values(half, part, theirs):
        return call(
            functools.partial(kv_kernel, half),
            2 * half_rows * width * 2 * hq_dec,
            [((half_rows, width), BF16)] + [((half_rows, 2 * LANES), BF16)] * tiles,
            [pltpu.VMEM((half_rows, width), BF16), pltpu.VMEM((half_rows, 2 * hq_dec), BF16)],
            page,
            part,
            theirs,
            wkv_dec,
            dkv_x,
        )

    part_a = window_half(0, above)
    wkv_dec = after(dec_keyval, part_a).reshape(width // 2, 2 * hq_dec)
    dkv_x = swapped(wkv_dec, "batch")
    theirs_a = swapped(part_a, "mp")
    part_b = window_half(1, after(below, part_a))
    theirs_b = swapped(part_b, "mp")
    encoded_a, *kv_a = key_values(0, part_a, theirs_a)
    kv_a = [kv_a[0]] + [from_behind(kv_a[s], "tile", s) for s in range(1, tiles)]
    theirs_b, *kv_a = lax.optimization_barrier((theirs_b, *kv_a))
    encoded_b, *kv_b = key_values(1, part_b, theirs_b)
    kv_b = [kv_b[0]] + [from_behind(kv_b[s], "tile", s) for s in range(1, tiles)]
    do_x = swapped(after(dec_out, encoded_b), "batch")
    encoded = jnp.concatenate([encoded_a, encoded_b], axis=0)

    def attend(queries, *earlier):
        count = len(queries)
        return call(
            functools.partial(cross_kernel, count, 2 * tiles),
            1,
            [((tokens, LANES), BF16)] * count,
            [
                pltpu.VMEM((tiles * rows, 3 * LANES), BF16),
                pltpu.VMEM((LANES // HEAD_DEC * tokens, LANES), BF16),
                pltpu.SemaphoreType.DMA((2 * tiles,)),
            ],
            *queries,
            *kv_a,
            *kv_b,
            specs=[VM] * count + [ANY] * (2 * tiles),
        )

    near = tiles // 2
    ctx_far = attend(q_in[near:])
    ctx_far_in = [from_behind(ctx_far[s - near], "tile", -s) for s in range(near, tiles)]
    ctx_near = attend([after(q_in[0], ctx_far[0]), *q_in[1:near]])
    ctx_in = [ctx_near[0]] + [from_behind(ctx_near[s], "tile", -s) for s in range(1, near)]
    ctx_in += ctx_far_in

    keep, send = call(
        functools.partial(out_kernel, tiles),
        2 * tokens * hq_dec * width,
        [((tokens // 2, width), F32), ((tokens // 2, width), BF16)],
        [pltpu.VMEM((tokens, hq_dec), BF16), pltpu.VMEM((tokens, width), F32)],
        *ctx_in,
        dec_out,
        do_x,
        text,
    )
    received = swapped(send, "mp")
    decoded = (keep + received.astype(F32)).astype(BF16)
    return (
        encoded.reshape(page_cells.shape),
        decoded.reshape(1, tokens // 2, width),
    )


def solution(mesh):
    placed = (
        P(("pages", "batch"), "tile", None, None),
        P(("pages", "batch"), "tile", None),
        P("batch", "mp"),
        P("batch", None, "mp"),
        P("mp", "batch"),
        P("batch", "mp"),
        P("batch", None, "mp"),
        P("mp", "batch"),
    )
    return jax.shard_map(
        body,
        mesh=mesh,
        in_specs=placed,
        out_specs=(
            P(("pages", "batch"), "tile", None, None),
            P(("pages", "batch"), ("tile", "mp"), None),
        ),
        check_vma=False,
    )
```

```python
import functools
import math

import jax
import jax.numpy as jnp
from jax import lax
from jax.experimental import pallas as pl
from jax.experimental.pallas import tpu as pltpu
from jax.sharding import PartitionSpec as P

HEAD_ENC = 32
HEAD_DEC = 64
LANES = 128
VMEM_LIMIT = 48 << 20
F32 = jnp.float32
BF16 = jnp.bfloat16


def from_behind(value, axis, by):
    devices = lax.axis_size(axis)
    return lax.ppermute(value, axis, [(i, (i + by) % devices) for i in range(devices)])


def layer_norm(values):
    center = values - jnp.mean(values, axis=-1, keepdims=True)
    variance = jnp.mean(center * center, axis=-1, keepdims=True)
    return center / jnp.sqrt(variance + 1e-05)


def regions(length, window, offset):
    index_row = jnp.arange(length, dtype=jnp.int32)
    return jnp.where(
        index_row < length - window, 0, jnp.where(index_row < length - offset, 1, 2)
    ).astype(jnp.int32)


def general_body(
    page_cells, text_states, enc_query, enc_keyval, enc_proj, dec_query, dec_keyval, dec_out
):
    wq_enc, wkv_enc, wproj_enc, wq_dec, wkv_dec, wout_dec = (
        lax.all_gather(enc_query, "batch", axis=0, tiled=True),
        lax.all_gather(enc_keyval, "batch", axis=0, tiled=True),
        lax.all_gather(enc_proj, "batch", axis=1, tiled=True),
        lax.all_gather(dec_query, "batch", axis=0, tiled=True),
        lax.all_gather(dec_keyval, "batch", axis=0, tiled=True),
        lax.all_gather(dec_out, "batch", axis=1, tiled=True),
    )
    pages_here, window, columns, width = page_cells.shape
    offset = window // 2
    own_rows = window * columns
    hq_enc = wq_enc.shape[1]
    heads_enc = hq_enc // HEAD_ENC
    joined = jnp.concatenate([wq_enc, wkv_enc.reshape(width, 2 * hq_enc)], axis=1)
    rows_below = from_behind(page_cells[:, :offset], "tile", -1)
    normed = layer_norm(
        jnp.concatenate([page_cells[:, offset:], rows_below], axis=1).astype(F32)
    ).astype(BF16)
    projected = jnp.einsum("prcd,de->prce", normed, joined, preferred_element_type=F32).astype(BF16)
    projected = jnp.roll(projected, -offset, axis=2)
    per_row = columns // window
    shaped = projected.reshape(pages_here, window, per_row, window, 3, heads_enc, HEAD_ENC)
    shaped = jnp.swapaxes(shaped, 1, 2).reshape(
        pages_here, per_row, window * window, 3, heads_enc, HEAD_ENC
    )
    win_q = shaped[:, :, :, 0]
    win_k = shaped[:, :, :, 1]
    win_v = shaped[:, :, :, 2]
    is_last = lax.axis_index("tile") == lax.axis_size("tile") - 1
    local_rows = jnp.arange(window, dtype=jnp.int32)
    row_region = jnp.where(is_last, jnp.where(local_rows < window - offset, 1, 2), 0).astype(
        jnp.int32
    )
    labels = row_region[:, None] * 3 + regions(columns, window, offset)[None, :]
    labels = jnp.swapaxes(labels.reshape(window, per_row, window), 0, 1).reshape(
        per_row, window * window
    )
    allowed = labels[:, :, None] == labels[:, None, :]
    win_scores = jnp.einsum(
        "pnqhd,pnkhd->pnhqk", win_q, win_k, preferred_element_type=F32
    ) / math.sqrt(HEAD_ENC)
    win_scores = jnp.where(allowed[None, :, None], win_scores, -jnp.inf)
    top = jnp.max(win_scores, axis=-1, keepdims=True)
    expd = jnp.exp(win_scores - top)
    win_weights = (expd / jnp.sum(expd, axis=-1, keepdims=True)).astype(BF16)
    win_out = jnp.einsum(
        "pnhqk,pnkhd->pnqhd", win_weights, win_v, preferred_element_type=F32
    ).astype(BF16)
    win_out = win_out.reshape(pages_here, per_row, window, window, hq_enc)
    win_out = jnp.swapaxes(win_out, 1, 2).reshape(pages_here, window, columns, hq_enc)
    win_out = jnp.roll(win_out, offset, axis=2)
    rows_above = from_behind(win_out[:, window - offset :], "tile", 1)
    unrolled = jnp.concatenate([rows_above, win_out[:, : window - offset]], axis=1)
    partial_proj = jnp.einsum("prce,ed->prcd", unrolled, wproj_enc, preferred_element_type=F32)
    summed = lax.psum(partial_proj.astype(BF16), "mp").astype(F32)
    encoded = (page_cells.astype(F32) + summed).astype(BF16)
    hq_dec = wq_dec.shape[1]
    heads_dec = hq_dec // HEAD_DEC
    page_normed = (
        layer_norm(encoded.astype(F32)).astype(BF16).reshape(pages_here, own_rows, width)
    )
    page_kv = jnp.einsum(
        "pnd,de->pne", page_normed, wkv_dec.reshape(width, 2 * hq_dec), preferred_element_type=F32
    ).astype(BF16)
    text_normed = layer_norm(text_states.astype(F32)).astype(BF16)
    queries = jnp.einsum("ptd,de->pte", text_normed, wq_dec, preferred_element_type=F32).astype(
        BF16
    )
    text_len = text_states.shape[1]
    query_heads = queries.reshape(pages_here, text_len, heads_dec, HEAD_DEC)
    carried = (
        jnp.full((pages_here, heads_dec, text_len), -jnp.inf, F32),
        jnp.zeros((pages_here, heads_dec, text_len), F32),
        jnp.zeros((pages_here, heads_dec, text_len, HEAD_DEC), F32),
    )
    shard_rows = lax.all_gather(page_kv, "tile", axis=1, tiled=True)
    count = shard_rows.shape[1] // own_rows
    grouped = max(
        (
            factor
            for factor in range(1, count + 1)
            if count % factor == 0 and factor * own_rows <= 2048
        )
    )
    blocks = jnp.moveaxis(
        shard_rows.reshape(pages_here, count // grouped, grouped * own_rows, 2 * hq_dec), 1, 0
    )

    def advance(running, block_kv):
        maxima, totals, accum = running
        span = block_kv.shape[1]
        block_keys = block_kv[..., :hq_dec].reshape(pages_here, span, heads_dec, HEAD_DEC)
        block_vals = block_kv[..., hq_dec:].reshape(pages_here, span, heads_dec, HEAD_DEC)
        cross_scores = jnp.einsum(
            "pqhd,pkhd->phqk", query_heads, block_keys, preferred_element_type=F32
        ) / math.sqrt(HEAD_DEC)
        newest = jnp.maximum(maxima, jnp.max(cross_scores, axis=-1))
        rescale = jnp.exp(maxima - newest)
        expo = jnp.exp(cross_scores - newest[..., None])
        totals = totals * rescale + jnp.sum(expo, axis=-1)
        accum = accum * rescale[..., None] + jnp.einsum(
            "phqk,pkhd->phqd", expo.astype(BF16), block_vals, preferred_element_type=F32
        )
        return ((newest, totals, accum), None)

    carried, unused = lax.scan(advance, carried, blocks)
    maxima, totals, accum = carried
    context = (
        jnp.transpose(accum / totals[..., None], (0, 2, 1, 3))
        .reshape(pages_here, text_len, hq_dec)
        .astype(BF16)
    )
    share = text_len // lax.axis_size("mp")
    mixed = lax.psum_scatter(
        jnp.einsum("pte,ed->tpd", context, wout_dec, preferred_element_type=F32).astype(BF16),
        "mp",
        scatter_dimension=0,
        tiled=True,
    ).astype(F32)
    own_text = lax.dynamic_slice_in_dim(text_states, lax.axis_index("mp") * share, share, 1)
    decoded = (own_text.astype(F32) + jnp.moveaxis(mixed, 0, 1)).astype(BF16)
    return (encoded, decoded)


def swapped(value, axis):
    return lax.ppermute(value, axis, [(0, 1), (1, 0)])


def norm_rows(ref):
    v = ref[...].astype(F32)
    center = v - jnp.mean(v, axis=-1, keepdims=True)
    variance = jnp.mean(center * center, axis=-1, keepdims=True)
    return (center / jnp.sqrt(variance + 1e-05)).astype(BF16)


def halves(width):
    b = lax.axis_index("batch")
    half = width // 2
    own = pl.multiple_of(b * half, half)
    other = pl.multiple_of((1 - b) * half, half)
    return pl.ds(own, half), pl.ds(other, half)


def dot(a, b):
    return jnp.dot(a, b, preferred_element_type=F32)


def dot_t(a, b):
    return lax.dot_general(a, b, (((1,), (1,)), ((), ())), preferred_element_type=F32)


def lane_head(shape, size):
    return lax.broadcasted_iota(jnp.int32, shape, 1) // size


LOG2E = math.log2(math.e)
EXCLUDED = -1e30


def col_group(col, offset):
    window = 2 * offset
    return jnp.where(col < offset, 0, 1 + jnp.maximum(col - offset, 0) // window)


def attend_part(stacked, keys, values, head_of, scale):
    rows = head_of.shape[0]
    s = dot_t(stacked, keys)
    top = jnp.max(s, axis=-1, keepdims=True)
    o = dot(jnp.exp2((s - top) * scale).astype(BF16), values)
    acc, total, highest = None, None, None
    for h in range(stacked.shape[0] // rows):
        block = slice(h * rows, (h + 1) * rows)
        here = (o[block, :LANES], o[block, LANES:], jnp.broadcast_to(top[block], (rows, LANES)))
        if acc is None:
            acc, total, highest = here
        else:
            acc, total, highest = (
                jnp.where(head_of == h, new, old) for new, old in zip(here, (acc, total, highest))
            )
    return acc, total, highest


def merged(first, second, scale):
    acc_1, total_1, top_1 = first
    acc_2, total_2, top_2 = second
    top = jnp.maximum(top_1, top_2)
    keep_1 = jnp.exp2((top_1 - top) * scale)
    keep_2 = jnp.exp2((top_2 - top) * scale)
    return (acc_1 * keep_1 + acc_2 * keep_2) / (total_1 * keep_1 + total_2 * keep_2)


def stack_heads(stacked, q, head_of):
    rows = head_of.shape[0]
    for h in range(stacked.shape[0] // rows):
        stacked[h * rows : (h + 1) * rows, :LANES] = jnp.where(head_of == h, q, jnp.zeros_like(q))


def window_marks(rows, columns, offset, edge):
    groups = columns // (2 * offset) + 1
    lane = lax.broadcasted_iota(jnp.int32, (rows, LANES), 1)
    group = col_group(lax.broadcasted_iota(jnp.int32, (rows, LANES), 0) % columns, offset)
    out = jnp.logical_and(lane < groups, lane != group)
    if edge is not None:
        out = jnp.logical_or(out, jnp.logical_and(lane == groups, edge))
    k_marks = jnp.where(out, jnp.full((rows, LANES), EXCLUDED, F32), 0.0).astype(BF16)
    q_marks = jnp.where(jnp.logical_or(lane == group, lane == groups), 1.0, 0.0).astype(BF16)
    return q_marks, k_marks


def spread(kx, vx, kv, marks):
    rows = kx.shape[0]
    hq = kv.shape[1] // 2
    ones = jnp.ones((rows, LANES), BF16)
    for g in range(hq // LANES):
        cols = slice(g * LANES, (g + 1) * LANES)
        wide = slice(2 * g * LANES, (2 * g + 1) * LANES)
        extra = slice((2 * g + 1) * LANES, (2 * g + 2) * LANES)
        kx[:, wide] = kv[:, cols]
        kx[:, extra] = marks
        vx[:, wide] = kv[:, hq + g * LANES : hq + (g + 1) * LANES]
        vx[:, extra] = ones


def own_kernel(
    columns, page, wq_o, wq_x, wkv_o, wkv_x, q_out, acc, total, top, xn, kx, vx, ql
):
    rows = page.shape[0]
    half_rows = rows // 2
    hq = q_out.shape[1]
    own, other = halves(page.shape[1])
    xn[...] = norm_rows(page)
    q_out[...] = (dot(xn[:, own], wq_o[...]) + dot(xn[:, other], wq_x[...])).astype(BF16)
    kv = (dot(xn[:, own], wkv_o[...]) + dot(xn[:, other], wkv_x[...])).astype(BF16)
    offset = half_rows // columns
    spread(kx, vx, kv, window_marks(rows, columns, offset, None)[1])
    q_marks = window_marks(half_rows, columns, offset, None)[0]
    head_of = lane_head((half_rows, LANES), HEAD_ENC)
    scale = LOG2E / math.sqrt(HEAD_ENC)
    for h in range(LANES // HEAD_ENC):
        ql[h * half_rows : (h + 1) * half_rows, LANES:] = q_marks
    for half in range(2):
        here = slice(half * half_rows, (half + 1) * half_rows)
        for g in range(hq // LANES):
            cols = slice(g * LANES, (g + 1) * LANES)
            both = slice(2 * g * LANES, (2 * g + 2) * LANES)
            stack_heads(ql, q_out[here, cols], head_of)
            state = attend_part(ql[...], kx[here, both], vx[here, both], head_of, scale)
            acc[here, cols], total[here, cols], top[here, cols] = state


def win_kernel(
    columns, half, q_own, acc, total, top, halo, wkv_o, wkv_x, wp_o, wp_x, part, xn, kx, vx, ql, wo
):
    rows, width = halo.shape
    hq = q_own.shape[1]
    own, other = halves(width)
    xn[...] = norm_rows(halo)
    kv = (dot(xn[:, own], wkv_o[...]) + dot(xn[:, other], wkv_x[...])).astype(BF16)
    tile = lax.axis_index("tile")
    edge = tile == (0 if half == 0 else lax.axis_size("tile") - 1)
    q_marks, k_marks = window_marks(rows, columns, rows // columns, edge)
    spread(kx, vx, kv, k_marks)
    head_of = lane_head((rows, LANES), HEAD_ENC)
    scale = LOG2E / math.sqrt(HEAD_ENC)
    for h in range(LANES // HEAD_ENC):
        ql[h * rows : (h + 1) * rows, LANES:] = q_marks
    here = slice(half * rows, (half + 1) * rows)
    for g in range(hq // LANES):
        cols = slice(g * LANES, (g + 1) * LANES)
        both = slice(2 * g * LANES, (2 * g + 2) * LANES)
        stack_heads(ql, q_own[here, cols], head_of)
        state = attend_part(ql[...], kx[:, both], vx[:, both], head_of, scale)
        first = (acc[here, cols], total[here, cols], top[here, cols])
        wo[:, cols] = merged(first, state, scale).astype(BF16)
    part[:, own] = dot(wo[...], wp_o[...]).astype(BF16)
    part[:, other] = dot(wo[...], wp_x[...]).astype(BF16)


def pieces(scratch, first_col, outs, out_col):
    tiles = len(outs)
    tile = lax.axis_index("tile")
    for s in range(tiles):
        dest = lax.rem(tile + s, tiles)
        start = pl.multiple_of(dest * LANES + first_col, LANES)
        outs[s][:, out_col : out_col + LANES] = scratch[:, pl.ds(start, LANES)]


def kv_kernel(half, page, mine, theirs, wkv_o, wkv_x, encoded, *rest):
    outs, (xn, kvs) = rest[:-2], rest[-2:]
    rows, width = mine.shape
    own, other = halves(width)
    total = mine[...].astype(F32) + theirs[...].astype(F32)
    here = page[half * rows : (half + 1) * rows, :]
    encoded[...] = (here.astype(F32) + total).astype(BF16)
    xn[...] = norm_rows(encoded)
    kvs[...] = (dot(xn[:, own], wkv_o[...]) + dot(xn[:, other], wkv_x[...])).astype(BF16)
    pieces(kvs, 0, outs, 0)
    pieces(kvs, kvs.shape[1] // 2, outs, LANES)


def query_kernel(text, wq_o, wq_x, *rest):
    outs, (xn, qs) = rest[:-2], rest[-2:]
    own, other = halves(text.shape[1])
    xn[...] = norm_rows(text)
    qs[...] = (dot(xn[:, own], wq_o[...]) + dot(xn[:, other], wq_x[...])).astype(BF16)
    pieces(qs, 0, outs, 0)


def load_strips(kv_in, kv, sem):
    rows = kv_in[0].shape[0]
    copies = [
        pltpu.make_async_copy(
            strip, kv.at[pl.ds(s * rows, rows), pl.ds(0, 2 * LANES)], sem.at[s]
        )
        for s, strip in enumerate(kv_in)
    ]
    for copy in copies:
        copy.start()
    kv[:, 2 * LANES :] = jnp.ones((kv.shape[0], LANES), BF16)
    for copy in copies:
        copy.wait()


def cross_first_kernel(tiles, *refs):
    q_in = refs[:tiles]
    kv_in = refs[tiles : 2 * tiles]
    acc, total, top, kv, ql, sem = refs[2 * tiles :]
    load_strips(kv_in, kv, sem)
    tokens = q_in[0].shape[0]
    head_of = lane_head(q_in[0].shape, HEAD_DEC)
    scale = LOG2E / math.sqrt(HEAD_DEC)
    for s in range(tiles):
        here = slice(s * tokens, (s + 1) * tokens)
        stack_heads(ql, q_in[s][...], head_of)
        state = attend_part(ql[...], kv[:, :LANES], kv[:, LANES:], head_of, scale)
        acc[here], total[here], top[here] = state


def cross_kernel(first, count, tiles, *refs):
    q_in = refs[:count]
    kv_in = refs[count : count + tiles]
    acc, total, top, keep, send, kv, ql, ctx, sem = refs[count + tiles :]
    load_strips(kv_in, kv, sem)
    tokens = q_in[0].shape[0]
    head_of = lane_head(q_in[0].shape, HEAD_DEC)
    scale = LOG2E / math.sqrt(HEAD_DEC)
    half = tokens // 2
    m = lax.axis_index("mp")
    own_rows = pl.ds(pl.multiple_of(m * half, half), half)
    send_rows = pl.ds(pl.multiple_of((1 - m) * half, half), half)
    for s in range(count):
        here = slice((first + s) * tokens, (first + s + 1) * tokens)
        stack_heads(ql, q_in[s][...], head_of)
        state = attend_part(ql[...], kv[:, :LANES], kv[:, LANES:], head_of, scale)
        ctx[...] = merged((acc[here], total[here], top[here]), state, scale).astype(BF16)
        keep[s * half : (s + 1) * half] = ctx[own_rows, :]
        send[s * half : (s + 1) * half] = ctx[send_rows, :]


def out_kernel(tiles, *refs):
    ctx_in = refs[:tiles]
    w_own, w_batch, w_mp, w_both, text, decoded, ctx = refs[tiles:]
    half = decoded.shape[0]
    width = decoded.shape[1]
    own, other = halves(width)
    tile = lax.axis_index("tile")
    m = lax.axis_index("mp")
    own_rows = pl.ds(pl.multiple_of(m * half, half), half)
    for s in range(tiles):
        start = lax.rem(tile + s, tiles) * LANES
        here = pl.ds(pl.multiple_of(start, LANES), LANES)
        there = pl.ds(pl.multiple_of(tiles * LANES + start, LANES), LANES)
        ctx[:, here] = ctx_in[s][:half]
        ctx[:, there] = ctx_in[s][half:]
    mine = ctx[:, : tiles * LANES]
    theirs = ctx[:, tiles * LANES :]
    for cols, first, second in ((own, w_own, w_mp), (other, w_batch, w_both)):
        mixed = dot(mine, first[...]) + dot(theirs, second[...])
        decoded[:, cols] = (text[own_rows, cols].astype(F32) + mixed).astype(BF16)


VM = pl.BlockSpec(memory_space=pltpu.VMEM)
ANY = pl.BlockSpec(memory_space=pl.ANY)


def call(kernel, flops, outs, scratch, *args, specs=None):
    moved = sum(math.prod(a.shape) * 2 for a in args) + sum(math.prod(s) * 2 for s, _ in outs)
    return pl.pallas_call(
        kernel,
        out_shape=[jax.ShapeDtypeStruct(shape, dtype) for shape, dtype in outs],
        in_specs=specs or [VM] * len(args),
        out_specs=[VM] * len(outs),
        scratch_shapes=scratch,
        cost_estimate=pl.CostEstimate(flops=flops, transcendentals=0, bytes_accessed=moved)
        if flops
        else None,
        compiler_params=pltpu.CompilerParams(vmem_limit_bytes=VMEM_LIMIT),
    )(*args)


def after(value, *earlier):
    return lax.optimization_barrier((value,) + earlier)[0]


def body(page_cells, text_states, enc_query, enc_keyval, enc_proj, dec_query, dec_keyval, dec_out):
    tiles = lax.axis_size("tile")
    pages_here, window, columns, width = page_cells.shape
    hq_enc = enc_query.shape[1]
    hq_dec = dec_query.shape[1]
    if (
        pages_here != 1
        or lax.axis_size("batch") != 2
        or lax.axis_size("mp") != 2
        or hq_dec != tiles * LANES
        or hq_enc % LANES
    ):
        return general_body(
            page_cells, text_states, enc_query, enc_keyval, enc_proj, dec_query, dec_keyval, dec_out
        )
    rows = window * columns
    half_rows = rows // 2
    page = page_cells.reshape(rows, width)
    text = text_states.reshape(-1, width)
    tokens = text.shape[0]
    up = [(i, i + 1) for i in range(tiles - 1)]
    down = [(i + 1, i) for i in range(tiles - 1)]
    upper, lower = page[:half_rows], page[half_rows:]
    above = lax.ppermute(lower, "tile", up)
    below = lax.ppermute(upper, "tile", down)
    wkv_x = swapped(enc_keyval, "batch").reshape(width // 2, 2 * hq_enc)
    wkv_enc = enc_keyval.reshape(width // 2, 2 * hq_enc)
    wq_x = swapped(enc_query, "batch")
    dq_x = swapped(dec_query, "batch")

    q_own, *win_state = call(
        functools.partial(own_kernel, columns),
        1,
        [((rows, hq_enc), BF16)] + [((rows, hq_enc), F32)] * 3,
        [
            pltpu.VMEM((rows, width), BF16),
            pltpu.VMEM((rows, 2 * hq_enc), BF16),
            pltpu.VMEM((rows, 2 * hq_enc), BF16),
            pltpu.VMEM((LANES // HEAD_ENC * half_rows, 2 * LANES), BF16),
        ],
        page,
        enc_query,
        wq_x,
        wkv_enc,
        wkv_x,
    )
    q_out = call(
        query_kernel,
        1,
        [((tokens, LANES), BF16)] * tiles,
        [pltpu.VMEM((tokens, width), BF16), pltpu.VMEM((tokens, hq_dec), BF16)],
        after(text, q_own),
        dec_query,
        dq_x,
    )
    q_in = [q_out[0]] + [from_behind(q_out[s], "tile", s) for s in range(1, tiles)]

    wp_x = swapped(enc_proj, "batch")
    above, below = lax.optimization_barrier((above, below, *q_out))[:2]

    def window_half(half, halo):
        (part,) = call(
            functools.partial(win_kernel, columns, half),
            2 * half_rows * width * 3 * hq_enc + 8 * half_rows * rows * LANES * hq_enc // HEAD_ENC,
            [((half_rows, width), BF16)],
            [
                pltpu.VMEM((half_rows, width), BF16),
                pltpu.VMEM((half_rows, 2 * hq_enc), BF16),
                pltpu.VMEM((half_rows, 2 * hq_enc), BF16),
                pltpu.VMEM((LANES // HEAD_ENC * half_rows, 2 * LANES), BF16),
                pltpu.VMEM((half_rows, hq_enc), BF16),
            ],
            q_own,
            *win_state,
            halo,
            wkv_enc,
            wkv_x,
            enc_proj,
            wp_x,
        )
        return part

    def key_values(half, part, theirs):
        return call(
            functools.partial(kv_kernel, half),
            2 * half_rows * width * 2 * hq_dec,
            [((half_rows, width), BF16)] + [((half_rows, 2 * LANES), BF16)] * tiles,
            [pltpu.VMEM((half_rows, width), BF16), pltpu.VMEM((half_rows, 2 * hq_dec), BF16)],
            page,
            part,
            theirs,
            wkv_dec,
            dkv_x,
        )

    part_a = window_half(0, above)
    wkv_dec = after(dec_keyval, part_a).reshape(width // 2, 2 * hq_dec)
    dkv_x = swapped(wkv_dec, "batch")
    theirs_a = swapped(part_a, "mp")
    part_b = window_half(1, after(below, part_a))
    theirs_b = swapped(part_b, "mp")
    encoded_a, *kv_a = key_values(0, part_a, theirs_a)
    kv_a, q_in = lax.optimization_barrier((list(kv_a), q_in))
    kv_a = [kv_a[0]] + [from_behind(kv_a[s], "tile", s) for s in range(1, tiles)]
    theirs_b, *kv_a = lax.optimization_barrier((theirs_b, *kv_a))
    encoded_b, *kv_b = key_values(1, part_b, theirs_b)
    kv_b = [kv_b[0]] + [from_behind(kv_b[s], "tile", s) for s in range(1, tiles)]
    out_half = after(dec_out, encoded_b)
    do_x = swapped(out_half, "batch")
    do_m = swapped(out_half, "mp")
    do_mx = swapped(do_m, "batch")
    encoded = jnp.concatenate([encoded_a, encoded_b], axis=0)

    cross_scratch = [
        pltpu.VMEM((tiles * half_rows, 3 * LANES), BF16),
        pltpu.VMEM((LANES // HEAD_DEC * tokens, LANES), BF16),
    ]
    arrivals = pltpu.SemaphoreType.DMA((tiles,))
    cross_state = call(
        functools.partial(cross_first_kernel, tiles),
        1,
        [((tiles * tokens, LANES), F32)] * 3,
        cross_scratch + [arrivals],
        *q_in,
        *kv_a,
        specs=[VM] * tiles + [ANY] * tiles,
    )

    def attend(first, queries):
        count = len(queries)
        return call(
            functools.partial(cross_kernel, first, count, tiles),
            1,
            [((count * tokens // 2, LANES), BF16)] * 2,
            cross_scratch + [pltpu.VMEM((tokens, LANES), BF16), arrivals],
            *queries,
            *kv_b,
            *cross_state,
            specs=[VM] * count + [ANY] * tiles + [VM] * 3,
        )

    def joined(keep, other, index):
        span = slice(index * tokens // 2, (index + 1) * tokens // 2)
        return jnp.concatenate([keep[span], other[span]], axis=0)

    near = tiles // 2
    keep_far, send_far = attend(near, q_in[near:])
    other_far = swapped(send_far, "mp")
    keep_near, send_near = attend(0, [after(q_in[0], keep_far), *q_in[1:near]])
    other_near = swapped(send_near, "mp")
    ctx_in = [joined(keep_near, other_near, 0)]
    for s in range(1, near):
        ctx_in.append(from_behind(joined(keep_near, other_near, s), "tile", -s))
    for s in range(near, tiles):
        ctx_in.append(from_behind(joined(keep_far, other_far, s - near), "tile", -s))

    (decoded,) = call(
        functools.partial(out_kernel, tiles),
        2 * tokens * hq_dec * width,
        [((tokens // 2, width), BF16)],
        [pltpu.VMEM((tokens // 2, 2 * hq_dec), BF16)],
        *ctx_in,
        dec_out,
        do_x,
        do_m,
        do_mx,
        text,
    )
    return (
        encoded.reshape(page_cells.shape),
        decoded.reshape(1, tokens // 2, width),
    )


def solution(mesh):
    placed = (
        P(("pages", "batch"), "tile", None, None),
        P(("pages", "batch"), "tile", None),
        P("batch", "mp"),
        P("batch", None, "mp"),
        P("mp", "batch"),
        P("batch", "mp"),
        P("batch", None, "mp"),
        P("mp", "batch"),
    )
    return jax.shard_map(
        body,
        mesh=mesh,
        in_specs=placed,
        out_specs=(
            P(("pages", "batch"), "tile", None, None),
            P(("pages", "batch"), ("tile", "mp"), None),
        ),
        check_vma=False,
    )
```

```python
import functools
import math

import jax
import jax.numpy as jnp
from jax import lax
from jax.experimental import pallas as pl
from jax.experimental.pallas import tpu as pltpu
from jax.sharding import PartitionSpec as P

HEAD_ENC = 32
HEAD_DEC = 64
LANES = 128
VMEM_LIMIT = 48 << 20
F32 = jnp.float32
BF16 = jnp.bfloat16


def from_behind(value, axis, by):
    devices = lax.axis_size(axis)
    return lax.ppermute(value, axis, [(i, (i + by) % devices) for i in range(devices)])


def layer_norm(values):
    center = values - jnp.mean(values, axis=-1, keepdims=True)
    variance = jnp.mean(center * center, axis=-1, keepdims=True)
    return center / jnp.sqrt(variance + 1e-05)


def regions(length, window, offset):
    index_row = jnp.arange(length, dtype=jnp.int32)
    return jnp.where(
        index_row < length - window, 0, jnp.where(index_row < length - offset, 1, 2)
    ).astype(jnp.int32)


def general_body(
    page_cells, text_states, enc_query, enc_keyval, enc_proj, dec_query, dec_keyval, dec_out
):
    wq_enc, wkv_enc, wproj_enc, wq_dec, wkv_dec, wout_dec = (
        lax.all_gather(enc_query, "batch", axis=0, tiled=True),
        lax.all_gather(enc_keyval, "batch", axis=0, tiled=True),
        lax.all_gather(enc_proj, "batch", axis=1, tiled=True),
        lax.all_gather(dec_query, "batch", axis=0, tiled=True),
        lax.all_gather(dec_keyval, "batch", axis=0, tiled=True),
        lax.all_gather(dec_out, "batch", axis=1, tiled=True),
    )
    pages_here, window, columns, width = page_cells.shape
    offset = window // 2
    own_rows = window * columns
    hq_enc = wq_enc.shape[1]
    heads_enc = hq_enc // HEAD_ENC
    joined = jnp.concatenate([wq_enc, wkv_enc.reshape(width, 2 * hq_enc)], axis=1)
    rows_below = from_behind(page_cells[:, :offset], "tile", -1)
    normed = layer_norm(
        jnp.concatenate([page_cells[:, offset:], rows_below], axis=1).astype(F32)
    ).astype(BF16)
    projected = jnp.einsum("prcd,de->prce", normed, joined, preferred_element_type=F32).astype(BF16)
    projected = jnp.roll(projected, -offset, axis=2)
    per_row = columns // window
    shaped = projected.reshape(pages_here, window, per_row, window, 3, heads_enc, HEAD_ENC)
    shaped = jnp.swapaxes(shaped, 1, 2).reshape(
        pages_here, per_row, window * window, 3, heads_enc, HEAD_ENC
    )
    win_q = shaped[:, :, :, 0]
    win_k = shaped[:, :, :, 1]
    win_v = shaped[:, :, :, 2]
    is_last = lax.axis_index("tile") == lax.axis_size("tile") - 1
    local_rows = jnp.arange(window, dtype=jnp.int32)
    row_region = jnp.where(is_last, jnp.where(local_rows < window - offset, 1, 2), 0).astype(
        jnp.int32
    )
    labels = row_region[:, None] * 3 + regions(columns, window, offset)[None, :]
    labels = jnp.swapaxes(labels.reshape(window, per_row, window), 0, 1).reshape(
        per_row, window * window
    )
    allowed = labels[:, :, None] == labels[:, None, :]
    win_scores = jnp.einsum(
        "pnqhd,pnkhd->pnhqk", win_q, win_k, preferred_element_type=F32
    ) / math.sqrt(HEAD_ENC)
    win_scores = jnp.where(allowed[None, :, None], win_scores, -jnp.inf)
    top = jnp.max(win_scores, axis=-1, keepdims=True)
    expd = jnp.exp(win_scores - top)
    win_weights = (expd / jnp.sum(expd, axis=-1, keepdims=True)).astype(BF16)
    win_out = jnp.einsum(
        "pnhqk,pnkhd->pnqhd", win_weights, win_v, preferred_element_type=F32
    ).astype(BF16)
    win_out = win_out.reshape(pages_here, per_row, window, window, hq_enc)
    win_out = jnp.swapaxes(win_out, 1, 2).reshape(pages_here, window, columns, hq_enc)
    win_out = jnp.roll(win_out, offset, axis=2)
    rows_above = from_behind(win_out[:, window - offset :], "tile", 1)
    unrolled = jnp.concatenate([rows_above, win_out[:, : window - offset]], axis=1)
    partial_proj = jnp.einsum("prce,ed->prcd", unrolled, wproj_enc, preferred_element_type=F32)
    summed = lax.psum(partial_proj.astype(BF16), "mp").astype(F32)
    encoded = (page_cells.astype(F32) + summed).astype(BF16)
    hq_dec = wq_dec.shape[1]
    heads_dec = hq_dec // HEAD_DEC
    page_normed = (
        layer_norm(encoded.astype(F32)).astype(BF16).reshape(pages_here, own_rows, width)
    )
    page_kv = jnp.einsum(
        "pnd,de->pne", page_normed, wkv_dec.reshape(width, 2 * hq_dec), preferred_element_type=F32
    ).astype(BF16)
    text_normed = layer_norm(text_states.astype(F32)).astype(BF16)
    queries = jnp.einsum("ptd,de->pte", text_normed, wq_dec, preferred_element_type=F32).astype(
        BF16
    )
    text_len = text_states.shape[1]
    query_heads = queries.reshape(pages_here, text_len, heads_dec, HEAD_DEC)
    carried = (
        jnp.full((pages_here, heads_dec, text_len), -jnp.inf, F32),
        jnp.zeros((pages_here, heads_dec, text_len), F32),
        jnp.zeros((pages_here, heads_dec, text_len, HEAD_DEC), F32),
    )
    shard_rows = lax.all_gather(page_kv, "tile", axis=1, tiled=True)
    count = shard_rows.shape[1] // own_rows
    grouped = max(
        (
            factor
            for factor in range(1, count + 1)
            if count % factor == 0 and factor * own_rows <= 2048
        )
    )
    blocks = jnp.moveaxis(
        shard_rows.reshape(pages_here, count // grouped, grouped * own_rows, 2 * hq_dec), 1, 0
    )

    def advance(running, block_kv):
        maxima, totals, accum = running
        span = block_kv.shape[1]
        block_keys = block_kv[..., :hq_dec].reshape(pages_here, span, heads_dec, HEAD_DEC)
        block_vals = block_kv[..., hq_dec:].reshape(pages_here, span, heads_dec, HEAD_DEC)
        cross_scores = jnp.einsum(
            "pqhd,pkhd->phqk", query_heads, block_keys, preferred_element_type=F32
        ) / math.sqrt(HEAD_DEC)
        newest = jnp.maximum(maxima, jnp.max(cross_scores, axis=-1))
        rescale = jnp.exp(maxima - newest)
        expo = jnp.exp(cross_scores - newest[..., None])
        totals = totals * rescale + jnp.sum(expo, axis=-1)
        accum = accum * rescale[..., None] + jnp.einsum(
            "phqk,pkhd->phqd", expo.astype(BF16), block_vals, preferred_element_type=F32
        )
        return ((newest, totals, accum), None)

    carried, unused = lax.scan(advance, carried, blocks)
    maxima, totals, accum = carried
    context = (
        jnp.transpose(accum / totals[..., None], (0, 2, 1, 3))
        .reshape(pages_here, text_len, hq_dec)
        .astype(BF16)
    )
    share = text_len // lax.axis_size("mp")
    mixed = lax.psum_scatter(
        jnp.einsum("pte,ed->tpd", context, wout_dec, preferred_element_type=F32).astype(BF16),
        "mp",
        scatter_dimension=0,
        tiled=True,
    ).astype(F32)
    own_text = lax.dynamic_slice_in_dim(text_states, lax.axis_index("mp") * share, share, 1)
    decoded = (own_text.astype(F32) + jnp.moveaxis(mixed, 0, 1)).astype(BF16)
    return (encoded, decoded)


def swapped(value, axis):
    return lax.ppermute(value, axis, [(0, 1), (1, 0)])


def norm_rows(ref):
    v = ref[...].astype(F32)
    center = v - jnp.mean(v, axis=-1, keepdims=True)
    variance = jnp.mean(center * center, axis=-1, keepdims=True)
    return (center / jnp.sqrt(variance + 1e-05)).astype(BF16)


def halves(width):
    b = lax.axis_index("batch")
    half = width // 2
    own = pl.multiple_of(b * half, half)
    other = pl.multiple_of((1 - b) * half, half)
    return pl.ds(own, half), pl.ds(other, half)


def dot(a, b):
    return jnp.dot(a, b, preferred_element_type=F32)


def dot_t(a, b):
    return lax.dot_general(a, b, (((1,), (1,)), ((), ())), preferred_element_type=F32)


def lane_head(shape, size):
    return lax.broadcasted_iota(jnp.int32, shape, 1) // size


LOG2E = math.log2(math.e)
EXCLUDED = -1e30


def col_group(col, offset):
    window = 2 * offset
    return jnp.where(col < offset, 0, 1 + jnp.maximum(col - offset, 0) // window)


def attend_part(stacked, keys, values, head_of, scale):
    rows = head_of.shape[0]
    s = dot_t(stacked, keys)
    top = jnp.max(s, axis=-1, keepdims=True)
    o = dot(jnp.exp2((s - top) * scale).astype(BF16), values)
    acc, total, highest = None, None, None
    for h in range(stacked.shape[0] // rows):
        block = slice(h * rows, (h + 1) * rows)
        here = (o[block, :LANES], o[block, LANES:], jnp.broadcast_to(top[block], (rows, LANES)))
        if acc is None:
            acc, total, highest = here
        else:
            acc, total, highest = (
                jnp.where(head_of == h, new, old) for new, old in zip(here, (acc, total, highest))
            )
    return acc, total, highest


def merged(first, second, scale):
    acc_1, total_1, top_1 = first
    acc_2, total_2, top_2 = second
    top = jnp.maximum(top_1, top_2)
    keep_1 = jnp.exp2((top_1 - top) * scale)
    keep_2 = jnp.exp2((top_2 - top) * scale)
    return (acc_1 * keep_1 + acc_2 * keep_2) / (total_1 * keep_1 + total_2 * keep_2)


def stack_heads(stacked, q, head_of):
    rows = head_of.shape[0]
    for h in range(stacked.shape[0] // rows):
        stacked[h * rows : (h + 1) * rows, :LANES] = jnp.where(head_of == h, q, jnp.zeros_like(q))


def window_marks(rows, columns, offset, edge):
    groups = columns // (2 * offset) + 1
    lane = lax.broadcasted_iota(jnp.int32, (rows, LANES), 1)
    group = col_group(lax.broadcasted_iota(jnp.int32, (rows, LANES), 0) % columns, offset)
    out = jnp.logical_and(lane < groups, lane != group)
    if edge is not None:
        out = jnp.logical_or(out, jnp.logical_and(lane == groups, edge))
    k_marks = jnp.where(out, jnp.full((rows, LANES), EXCLUDED, F32), 0.0).astype(BF16)
    q_marks = jnp.where(jnp.logical_or(lane == group, lane == groups), 1.0, 0.0).astype(BF16)
    return q_marks, k_marks


def spread(kx, vx, kv, marks):
    rows = kx.shape[0]
    hq = kv.shape[1] // 2
    ones = jnp.ones((rows, LANES), BF16)
    for g in range(hq // LANES):
        cols = slice(g * LANES, (g + 1) * LANES)
        wide = slice(2 * g * LANES, (2 * g + 1) * LANES)
        extra = slice((2 * g + 1) * LANES, (2 * g + 2) * LANES)
        kx[:, wide] = kv[:, cols]
        kx[:, extra] = marks
        vx[:, wide] = kv[:, hq + g * LANES : hq + (g + 1) * LANES]
        vx[:, extra] = ones


def own_kernel(
    columns, page, wq_o, wq_x, wkv_o, wkv_x, q_out, acc, total, top, xn, kx, vx, ql
):
    rows = page.shape[0]
    half_rows = rows // 2
    hq = q_out.shape[1]
    own, other = halves(page.shape[1])
    xn[...] = norm_rows(page)
    q_out[...] = (dot(xn[:, own], wq_o[...]) + dot(xn[:, other], wq_x[...])).astype(BF16)
    kv = (dot(xn[:, own], wkv_o[...]) + dot(xn[:, other], wkv_x[...])).astype(BF16)
    offset = half_rows // columns
    spread(kx, vx, kv, window_marks(rows, columns, offset, None)[1])
    q_marks = window_marks(half_rows, columns, offset, None)[0]
    head_of = lane_head((half_rows, LANES), HEAD_ENC)
    scale = LOG2E / math.sqrt(HEAD_ENC)
    for h in range(LANES // HEAD_ENC):
        ql[h * half_rows : (h + 1) * half_rows, LANES:] = q_marks
    for half in range(2):
        here = slice(half * half_rows, (half + 1) * half_rows)
        for g in range(hq // LANES):
            cols = slice(g * LANES, (g + 1) * LANES)
            both = slice(2 * g * LANES, (2 * g + 2) * LANES)
            stack_heads(ql, q_out[here, cols], head_of)
            state = attend_part(ql[...], kx[here, both], vx[here, both], head_of, scale)
            acc[here, cols], total[here, cols], top[here, cols] = state


def win_kernel(
    columns, half, q_own, acc, total, top, halo, wkv_o, wkv_x, wp_o, wp_x, part, xn, kx, vx, ql, wo
):
    rows, width = halo.shape
    hq = q_own.shape[1]
    own, other = halves(width)
    xn[...] = norm_rows(halo)
    kv = (dot(xn[:, own], wkv_o[...]) + dot(xn[:, other], wkv_x[...])).astype(BF16)
    tile = lax.axis_index("tile")
    edge = tile == (0 if half == 0 else lax.axis_size("tile") - 1)
    q_marks, k_marks = window_marks(rows, columns, rows // columns, edge)
    spread(kx, vx, kv, k_marks)
    head_of = lane_head((rows, LANES), HEAD_ENC)
    scale = LOG2E / math.sqrt(HEAD_ENC)
    for h in range(LANES // HEAD_ENC):
        ql[h * rows : (h + 1) * rows, LANES:] = q_marks
    here = slice(half * rows, (half + 1) * rows)
    for g in range(hq // LANES):
        cols = slice(g * LANES, (g + 1) * LANES)
        both = slice(2 * g * LANES, (2 * g + 2) * LANES)
        stack_heads(ql, q_own[here, cols], head_of)
        state = attend_part(ql[...], kx[:, both], vx[:, both], head_of, scale)
        first = (acc[here, cols], total[here, cols], top[here, cols])
        wo[:, cols] = merged(first, state, scale).astype(BF16)
    part[:, own] = dot(wo[...], wp_o[...]).astype(BF16)
    part[:, other] = dot(wo[...], wp_x[...]).astype(BF16)


def pieces(scratch, first_col, outs, out_col):
    tiles = len(outs)
    tile = lax.axis_index("tile")
    for s in range(tiles):
        dest = lax.rem(tile + s, tiles)
        start = pl.multiple_of(dest * LANES + first_col, LANES)
        outs[s][:, out_col : out_col + LANES] = scratch[:, pl.ds(start, LANES)]


def kv_kernel(half, page, mine, theirs, wkv_o, wkv_x, encoded, *rest):
    outs, (xn, kvs) = rest[:-2], rest[-2:]
    rows, width = mine.shape
    own, other = halves(width)
    total = mine[...].astype(F32) + theirs[...].astype(F32)
    here = page[half * rows : (half + 1) * rows, :]
    encoded[...] = (here.astype(F32) + total).astype(BF16)
    xn[...] = norm_rows(encoded)
    kvs[...] = (dot(xn[:, own], wkv_o[...]) + dot(xn[:, other], wkv_x[...])).astype(BF16)
    pieces(kvs, 0, outs, 0)
    pieces(kvs, kvs.shape[1] // 2, outs, LANES)


def query_kernel(text, wq_o, wq_x, *rest):
    outs, (xn, qs) = rest[:-2], rest[-2:]
    own, other = halves(text.shape[1])
    xn[...] = norm_rows(text)
    qs[...] = (dot(xn[:, own], wq_o[...]) + dot(xn[:, other], wq_x[...])).astype(BF16)
    pieces(qs, 0, outs, 0)


def load_strips(kv_in, kv, sem):
    rows = kv_in[0].shape[0]
    copies = [
        pltpu.make_async_copy(
            strip, kv.at[pl.ds(s * rows, rows), pl.ds(0, 2 * LANES)], sem.at[s]
        )
        for s, strip in enumerate(kv_in)
    ]
    for copy in copies:
        copy.start()
    kv[:, 2 * LANES :] = jnp.ones((kv.shape[0], LANES), BF16)
    for copy in copies:
        copy.wait()


def cross_first_kernel(tiles, *refs):
    q_in = refs[:tiles]
    kv_in = refs[tiles : 2 * tiles]
    acc, total, top, kv, ql, sem = refs[2 * tiles :]
    load_strips(kv_in, kv, sem)
    tokens = q_in[0].shape[0]
    head_of = lane_head(q_in[0].shape, HEAD_DEC)
    scale = LOG2E / math.sqrt(HEAD_DEC)
    for s in range(tiles):
        here = slice(s * tokens, (s + 1) * tokens)
        stack_heads(ql, q_in[s][...], head_of)
        state = attend_part(ql[...], kv[:, :LANES], kv[:, LANES:], head_of, scale)
        acc[here], total[here], top[here] = state


def cross_kernel(first, count, tiles, *refs):
    q_in = refs[:count]
    kv_in = refs[count : count + tiles]
    acc, total, top, keep, send, kv, ql, ctx, sem = refs[count + tiles :]
    load_strips(kv_in, kv, sem)
    tokens = q_in[0].shape[0]
    head_of = lane_head(q_in[0].shape, HEAD_DEC)
    scale = LOG2E / math.sqrt(HEAD_DEC)
    half = tokens // 2
    m = lax.axis_index("mp")
    own_rows = pl.ds(pl.multiple_of(m * half, half), half)
    send_rows = pl.ds(pl.multiple_of((1 - m) * half, half), half)
    for s in range(count):
        here = slice((first + s) * tokens, (first + s + 1) * tokens)
        stack_heads(ql, q_in[s][...], head_of)
        state = attend_part(ql[...], kv[:, :LANES], kv[:, LANES:], head_of, scale)
        ctx[...] = merged((acc[here], total[here], top[here]), state, scale).astype(BF16)
        keep[s * half : (s + 1) * half] = ctx[own_rows, :]
        send[s * half : (s + 1) * half] = ctx[send_rows, :]


def out_kernel(tiles, *refs):
    ctx_in = refs[:tiles]
    w_own, w_batch, w_mp, w_both, text, decoded, ctx = refs[tiles:]
    half = decoded.shape[0]
    width = decoded.shape[1]
    own, other = halves(width)
    tile = lax.axis_index("tile")
    m = lax.axis_index("mp")
    own_rows = pl.ds(pl.multiple_of(m * half, half), half)
    for s in range(tiles):
        start = lax.rem(tile + s, tiles) * LANES
        here = pl.ds(pl.multiple_of(start, LANES), LANES)
        there = pl.ds(pl.multiple_of(tiles * LANES + start, LANES), LANES)
        ctx[:, here] = ctx_in[s][:half]
        ctx[:, there] = ctx_in[s][half:]
    mine = ctx[:, : tiles * LANES]
    theirs = ctx[:, tiles * LANES :]
    for cols, first, second in ((own, w_own, w_mp), (other, w_batch, w_both)):
        mixed = dot(mine, first[...]) + dot(theirs, second[...])
        decoded[:, cols] = (text[own_rows, cols].astype(F32) + mixed).astype(BF16)


VM = pl.BlockSpec(memory_space=pltpu.VMEM)
ANY = pl.BlockSpec(memory_space=pl.ANY)


def call(kernel, flops, outs, scratch, *args, specs=None):
    moved = sum(math.prod(a.shape) * 2 for a in args) + sum(math.prod(s) * 2 for s, _ in outs)
    return pl.pallas_call(
        kernel,
        out_shape=[jax.ShapeDtypeStruct(shape, dtype) for shape, dtype in outs],
        in_specs=specs or [VM] * len(args),
        out_specs=[VM] * len(outs),
        scratch_shapes=scratch,
        cost_estimate=pl.CostEstimate(flops=flops, transcendentals=0, bytes_accessed=moved)
        if flops
        else None,
        compiler_params=pltpu.CompilerParams(vmem_limit_bytes=VMEM_LIMIT),
    )(*args)


def after(value, *earlier):
    return lax.optimization_barrier((value,) + earlier)[0]


def body(page_cells, text_states, enc_query, enc_keyval, enc_proj, dec_query, dec_keyval, dec_out):
    tiles = lax.axis_size("tile")
    pages_here, window, columns, width = page_cells.shape
    hq_enc = enc_query.shape[1]
    hq_dec = dec_query.shape[1]
    if (
        pages_here != 1
        or lax.axis_size("batch") != 2
        or lax.axis_size("mp") != 2
        or hq_dec != tiles * LANES
        or hq_enc % LANES
    ):
        return general_body(
            page_cells, text_states, enc_query, enc_keyval, enc_proj, dec_query, dec_keyval, dec_out
        )
    rows = window * columns
    half_rows = rows // 2
    page = page_cells.reshape(rows, width)
    text = text_states.reshape(-1, width)
    tokens = text.shape[0]
    up = [(i, i + 1) for i in range(tiles - 1)]
    down = [(i + 1, i) for i in range(tiles - 1)]
    upper, lower = page[:half_rows], page[half_rows:]
    above = lax.ppermute(lower, "tile", up)
    below = lax.ppermute(upper, "tile", down)
    wkv_x = swapped(enc_keyval, "batch").reshape(width // 2, 2 * hq_enc)
    wkv_enc = enc_keyval.reshape(width // 2, 2 * hq_enc)
    wq_x = swapped(enc_query, "batch")
    dq_x = swapped(dec_query, "batch")
    dkv_x = swapped(dec_keyval, "batch").reshape(width // 2, 2 * hq_dec)
    wkv_dec = dec_keyval.reshape(width // 2, 2 * hq_dec)

    q_own, *win_state = call(
        functools.partial(own_kernel, columns),
        1,
        [((rows, hq_enc), BF16)] + [((rows, hq_enc), F32)] * 3,
        [
            pltpu.VMEM((rows, width), BF16),
            pltpu.VMEM((rows, 2 * hq_enc), BF16),
            pltpu.VMEM((rows, 2 * hq_enc), BF16),
            pltpu.VMEM((LANES // HEAD_ENC * half_rows, 2 * LANES), BF16),
        ],
        page,
        enc_query,
        wq_x,
        wkv_enc,
        wkv_x,
    )
    q_out = call(
        query_kernel,
        1,
        [((tokens, LANES), BF16)] * tiles,
        [pltpu.VMEM((tokens, width), BF16), pltpu.VMEM((tokens, hq_dec), BF16)],
        after(text, q_own),
        dec_query,
        dq_x,
    )
    q_in = [q_out[0]] + [from_behind(q_out[s], "tile", s) for s in range(1, tiles)]

    wp_x = swapped(enc_proj, "batch")
    above = after(above, *q_out)

    def window_half(half, halo):
        (part,) = call(
            functools.partial(win_kernel, columns, half),
            2 * half_rows * width * 3 * hq_enc + 8 * half_rows * rows * LANES * hq_enc // HEAD_ENC,
            [((half_rows, width), BF16)],
            [
                pltpu.VMEM((half_rows, width), BF16),
                pltpu.VMEM((half_rows, 2 * hq_enc), BF16),
                pltpu.VMEM((half_rows, 2 * hq_enc), BF16),
                pltpu.VMEM((LANES // HEAD_ENC * half_rows, 2 * LANES), BF16),
                pltpu.VMEM((half_rows, hq_enc), BF16),
            ],
            q_own,
            *win_state,
            halo,
            wkv_enc,
            wkv_x,
            enc_proj,
            wp_x,
        )
        return part

    def key_values(half, part, theirs):
        return call(
            functools.partial(kv_kernel, half),
            2 * half_rows * width * 2 * hq_dec,
            [((half_rows, width), BF16)] + [((half_rows, 2 * LANES), BF16)] * tiles,
            [pltpu.VMEM((half_rows, width), BF16), pltpu.VMEM((half_rows, 2 * hq_dec), BF16)],
            page,
            part,
            theirs,
            wkv_dec,
            dkv_x,
        )

    part_a = window_half(0, above)
    theirs_a = swapped(part_a, "mp")
    part_b = window_half(1, after(below, part_a))
    theirs_b = swapped(part_b, "mp")
    encoded_a, *kv_a = key_values(0, part_a, theirs_a)
    kv_a, q_in = lax.optimization_barrier((list(kv_a), q_in))
    kv_a = [kv_a[0]] + [from_behind(kv_a[s], "tile", s) for s in range(1, tiles)]
    theirs_b, *kv_a = lax.optimization_barrier((theirs_b, *kv_a))
    encoded_b, *kv_b = key_values(1, part_b, theirs_b)
    kv_b = [kv_b[0]] + [from_behind(kv_b[s], "tile", s) for s in range(1, tiles)]
    out_half = after(dec_out, encoded_b)
    do_x = swapped(out_half, "batch")
    do_m = swapped(out_half, "mp")
    do_mx = swapped(do_m, "batch")
    encoded = jnp.concatenate([encoded_a, encoded_b], axis=0)

    cross_scratch = [
        pltpu.VMEM((tiles * half_rows, 3 * LANES), BF16),
        pltpu.VMEM((LANES // HEAD_DEC * tokens, LANES), BF16),
    ]
    arrivals = pltpu.SemaphoreType.DMA((tiles,))
    cross_state = call(
        functools.partial(cross_first_kernel, tiles),
        1,
        [((tiles * tokens, LANES), F32)] * 3,
        cross_scratch + [arrivals],
        *q_in,
        *kv_a,
        specs=[VM] * tiles + [ANY] * tiles,
    )

    def attend(first, queries):
        count = len(queries)
        return call(
            functools.partial(cross_kernel, first, count, tiles),
            1,
            [((count * tokens // 2, LANES), BF16)] * 2,
            cross_scratch + [pltpu.VMEM((tokens, LANES), BF16), arrivals],
            *queries,
            *kv_b,
            *cross_state,
            specs=[VM] * count + [ANY] * tiles + [VM] * 3,
        )

    def joined(keep, other, index):
        span = slice(index * tokens // 2, (index + 1) * tokens // 2)
        return jnp.concatenate([keep[span], other[span]], axis=0)

    near = tiles // 2
    keep_far, send_far = attend(near, q_in[near:])
    other_far = swapped(send_far, "mp")
    keep_near, send_near = attend(0, [after(q_in[0], keep_far), *q_in[1:near]])
    other_near = swapped(send_near, "mp")
    ctx_in = [joined(keep_near, other_near, 0)]
    for s in range(1, near):
        ctx_in.append(from_behind(joined(keep_near, other_near, s), "tile", -s))
    for s in range(near, tiles):
        ctx_in.append(from_behind(joined(keep_far, other_far, s - near), "tile", -s))

    (decoded,) = call(
        functools.partial(out_kernel, tiles),
        2 * tokens * hq_dec * width,
        [((tokens // 2, width), BF16)],
        [pltpu.VMEM((tokens // 2, 2 * hq_dec), BF16)],
        *ctx_in,
        dec_out,
        do_x,
        do_m,
        do_mx,
        text,
    )
    return (
        encoded.reshape(page_cells.shape),
        decoded.reshape(1, tokens // 2, width),
    )


def solution(mesh):
    placed = (
        P(("pages", "batch"), "tile", None, None),
        P(("pages", "batch"), "tile", None),
        P("batch", "mp"),
        P("batch", None, "mp"),
        P("mp", "batch"),
        P("batch", "mp"),
        P("batch", None, "mp"),
        P("mp", "batch"),
    )
    return jax.shard_map(
        body,
        mesh=mesh,
        in_specs=placed,
        out_specs=(
            P(("pages", "batch"), "tile", None, None),
            P(("pages", "batch"), ("tile", "mp"), None),
        ),
        check_vma=False,
    )
```

```python
import functools
import math

import jax
import jax.numpy as jnp
from jax import lax
from jax.experimental import pallas as pl
from jax.experimental.pallas import tpu as pltpu
from jax.sharding import PartitionSpec as P

HEAD_ENC = 32
HEAD_DEC = 64
LANES = 128
VMEM_LIMIT = 48 << 20
F32 = jnp.float32
BF16 = jnp.bfloat16


def from_behind(value, axis, by):
    devices = lax.axis_size(axis)
    return lax.ppermute(value, axis, [(i, (i + by) % devices) for i in range(devices)])


def layer_norm(values):
    center = values - jnp.mean(values, axis=-1, keepdims=True)
    variance = jnp.mean(center * center, axis=-1, keepdims=True)
    return center / jnp.sqrt(variance + 1e-05)


def regions(length, window, offset):
    index_row = jnp.arange(length, dtype=jnp.int32)
    return jnp.where(
        index_row < length - window, 0, jnp.where(index_row < length - offset, 1, 2)
    ).astype(jnp.int32)


def general_body(
    page_cells, text_states, enc_query, enc_keyval, enc_proj, dec_query, dec_keyval, dec_out
):
    wq_enc, wkv_enc, wproj_enc, wq_dec, wkv_dec, wout_dec = (
        lax.all_gather(enc_query, "batch", axis=0, tiled=True),
        lax.all_gather(enc_keyval, "batch", axis=0, tiled=True),
        lax.all_gather(enc_proj, "batch", axis=1, tiled=True),
        lax.all_gather(dec_query, "batch", axis=0, tiled=True),
        lax.all_gather(dec_keyval, "batch", axis=0, tiled=True),
        lax.all_gather(dec_out, "batch", axis=1, tiled=True),
    )
    pages_here, window, columns, width = page_cells.shape
    offset = window // 2
    own_rows = window * columns
    hq_enc = wq_enc.shape[1]
    heads_enc = hq_enc // HEAD_ENC
    joined = jnp.concatenate([wq_enc, wkv_enc.reshape(width, 2 * hq_enc)], axis=1)
    rows_below = from_behind(page_cells[:, :offset], "tile", -1)
    normed = layer_norm(
        jnp.concatenate([page_cells[:, offset:], rows_below], axis=1).astype(F32)
    ).astype(BF16)
    projected = jnp.einsum("prcd,de->prce", normed, joined, preferred_element_type=F32).astype(BF16)
    projected = jnp.roll(projected, -offset, axis=2)
    per_row = columns // window
    shaped = projected.reshape(pages_here, window, per_row, window, 3, heads_enc, HEAD_ENC)
    shaped = jnp.swapaxes(shaped, 1, 2).reshape(
        pages_here, per_row, window * window, 3, heads_enc, HEAD_ENC
    )
    win_q = shaped[:, :, :, 0]
    win_k = shaped[:, :, :, 1]
    win_v = shaped[:, :, :, 2]
    is_last = lax.axis_index("tile") == lax.axis_size("tile") - 1
    local_rows = jnp.arange(window, dtype=jnp.int32)
    row_region = jnp.where(is_last, jnp.where(local_rows < window - offset, 1, 2), 0).astype(
        jnp.int32
    )
    labels = row_region[:, None] * 3 + regions(columns, window, offset)[None, :]
    labels = jnp.swapaxes(labels.reshape(window, per_row, window), 0, 1).reshape(
        per_row, window * window
    )
    allowed = labels[:, :, None] == labels[:, None, :]
    win_scores = jnp.einsum(
        "pnqhd,pnkhd->pnhqk", win_q, win_k, preferred_element_type=F32
    ) / math.sqrt(HEAD_ENC)
    win_scores = jnp.where(allowed[None, :, None], win_scores, -jnp.inf)
    top = jnp.max(win_scores, axis=-1, keepdims=True)
    expd = jnp.exp(win_scores - top)
    win_weights = (expd / jnp.sum(expd, axis=-1, keepdims=True)).astype(BF16)
    win_out = jnp.einsum(
        "pnhqk,pnkhd->pnqhd", win_weights, win_v, preferred_element_type=F32
    ).astype(BF16)
    win_out = win_out.reshape(pages_here, per_row, window, window, hq_enc)
    win_out = jnp.swapaxes(win_out, 1, 2).reshape(pages_here, window, columns, hq_enc)
    win_out = jnp.roll(win_out, offset, axis=2)
    rows_above = from_behind(win_out[:, window - offset :], "tile", 1)
    unrolled = jnp.concatenate([rows_above, win_out[:, : window - offset]], axis=1)
    partial_proj = jnp.einsum("prce,ed->prcd", unrolled, wproj_enc, preferred_element_type=F32)
    summed = lax.psum(partial_proj.astype(BF16), "mp").astype(F32)
    encoded = (page_cells.astype(F32) + summed).astype(BF16)
    hq_dec = wq_dec.shape[1]
    heads_dec = hq_dec // HEAD_DEC
    page_normed = (
        layer_norm(encoded.astype(F32)).astype(BF16).reshape(pages_here, own_rows, width)
    )
    page_kv = jnp.einsum(
        "pnd,de->pne", page_normed, wkv_dec.reshape(width, 2 * hq_dec), preferred_element_type=F32
    ).astype(BF16)
    text_normed = layer_norm(text_states.astype(F32)).astype(BF16)
    queries = jnp.einsum("ptd,de->pte", text_normed, wq_dec, preferred_element_type=F32).astype(
        BF16
    )
    text_len = text_states.shape[1]
    query_heads = queries.reshape(pages_here, text_len, heads_dec, HEAD_DEC)
    carried = (
        jnp.full((pages_here, heads_dec, text_len), -jnp.inf, F32),
        jnp.zeros((pages_here, heads_dec, text_len), F32),
        jnp.zeros((pages_here, heads_dec, text_len, HEAD_DEC), F32),
    )
    shard_rows = lax.all_gather(page_kv, "tile", axis=1, tiled=True)
    count = shard_rows.shape[1] // own_rows
    grouped = max(
        (
            factor
            for factor in range(1, count + 1)
            if count % factor == 0 and factor * own_rows <= 2048
        )
    )
    blocks = jnp.moveaxis(
        shard_rows.reshape(pages_here, count // grouped, grouped * own_rows, 2 * hq_dec), 1, 0
    )

    def advance(running, block_kv):
        maxima, totals, accum = running
        span = block_kv.shape[1]
        block_keys = block_kv[..., :hq_dec].reshape(pages_here, span, heads_dec, HEAD_DEC)
        block_vals = block_kv[..., hq_dec:].reshape(pages_here, span, heads_dec, HEAD_DEC)
        cross_scores = jnp.einsum(
            "pqhd,pkhd->phqk", query_heads, block_keys, preferred_element_type=F32
        ) / math.sqrt(HEAD_DEC)
        newest = jnp.maximum(maxima, jnp.max(cross_scores, axis=-1))
        rescale = jnp.exp(maxima - newest)
        expo = jnp.exp(cross_scores - newest[..., None])
        totals = totals * rescale + jnp.sum(expo, axis=-1)
        accum = accum * rescale[..., None] + jnp.einsum(
            "phqk,pkhd->phqd", expo.astype(BF16), block_vals, preferred_element_type=F32
        )
        return ((newest, totals, accum), None)

    carried, unused = lax.scan(advance, carried, blocks)
    maxima, totals, accum = carried
    context = (
        jnp.transpose(accum / totals[..., None], (0, 2, 1, 3))
        .reshape(pages_here, text_len, hq_dec)
        .astype(BF16)
    )
    share = text_len // lax.axis_size("mp")
    mixed = lax.psum_scatter(
        jnp.einsum("pte,ed->tpd", context, wout_dec, preferred_element_type=F32).astype(BF16),
        "mp",
        scatter_dimension=0,
        tiled=True,
    ).astype(F32)
    own_text = lax.dynamic_slice_in_dim(text_states, lax.axis_index("mp") * share, share, 1)
    decoded = (own_text.astype(F32) + jnp.moveaxis(mixed, 0, 1)).astype(BF16)
    return (encoded, decoded)


def swapped(value, axis):
    return lax.ppermute(value, axis, [(0, 1), (1, 0)])


def norm_rows(ref):
    v = ref[...].astype(F32)
    center = v - jnp.mean(v, axis=-1, keepdims=True)
    variance = jnp.mean(center * center, axis=-1, keepdims=True)
    return (center / jnp.sqrt(variance + 1e-05)).astype(BF16)


def halves(width):
    b = lax.axis_index("batch")
    half = width // 2
    own = pl.multiple_of(b * half, half)
    other = pl.multiple_of((1 - b) * half, half)
    return pl.ds(own, half), pl.ds(other, half)


def dot(a, b):
    return jnp.dot(a, b, preferred_element_type=F32)


def dot_t(a, b):
    return lax.dot_general(a, b, (((1,), (1,)), ((), ())), preferred_element_type=F32)


def lane_head(shape, size):
    return lax.broadcasted_iota(jnp.int32, shape, 1) // size


LOG2E = math.log2(math.e)
EXCLUDED = -1e30


def col_group(col, offset):
    window = 2 * offset
    return jnp.where(col < offset, 0, 1 + jnp.maximum(col - offset, 0) // window)


def attend_part(stacked, keys, values, head_of, scale):
    rows = head_of.shape[0]
    s = dot_t(stacked, keys)
    top = jnp.max(s, axis=-1, keepdims=True)
    o = dot(jnp.exp2((s - top) * scale).astype(BF16), values)
    acc, total, highest = None, None, None
    for h in range(stacked.shape[0] // rows):
        block = slice(h * rows, (h + 1) * rows)
        here = (o[block, :LANES], o[block, LANES:], jnp.broadcast_to(top[block], (rows, LANES)))
        if acc is None:
            acc, total, highest = here
        else:
            acc, total, highest = (
                jnp.where(head_of == h, new, old) for new, old in zip(here, (acc, total, highest))
            )
    return acc, total, highest


def merged(first, second, scale):
    acc_1, total_1, top_1 = first
    acc_2, total_2, top_2 = second
    top = jnp.maximum(top_1, top_2)
    keep_1 = jnp.exp2((top_1 - top) * scale)
    keep_2 = jnp.exp2((top_2 - top) * scale)
    return (acc_1 * keep_1 + acc_2 * keep_2) / (total_1 * keep_1 + total_2 * keep_2)


def stack_heads(stacked, q, head_of):
    rows = head_of.shape[0]
    for h in range(stacked.shape[0] // rows):
        stacked[h * rows : (h + 1) * rows, :LANES] = jnp.where(head_of == h, q, jnp.zeros_like(q))


def window_marks(rows, columns, offset, edge):
    groups = columns // (2 * offset) + 1
    lane = lax.broadcasted_iota(jnp.int32, (rows, LANES), 1)
    group = col_group(lax.broadcasted_iota(jnp.int32, (rows, LANES), 0) % columns, offset)
    out = jnp.logical_and(lane < groups, lane != group)
    if edge is not None:
        out = jnp.logical_or(out, jnp.logical_and(lane == groups, edge))
    k_marks = jnp.where(out, jnp.full((rows, LANES), EXCLUDED, F32), 0.0).astype(BF16)
    q_marks = jnp.where(jnp.logical_or(lane == group, lane == groups), 1.0, 0.0).astype(BF16)
    return q_marks, k_marks


def spread(kx, vx, kv, marks):
    rows = kx.shape[0]
    hq = kv.shape[1] // 2
    ones = jnp.ones((rows, LANES), BF16)
    for g in range(hq // LANES):
        cols = slice(g * LANES, (g + 1) * LANES)
        wide = slice(2 * g * LANES, (2 * g + 1) * LANES)
        extra = slice((2 * g + 1) * LANES, (2 * g + 2) * LANES)
        kx[:, wide] = kv[:, cols]
        kx[:, extra] = marks
        vx[:, wide] = kv[:, hq + g * LANES : hq + (g + 1) * LANES]
        vx[:, extra] = ones


def own_kernel(
    columns, page, wq_o, wq_x, wkv_o, wkv_x, q_out, acc, total, top, xn, kx, vx, ql
):
    rows = page.shape[0]
    half_rows = rows // 2
    hq = q_out.shape[1]
    own, other = halves(page.shape[1])
    xn[...] = norm_rows(page)
    q_out[...] = (dot(xn[:, own], wq_o[...]) + dot(xn[:, other], wq_x[...])).astype(BF16)
    kv = (dot(xn[:, own], wkv_o[...]) + dot(xn[:, other], wkv_x[...])).astype(BF16)
    offset = half_rows // columns
    spread(kx, vx, kv, window_marks(rows, columns, offset, None)[1])
    q_marks = window_marks(half_rows, columns, offset, None)[0]
    head_of = lane_head((half_rows, LANES), HEAD_ENC)
    scale = LOG2E / math.sqrt(HEAD_ENC)
    for h in range(LANES // HEAD_ENC):
        ql[h * half_rows : (h + 1) * half_rows, LANES:] = q_marks
    for half in range(2):
        here = slice(half * half_rows, (half + 1) * half_rows)
        for g in range(hq // LANES):
            cols = slice(g * LANES, (g + 1) * LANES)
            both = slice(2 * g * LANES, (2 * g + 2) * LANES)
            stack_heads(ql, q_out[here, cols], head_of)
            state = attend_part(ql[...], kx[here, both], vx[here, both], head_of, scale)
            acc[here, cols], total[here, cols], top[here, cols] = state


def win_kernel(
    columns, half, q_own, acc, total, top, halo, wkv_o, wkv_x, wp_o, wp_x, part, xn, kx, vx, ql, wo
):
    rows, width = halo.shape
    hq = q_own.shape[1]
    own, other = halves(width)
    xn[...] = norm_rows(halo)
    kv = (dot(xn[:, own], wkv_o[...]) + dot(xn[:, other], wkv_x[...])).astype(BF16)
    tile = lax.axis_index("tile")
    edge = tile == (0 if half == 0 else lax.axis_size("tile") - 1)
    q_marks, k_marks = window_marks(rows, columns, rows // columns, edge)
    spread(kx, vx, kv, k_marks)
    head_of = lane_head((rows, LANES), HEAD_ENC)
    scale = LOG2E / math.sqrt(HEAD_ENC)
    for h in range(LANES // HEAD_ENC):
        ql[h * rows : (h + 1) * rows, LANES:] = q_marks
    here = slice(half * rows, (half + 1) * rows)
    for g in range(hq // LANES):
        cols = slice(g * LANES, (g + 1) * LANES)
        both = slice(2 * g * LANES, (2 * g + 2) * LANES)
        stack_heads(ql, q_own[here, cols], head_of)
        state = attend_part(ql[...], kx[:, both], vx[:, both], head_of, scale)
        first = (acc[here, cols], total[here, cols], top[here, cols])
        wo[:, cols] = merged(first, state, scale).astype(BF16)
    part[:, own] = dot(wo[...], wp_o[...]).astype(BF16)
    part[:, other] = dot(wo[...], wp_x[...]).astype(BF16)


def pieces(scratch, first_col, outs, out_col):
    tiles = len(outs)
    tile = lax.axis_index("tile")
    for s in range(tiles):
        dest = lax.rem(tile + s, tiles)
        start = pl.multiple_of(dest * LANES + first_col, LANES)
        outs[s][:, out_col : out_col + LANES] = scratch[:, pl.ds(start, LANES)]


def kv_kernel(half, page, mine, theirs, wkv_o, wkv_x, encoded, *rest):
    outs, (xn, kvs) = rest[:-2], rest[-2:]
    rows, width = mine.shape
    own, other = halves(width)
    total = mine[...].astype(F32) + theirs[...].astype(F32)
    here = page[half * rows : (half + 1) * rows, :]
    encoded[...] = (here.astype(F32) + total).astype(BF16)
    xn[...] = norm_rows(encoded)
    kvs[...] = (dot(xn[:, own], wkv_o[...]) + dot(xn[:, other], wkv_x[...])).astype(BF16)
    pieces(kvs, 0, outs, 0)
    pieces(kvs, kvs.shape[1] // 2, outs, LANES)


def query_kernel(text, wq_o, wq_x, *rest):
    outs, (xn, qs) = rest[:-2], rest[-2:]
    own, other = halves(text.shape[1])
    xn[...] = norm_rows(text)
    qs[...] = (dot(xn[:, own], wq_o[...]) + dot(xn[:, other], wq_x[...])).astype(BF16)
    pieces(qs, 0, outs, 0)


def load_strips(kv_in, kv, sem):
    rows = kv_in[0].shape[0]
    copies = [
        pltpu.make_async_copy(
            strip, kv.at[pl.ds(s * rows, rows), pl.ds(0, 2 * LANES)], sem.at[s]
        )
        for s, strip in enumerate(kv_in)
    ]
    for copy in copies:
        copy.start()
    kv[:, 2 * LANES :] = jnp.ones((kv.shape[0], LANES), BF16)
    for copy in copies:
        copy.wait()


def cross_first_kernel(tiles, *refs):
    q_in = refs[:tiles]
    kv_in = refs[tiles : 2 * tiles]
    acc, total, top, kv, ql, sem = refs[2 * tiles :]
    load_strips(kv_in, kv, sem)
    tokens = q_in[0].shape[0]
    head_of = lane_head(q_in[0].shape, HEAD_DEC)
    scale = LOG2E / math.sqrt(HEAD_DEC)
    for s in range(tiles):
        here = slice(s * tokens, (s + 1) * tokens)
        stack_heads(ql, q_in[s][...], head_of)
        state = attend_part(ql[...], kv[:, :LANES], kv[:, LANES:], head_of, scale)
        acc[here], total[here], top[here] = state


def cross_kernel(first, count, tiles, *refs):
    q_in = refs[:count]
    kv_in = refs[count : count + tiles]
    acc, total, top, keep, send, kv, ql, ctx, sem = refs[count + tiles :]
    load_strips(kv_in, kv, sem)
    tokens = q_in[0].shape[0]
    head_of = lane_head(q_in[0].shape, HEAD_DEC)
    scale = LOG2E / math.sqrt(HEAD_DEC)
    half = tokens // 2
    m = lax.axis_index("mp")
    own_rows = pl.ds(pl.multiple_of(m * half, half), half)
    send_rows = pl.ds(pl.multiple_of((1 - m) * half, half), half)
    for s in range(count):
        here = slice((first + s) * tokens, (first + s + 1) * tokens)
        stack_heads(ql, q_in[s][...], head_of)
        state = attend_part(ql[...], kv[:, :LANES], kv[:, LANES:], head_of, scale)
        ctx[...] = merged((acc[here], total[here], top[here]), state, scale).astype(BF16)
        keep[s * half : (s + 1) * half] = ctx[own_rows, :]
        send[s * half : (s + 1) * half] = ctx[send_rows, :]


def out_kernel(tiles, *refs):
    ctx_in = refs[:tiles]
    w_own, w_batch, w_mp, w_both, text, decoded, ctx = refs[tiles:]
    half = decoded.shape[0]
    width = decoded.shape[1]
    own, other = halves(width)
    tile = lax.axis_index("tile")
    m = lax.axis_index("mp")
    own_rows = pl.ds(pl.multiple_of(m * half, half), half)
    for s in range(tiles):
        start = lax.rem(tile + s, tiles) * LANES
        here = pl.ds(pl.multiple_of(start, LANES), LANES)
        there = pl.ds(pl.multiple_of(tiles * LANES + start, LANES), LANES)
        ctx[:, here] = ctx_in[s][:half]
        ctx[:, there] = ctx_in[s][half:]
    mine = ctx[:, : tiles * LANES]
    theirs = ctx[:, tiles * LANES :]
    for cols, first, second in ((own, w_own, w_mp), (other, w_batch, w_both)):
        mixed = dot(mine, first[...]) + dot(theirs, second[...])
        decoded[:, cols] = (text[own_rows, cols].astype(F32) + mixed).astype(BF16)


VM = pl.BlockSpec(memory_space=pltpu.VMEM)
ANY = pl.BlockSpec(memory_space=pl.ANY)


def call(kernel, flops, outs, scratch, *args, specs=None):
    moved = sum(math.prod(a.shape) * 2 for a in args) + sum(math.prod(s) * 2 for s, _ in outs)
    return pl.pallas_call(
        kernel,
        out_shape=[jax.ShapeDtypeStruct(shape, dtype) for shape, dtype in outs],
        in_specs=specs or [VM] * len(args),
        out_specs=[VM] * len(outs),
        scratch_shapes=scratch,
        cost_estimate=pl.CostEstimate(flops=flops, transcendentals=0, bytes_accessed=moved)
        if flops
        else None,
        compiler_params=pltpu.CompilerParams(vmem_limit_bytes=VMEM_LIMIT),
    )(*args)


def after(value, *earlier):
    return lax.optimization_barrier((value,) + earlier)[0]


def body(page_cells, text_states, enc_query, enc_keyval, enc_proj, dec_query, dec_keyval, dec_out):
    tiles = lax.axis_size("tile")
    pages_here, window, columns, width = page_cells.shape
    hq_enc = enc_query.shape[1]
    hq_dec = dec_query.shape[1]
    if (
        pages_here != 1
        or lax.axis_size("batch") != 2
        or lax.axis_size("mp") != 2
        or hq_dec != tiles * LANES
        or hq_enc % LANES
    ):
        return general_body(
            page_cells, text_states, enc_query, enc_keyval, enc_proj, dec_query, dec_keyval, dec_out
        )
    rows = window * columns
    half_rows = rows // 2
    page = page_cells.reshape(rows, width)
    text = text_states.reshape(-1, width)
    tokens = text.shape[0]
    up = [(i, i + 1) for i in range(tiles - 1)]
    down = [(i + 1, i) for i in range(tiles - 1)]
    upper, lower = page[:half_rows], page[half_rows:]
    above = lax.ppermute(lower, "tile", up)
    below = lax.ppermute(upper, "tile", down)
    wkv_x = swapped(enc_keyval, "batch").reshape(width // 2, 2 * hq_enc)
    wkv_enc = enc_keyval.reshape(width // 2, 2 * hq_enc)
    wq_x = swapped(enc_query, "batch")
    dq_x = swapped(dec_query, "batch")
    dkv_x = swapped(dec_keyval, "batch").reshape(width // 2, 2 * hq_dec)
    wkv_dec = dec_keyval.reshape(width // 2, 2 * hq_dec)

    q_own, *win_state = call(
        functools.partial(own_kernel, columns),
        1,
        [((rows, hq_enc), BF16)] + [((rows, hq_enc), F32)] * 3,
        [
            pltpu.VMEM((rows, width), BF16),
            pltpu.VMEM((rows, 2 * hq_enc), BF16),
            pltpu.VMEM((rows, 2 * hq_enc), BF16),
            pltpu.VMEM((LANES // HEAD_ENC * half_rows, 2 * LANES), BF16),
        ],
        page,
        enc_query,
        wq_x,
        wkv_enc,
        wkv_x,
    )
    q_out = call(
        query_kernel,
        1,
        [((tokens, LANES), BF16)] * tiles,
        [pltpu.VMEM((tokens, width), BF16), pltpu.VMEM((tokens, hq_dec), BF16)],
        after(text, q_own),
        dec_query,
        dq_x,
    )
    q_in = [q_out[0]] + [from_behind(q_out[s], "tile", s) for s in range(1, tiles)]

    wp_x = swapped(enc_proj, "batch")
    above = after(above, *q_out)

    def window_half(half, halo):
        (part,) = call(
            functools.partial(win_kernel, columns, half),
            2 * half_rows * width * 3 * hq_enc + 8 * half_rows * rows * LANES * hq_enc // HEAD_ENC,
            [((half_rows, width), BF16)],
            [
                pltpu.VMEM((half_rows, width), BF16),
                pltpu.VMEM((half_rows, 2 * hq_enc), BF16),
                pltpu.VMEM((half_rows, 2 * hq_enc), BF16),
                pltpu.VMEM((LANES // HEAD_ENC * half_rows, 2 * LANES), BF16),
                pltpu.VMEM((half_rows, hq_enc), BF16),
            ],
            q_own,
            *win_state,
            halo,
            wkv_enc,
            wkv_x,
            enc_proj,
            wp_x,
        )
        return part

    def key_values(half, part, theirs):
        return call(
            functools.partial(kv_kernel, half),
            2 * half_rows * width * 2 * hq_dec,
            [((half_rows, width), BF16)] + [((half_rows, 2 * LANES), BF16)] * tiles,
            [pltpu.VMEM((half_rows, width), BF16), pltpu.VMEM((half_rows, 2 * hq_dec), BF16)],
            page,
            part,
            theirs,
            wkv_dec,
            dkv_x,
        )

    part_a = window_half(0, above)
    theirs_a = swapped(part_a, "mp")
    part_b = window_half(1, after(below, part_a))
    theirs_b = swapped(part_b, "mp")
    encoded_a, *kv_a = key_values(0, part_a, theirs_a)
    kv_a = [kv_a[0]] + [from_behind(kv_a[s], "tile", s) for s in range(1, tiles)]
    theirs_b, kv_a, q_in = lax.optimization_barrier((theirs_b, kv_a, q_in))
    encoded_b, *kv_b = key_values(1, part_b, theirs_b)
    kv_b = [kv_b[0]] + [from_behind(kv_b[s], "tile", s) for s in range(1, tiles)]
    out_half = after(dec_out, kv_a[1])
    do_x = swapped(out_half, "batch")
    do_m = swapped(out_half, "mp")
    do_mx = swapped(do_m, "batch")
    encoded = jnp.concatenate([encoded_a, encoded_b], axis=0)

    cross_scratch = [
        pltpu.VMEM((tiles * half_rows, 3 * LANES), BF16),
        pltpu.VMEM((LANES // HEAD_DEC * tokens, LANES), BF16),
    ]
    arrivals = pltpu.SemaphoreType.DMA((tiles,))
    cross_state = call(
        functools.partial(cross_first_kernel, tiles),
        1,
        [((tiles * tokens, LANES), F32)] * 3,
        cross_scratch + [arrivals],
        *q_in,
        *kv_a,
        specs=[VM] * tiles + [ANY] * tiles,
    )

    def attend(first, queries):
        count = len(queries)
        return call(
            functools.partial(cross_kernel, first, count, tiles),
            1,
            [((count * tokens // 2, LANES), BF16)] * 2,
            cross_scratch + [pltpu.VMEM((tokens, LANES), BF16), arrivals],
            *queries,
            *kv_b,
            *cross_state,
            specs=[VM] * count + [ANY] * tiles + [VM] * 3,
        )

    def joined(keep, other, index):
        span = slice(index * tokens // 2, (index + 1) * tokens // 2)
        return jnp.concatenate([keep[span], other[span]], axis=0)

    near = tiles // 2
    keep_far, send_far = attend(near, q_in[near:])
    other_far = swapped(send_far, "mp")
    keep_near, send_near = attend(0, [after(q_in[0], keep_far), *q_in[1:near]])
    other_near = swapped(send_near, "mp")
    ctx_in = [joined(keep_near, other_near, 0)]
    for s in range(1, near):
        ctx_in.append(from_behind(joined(keep_near, other_near, s), "tile", -s))
    for s in range(near, tiles):
        ctx_in.append(from_behind(joined(keep_far, other_far, s - near), "tile", -s))

    (decoded,) = call(
        functools.partial(out_kernel, tiles),
        2 * tokens * hq_dec * width,
        [((tokens // 2, width), BF16)],
        [pltpu.VMEM((tokens // 2, 2 * hq_dec), BF16)],
        *ctx_in,
        dec_out,
        do_x,
        do_m,
        do_mx,
        text,
    )
    return (
        encoded.reshape(page_cells.shape),
        decoded.reshape(1, tokens // 2, width),
    )


def solution(mesh):
    placed = (
        P(("pages", "batch"), "tile", None, None),
        P(("pages", "batch"), "tile", None),
        P("batch", "mp"),
        P("batch", None, "mp"),
        P("mp", "batch"),
        P("batch", "mp"),
        P("batch", None, "mp"),
        P("mp", "batch"),
    )
    return jax.shard_map(
        body,
        mesh=mesh,
        in_specs=placed,
        out_specs=(
            P(("pages", "batch"), "tile", None, None),
            P(("pages", "batch"), ("tile", "mp"), None),
        ),
        check_vma=False,
    )
```

```python
import functools
import math

import jax
import jax.numpy as jnp
from jax import lax
from jax.experimental import pallas as pl
from jax.experimental.pallas import tpu as pltpu
from jax.sharding import PartitionSpec as P

HEAD_ENC = 32
HEAD_DEC = 64
LANES = 128
VMEM_LIMIT = 48 << 20
F32 = jnp.float32
BF16 = jnp.bfloat16


def from_behind(value, axis, by):
    devices = lax.axis_size(axis)
    return lax.ppermute(value, axis, [(i, (i + by) % devices) for i in range(devices)])


def layer_norm(values):
    center = values - jnp.mean(values, axis=-1, keepdims=True)
    variance = jnp.mean(center * center, axis=-1, keepdims=True)
    return center / jnp.sqrt(variance + 1e-05)


def regions(length, window, offset):
    index_row = jnp.arange(length, dtype=jnp.int32)
    return jnp.where(
        index_row < length - window, 0, jnp.where(index_row < length - offset, 1, 2)
    ).astype(jnp.int32)


def general_body(
    page_cells, text_states, enc_query, enc_keyval, enc_proj, dec_query, dec_keyval, dec_out
):
    wq_enc, wkv_enc, wproj_enc, wq_dec, wkv_dec, wout_dec = (
        lax.all_gather(enc_query, "batch", axis=0, tiled=True),
        lax.all_gather(enc_keyval, "batch", axis=0, tiled=True),
        lax.all_gather(enc_proj, "batch", axis=1, tiled=True),
        lax.all_gather(dec_query, "batch", axis=0, tiled=True),
        lax.all_gather(dec_keyval, "batch", axis=0, tiled=True),
        lax.all_gather(dec_out, "batch", axis=1, tiled=True),
    )
    pages_here, window, columns, width = page_cells.shape
    offset = window // 2
    own_rows = window * columns
    hq_enc = wq_enc.shape[1]
    heads_enc = hq_enc // HEAD_ENC
    joined = jnp.concatenate([wq_enc, wkv_enc.reshape(width, 2 * hq_enc)], axis=1)
    rows_below = from_behind(page_cells[:, :offset], "tile", -1)
    normed = layer_norm(
        jnp.concatenate([page_cells[:, offset:], rows_below], axis=1).astype(F32)
    ).astype(BF16)
    projected = jnp.einsum("prcd,de->prce", normed, joined, preferred_element_type=F32).astype(BF16)
    projected = jnp.roll(projected, -offset, axis=2)
    per_row = columns // window
    shaped = projected.reshape(pages_here, window, per_row, window, 3, heads_enc, HEAD_ENC)
    shaped = jnp.swapaxes(shaped, 1, 2).reshape(
        pages_here, per_row, window * window, 3, heads_enc, HEAD_ENC
    )
    win_q = shaped[:, :, :, 0]
    win_k = shaped[:, :, :, 1]
    win_v = shaped[:, :, :, 2]
    is_last = lax.axis_index("tile") == lax.axis_size("tile") - 1
    local_rows = jnp.arange(window, dtype=jnp.int32)
    row_region = jnp.where(is_last, jnp.where(local_rows < window - offset, 1, 2), 0).astype(
        jnp.int32
    )
    labels = row_region[:, None] * 3 + regions(columns, window, offset)[None, :]
    labels = jnp.swapaxes(labels.reshape(window, per_row, window), 0, 1).reshape(
        per_row, window * window
    )
    allowed = labels[:, :, None] == labels[:, None, :]
    win_scores = jnp.einsum(
        "pnqhd,pnkhd->pnhqk", win_q, win_k, preferred_element_type=F32
    ) / math.sqrt(HEAD_ENC)
    win_scores = jnp.where(allowed[None, :, None], win_scores, -jnp.inf)
    top = jnp.max(win_scores, axis=-1, keepdims=True)
    expd = jnp.exp(win_scores - top)
    win_weights = (expd / jnp.sum(expd, axis=-1, keepdims=True)).astype(BF16)
    win_out = jnp.einsum(
        "pnhqk,pnkhd->pnqhd", win_weights, win_v, preferred_element_type=F32
    ).astype(BF16)
    win_out = win_out.reshape(pages_here, per_row, window, window, hq_enc)
    win_out = jnp.swapaxes(win_out, 1, 2).reshape(pages_here, window, columns, hq_enc)
    win_out = jnp.roll(win_out, offset, axis=2)
    rows_above = from_behind(win_out[:, window - offset :], "tile", 1)
    unrolled = jnp.concatenate([rows_above, win_out[:, : window - offset]], axis=1)
    partial_proj = jnp.einsum("prce,ed->prcd", unrolled, wproj_enc, preferred_element_type=F32)
    summed = lax.psum(partial_proj.astype(BF16), "mp").astype(F32)
    encoded = (page_cells.astype(F32) + summed).astype(BF16)
    hq_dec = wq_dec.shape[1]
    heads_dec = hq_dec // HEAD_DEC
    page_normed = (
        layer_norm(encoded.astype(F32)).astype(BF16).reshape(pages_here, own_rows, width)
    )
    page_kv = jnp.einsum(
        "pnd,de->pne", page_normed, wkv_dec.reshape(width, 2 * hq_dec), preferred_element_type=F32
    ).astype(BF16)
    text_normed = layer_norm(text_states.astype(F32)).astype(BF16)
    queries = jnp.einsum("ptd,de->pte", text_normed, wq_dec, preferred_element_type=F32).astype(
        BF16
    )
    text_len = text_states.shape[1]
    query_heads = queries.reshape(pages_here, text_len, heads_dec, HEAD_DEC)
    carried = (
        jnp.full((pages_here, heads_dec, text_len), -jnp.inf, F32),
        jnp.zeros((pages_here, heads_dec, text_len), F32),
        jnp.zeros((pages_here, heads_dec, text_len, HEAD_DEC), F32),
    )
    shard_rows = lax.all_gather(page_kv, "tile", axis=1, tiled=True)
    count = shard_rows.shape[1] // own_rows
    grouped = max(
        (
            factor
            for factor in range(1, count + 1)
            if count % factor == 0 and factor * own_rows <= 2048
        )
    )
    blocks = jnp.moveaxis(
        shard_rows.reshape(pages_here, count // grouped, grouped * own_rows, 2 * hq_dec), 1, 0
    )

    def advance(running, block_kv):
        maxima, totals, accum = running
        span = block_kv.shape[1]
        block_keys = block_kv[..., :hq_dec].reshape(pages_here, span, heads_dec, HEAD_DEC)
        block_vals = block_kv[..., hq_dec:].reshape(pages_here, span, heads_dec, HEAD_DEC)
        cross_scores = jnp.einsum(
            "pqhd,pkhd->phqk", query_heads, block_keys, preferred_element_type=F32
        ) / math.sqrt(HEAD_DEC)
        newest = jnp.maximum(maxima, jnp.max(cross_scores, axis=-1))
        rescale = jnp.exp(maxima - newest)
        expo = jnp.exp(cross_scores - newest[..., None])
        totals = totals * rescale + jnp.sum(expo, axis=-1)
        accum = accum * rescale[..., None] + jnp.einsum(
            "phqk,pkhd->phqd", expo.astype(BF16), block_vals, preferred_element_type=F32
        )
        return ((newest, totals, accum), None)

    carried, unused = lax.scan(advance, carried, blocks)
    maxima, totals, accum = carried
    context = (
        jnp.transpose(accum / totals[..., None], (0, 2, 1, 3))
        .reshape(pages_here, text_len, hq_dec)
        .astype(BF16)
    )
    share = text_len // lax.axis_size("mp")
    mixed = lax.psum_scatter(
        jnp.einsum("pte,ed->tpd", context, wout_dec, preferred_element_type=F32).astype(BF16),
        "mp",
        scatter_dimension=0,
        tiled=True,
    ).astype(F32)
    own_text = lax.dynamic_slice_in_dim(text_states, lax.axis_index("mp") * share, share, 1)
    decoded = (own_text.astype(F32) + jnp.moveaxis(mixed, 0, 1)).astype(BF16)
    return (encoded, decoded)


def swapped(value, axis):
    return lax.ppermute(value, axis, [(0, 1), (1, 0)])


def norm_rows(ref):
    v = ref[...].astype(F32)
    center = v - jnp.mean(v, axis=-1, keepdims=True)
    variance = jnp.mean(center * center, axis=-1, keepdims=True)
    return (center / jnp.sqrt(variance + 1e-05)).astype(BF16)


def halves(width):
    b = lax.axis_index("batch")
    half = width // 2
    own = pl.multiple_of(b * half, half)
    other = pl.multiple_of((1 - b) * half, half)
    return pl.ds(own, half), pl.ds(other, half)


def dot(a, b):
    return jnp.dot(a, b, preferred_element_type=F32)


def dot_t(a, b):
    return lax.dot_general(a, b, (((1,), (1,)), ((), ())), preferred_element_type=F32)


def lane_head(shape, size):
    return lax.broadcasted_iota(jnp.int32, shape, 1) // size


LOG2E = math.log2(math.e)
EXCLUDED = -1e30


def col_group(col, offset):
    window = 2 * offset
    return jnp.where(col < offset, 0, 1 + jnp.maximum(col - offset, 0) // window)


def attend_part(stacked, keys, values, head_of, scale):
    rows = head_of.shape[0]
    s = dot_t(stacked, keys)
    top = jnp.max(s, axis=-1, keepdims=True)
    o = dot(jnp.exp2((s - top) * scale).astype(BF16), values)
    acc, total, highest = None, None, None
    for h in range(stacked.shape[0] // rows):
        block = slice(h * rows, (h + 1) * rows)
        here = (o[block, :LANES], o[block, LANES:], jnp.broadcast_to(top[block], (rows, LANES)))
        if acc is None:
            acc, total, highest = here
        else:
            acc, total, highest = (
                jnp.where(head_of == h, new, old) for new, old in zip(here, (acc, total, highest))
            )
    return acc, total, highest


def merged(first, second, scale):
    acc_1, total_1, top_1 = first
    acc_2, total_2, top_2 = second
    top = jnp.maximum(top_1, top_2)
    keep_1 = jnp.exp2((top_1 - top) * scale)
    keep_2 = jnp.exp2((top_2 - top) * scale)
    return (acc_1 * keep_1 + acc_2 * keep_2) / (total_1 * keep_1 + total_2 * keep_2)


def stack_heads(stacked, q, head_of):
    rows = head_of.shape[0]
    for h in range(stacked.shape[0] // rows):
        stacked[h * rows : (h + 1) * rows, :LANES] = jnp.where(head_of == h, q, jnp.zeros_like(q))


def window_marks(rows, columns, offset, edge):
    groups = columns // (2 * offset) + 1
    lane = lax.broadcasted_iota(jnp.int32, (rows, LANES), 1)
    group = col_group(lax.broadcasted_iota(jnp.int32, (rows, LANES), 0) % columns, offset)
    out = jnp.logical_and(lane < groups, lane != group)
    if edge is not None:
        out = jnp.logical_or(out, jnp.logical_and(lane == groups, edge))
    k_marks = jnp.where(out, jnp.full((rows, LANES), EXCLUDED, F32), 0.0).astype(BF16)
    q_marks = jnp.where(jnp.logical_or(lane == group, lane == groups), 1.0, 0.0).astype(BF16)
    return q_marks, k_marks


def spread(kx, vx, kv, marks):
    rows = kx.shape[0]
    hq = kv.shape[1] // 2
    ones = jnp.ones((rows, LANES), BF16)
    for g in range(hq // LANES):
        cols = slice(g * LANES, (g + 1) * LANES)
        wide = slice(2 * g * LANES, (2 * g + 1) * LANES)
        extra = slice((2 * g + 1) * LANES, (2 * g + 2) * LANES)
        kx[:, wide] = kv[:, cols]
        kx[:, extra] = marks
        vx[:, wide] = kv[:, hq + g * LANES : hq + (g + 1) * LANES]
        vx[:, extra] = ones


def own_kernel(
    columns, page, wq_o, wq_x, wkv_o, wkv_x, q_out, acc, total, top, xn, kx, vx, ql
):
    rows = page.shape[0]
    half_rows = rows // 2
    hq = q_out.shape[1]
    own, other = halves(page.shape[1])
    xn[...] = norm_rows(page)
    q_out[...] = (dot(xn[:, own], wq_o[...]) + dot(xn[:, other], wq_x[...])).astype(BF16)
    kv = (dot(xn[:, own], wkv_o[...]) + dot(xn[:, other], wkv_x[...])).astype(BF16)
    offset = half_rows // columns
    spread(kx, vx, kv, window_marks(rows, columns, offset, None)[1])
    q_marks = window_marks(half_rows, columns, offset, None)[0]
    head_of = lane_head((half_rows, LANES), HEAD_ENC)
    scale = LOG2E / math.sqrt(HEAD_ENC)
    for h in range(LANES // HEAD_ENC):
        ql[h * half_rows : (h + 1) * half_rows, LANES:] = q_marks
    for half in range(2):
        here = slice(half * half_rows, (half + 1) * half_rows)
        for g in range(hq // LANES):
            cols = slice(g * LANES, (g + 1) * LANES)
            both = slice(2 * g * LANES, (2 * g + 2) * LANES)
            stack_heads(ql, q_out[here, cols], head_of)
            state = attend_part(ql[...], kx[here, both], vx[here, both], head_of, scale)
            acc[here, cols], total[here, cols], top[here, cols] = state


def win_kernel(
    columns, half, q_own, acc, total, top, halo, wkv_o, wkv_x, wp_o, wp_x, part, xn, kx, vx, ql, wo
):
    rows, width = halo.shape
    hq = q_own.shape[1]
    own, other = halves(width)
    xn[...] = norm_rows(halo)
    kv = (dot(xn[:, own], wkv_o[...]) + dot(xn[:, other], wkv_x[...])).astype(BF16)
    tile = lax.axis_index("tile")
    edge = tile == (0 if half == 0 else lax.axis_size("tile") - 1)
    q_marks, k_marks = window_marks(rows, columns, rows // columns, edge)
    spread(kx, vx, kv, k_marks)
    head_of = lane_head((rows, LANES), HEAD_ENC)
    scale = LOG2E / math.sqrt(HEAD_ENC)
    for h in range(LANES // HEAD_ENC):
        ql[h * rows : (h + 1) * rows, LANES:] = q_marks
    here = slice(half * rows, (half + 1) * rows)
    for g in range(hq // LANES):
        cols = slice(g * LANES, (g + 1) * LANES)
        both = slice(2 * g * LANES, (2 * g + 2) * LANES)
        stack_heads(ql, q_own[here, cols], head_of)
        state = attend_part(ql[...], kx[:, both], vx[:, both], head_of, scale)
        first = (acc[here, cols], total[here, cols], top[here, cols])
        wo[:, cols] = merged(first, state, scale).astype(BF16)
    part[:, own] = dot(wo[...], wp_o[...]).astype(BF16)
    part[:, other] = dot(wo[...], wp_x[...]).astype(BF16)


def pieces(scratch, first_col, outs, out_col):
    tiles = len(outs)
    tile = lax.axis_index("tile")
    for s in range(tiles):
        dest = lax.rem(tile + s, tiles)
        start = pl.multiple_of(dest * LANES + first_col, LANES)
        outs[s][:, out_col : out_col + LANES] = scratch[:, pl.ds(start, LANES)]


def kv_kernel(half, page, mine, theirs, wkv_o, wkv_x, encoded, *rest):
    outs, (xn, kvs) = rest[:-2], rest[-2:]
    rows, width = mine.shape
    own, other = halves(width)
    total = mine[...].astype(F32) + theirs[...].astype(F32)
    here = page[half * rows : (half + 1) * rows, :]
    encoded[...] = (here.astype(F32) + total).astype(BF16)
    xn[...] = norm_rows(encoded)
    kvs[...] = (dot(xn[:, own], wkv_o[...]) + dot(xn[:, other], wkv_x[...])).astype(BF16)
    pieces(kvs, 0, outs, 0)
    pieces(kvs, kvs.shape[1] // 2, outs, LANES)


def query_kernel(text, wq_o, wq_x, *rest):
    outs, (xn, qs) = rest[:-2], rest[-2:]
    own, other = halves(text.shape[1])
    xn[...] = norm_rows(text)
    qs[...] = (dot(xn[:, own], wq_o[...]) + dot(xn[:, other], wq_x[...])).astype(BF16)
    pieces(qs, 0, outs, 0)


def load_strips(kv_in, kv, sem):
    rows = kv_in[0].shape[0]
    copies = [
        pltpu.make_async_copy(
            strip, kv.at[pl.ds(s * rows, rows), pl.ds(0, 2 * LANES)], sem.at[s]
        )
        for s, strip in enumerate(kv_in)
    ]
    for copy in copies:
        copy.start()
    kv[:, 2 * LANES :] = jnp.ones((kv.shape[0], LANES), BF16)
    for copy in copies:
        copy.wait()


def cross_first_kernel(tiles, *refs):
    q_in = refs[:tiles]
    kv_in = refs[tiles : 2 * tiles]
    acc, total, top, kv, ql, sem = refs[2 * tiles :]
    load_strips(kv_in, kv, sem)
    tokens = q_in[0].shape[0]
    head_of = lane_head(q_in[0].shape, HEAD_DEC)
    scale = LOG2E / math.sqrt(HEAD_DEC)
    for s in range(tiles):
        here = slice(s * tokens, (s + 1) * tokens)
        stack_heads(ql, q_in[s][...], head_of)
        state = attend_part(ql[...], kv[:, :LANES], kv[:, LANES:], head_of, scale)
        acc[here], total[here], top[here] = state


def cross_kernel(first, count, tiles, *refs):
    q_in = refs[:count]
    kv_in = refs[count : count + tiles]
    acc, total, top, keep, send, kv, ql, ctx, sem = refs[count + tiles :]
    load_strips(kv_in, kv, sem)
    tokens = q_in[0].shape[0]
    head_of = lane_head(q_in[0].shape, HEAD_DEC)
    scale = LOG2E / math.sqrt(HEAD_DEC)
    half = tokens // 2
    m = lax.axis_index("mp")
    own_rows = pl.ds(pl.multiple_of(m * half, half), half)
    send_rows = pl.ds(pl.multiple_of((1 - m) * half, half), half)
    for s in range(count):
        here = slice((first + s) * tokens, (first + s + 1) * tokens)
        stack_heads(ql, q_in[s][...], head_of)
        state = attend_part(ql[...], kv[:, :LANES], kv[:, LANES:], head_of, scale)
        ctx[...] = merged((acc[here], total[here], top[here]), state, scale).astype(BF16)
        keep[s * half : (s + 1) * half] = ctx[own_rows, :]
        send[s * half : (s + 1) * half] = ctx[send_rows, :]


def out_kernel(tiles, *refs):
    ctx_in = refs[:tiles]
    w_own, w_batch, w_mp, w_both, text, decoded, ctx = refs[tiles:]
    half = decoded.shape[0]
    width = decoded.shape[1]
    own, other = halves(width)
    tile = lax.axis_index("tile")
    m = lax.axis_index("mp")
    own_rows = pl.ds(pl.multiple_of(m * half, half), half)
    for s in range(tiles):
        start = lax.rem(tile + s, tiles) * LANES
        here = pl.ds(pl.multiple_of(start, LANES), LANES)
        there = pl.ds(pl.multiple_of(tiles * LANES + start, LANES), LANES)
        ctx[:, here] = ctx_in[s][:half]
        ctx[:, there] = ctx_in[s][half:]
    mine = ctx[:, : tiles * LANES]
    theirs = ctx[:, tiles * LANES :]
    for cols, first, second in ((own, w_own, w_mp), (other, w_batch, w_both)):
        mixed = dot(mine, first[...]) + dot(theirs, second[...])
        decoded[:, cols] = (text[own_rows, cols].astype(F32) + mixed).astype(BF16)


VM = pl.BlockSpec(memory_space=pltpu.VMEM)
ANY = pl.BlockSpec(memory_space=pl.ANY)


def call(kernel, flops, outs, scratch, *args, specs=None):
    moved = sum(math.prod(a.shape) * 2 for a in args) + sum(math.prod(s) * 2 for s, _ in outs)
    return pl.pallas_call(
        kernel,
        out_shape=[jax.ShapeDtypeStruct(shape, dtype) for shape, dtype in outs],
        in_specs=specs or [VM] * len(args),
        out_specs=[VM] * len(outs),
        scratch_shapes=scratch,
        cost_estimate=pl.CostEstimate(flops=flops, transcendentals=0, bytes_accessed=moved)
        if flops
        else None,
        compiler_params=pltpu.CompilerParams(vmem_limit_bytes=VMEM_LIMIT),
    )(*args)


def after(value, *earlier):
    return lax.optimization_barrier((value,) + earlier)[0]


def body(page_cells, text_states, enc_query, enc_keyval, enc_proj, dec_query, dec_keyval, dec_out):
    tiles = lax.axis_size("tile")
    pages_here, window, columns, width = page_cells.shape
    hq_enc = enc_query.shape[1]
    hq_dec = dec_query.shape[1]
    if (
        pages_here != 1
        or lax.axis_size("batch") != 2
        or lax.axis_size("mp") != 2
        or hq_dec != tiles * LANES
        or hq_enc % LANES
    ):
        return general_body(
            page_cells, text_states, enc_query, enc_keyval, enc_proj, dec_query, dec_keyval, dec_out
        )
    rows = window * columns
    half_rows = rows // 2
    page = page_cells.reshape(rows, width)
    text = text_states.reshape(-1, width)
    tokens = text.shape[0]
    up = [(i, i + 1) for i in range(tiles - 1)]
    down = [(i + 1, i) for i in range(tiles - 1)]
    upper, lower = page[:half_rows], page[half_rows:]
    above = lax.ppermute(lower, "tile", up)
    below = lax.ppermute(upper, "tile", down)
    wkv_x = swapped(enc_keyval, "batch").reshape(width // 2, 2 * hq_enc)
    wkv_enc = enc_keyval.reshape(width // 2, 2 * hq_enc)
    wq_x = swapped(enc_query, "batch")
    dq_x = swapped(dec_query, "batch")
    dkv_x = swapped(dec_keyval, "batch").reshape(width // 2, 2 * hq_dec)
    wkv_dec = dec_keyval.reshape(width // 2, 2 * hq_dec)

    q_own, *win_state = call(
        functools.partial(own_kernel, columns),
        1,
        [((rows, hq_enc), BF16)] + [((rows, hq_enc), F32)] * 3,
        [
            pltpu.VMEM((rows, width), BF16),
            pltpu.VMEM((rows, 2 * hq_enc), BF16),
            pltpu.VMEM((rows, 2 * hq_enc), BF16),
            pltpu.VMEM((LANES // HEAD_ENC * half_rows, 2 * LANES), BF16),
        ],
        page,
        enc_query,
        wq_x,
        wkv_enc,
        wkv_x,
    )
    q_out = call(
        query_kernel,
        1,
        [((tokens, LANES), BF16)] * tiles,
        [pltpu.VMEM((tokens, width), BF16), pltpu.VMEM((tokens, hq_dec), BF16)],
        after(text, q_own),
        dec_query,
        dq_x,
    )
    q_in = [q_out[0]] + [from_behind(q_out[s], "tile", s) for s in range(1, tiles)]

    wp_x = swapped(enc_proj, "batch")

    def window_half(half, halo):
        (part,) = call(
            functools.partial(win_kernel, columns, half),
            2 * half_rows * width * 3 * hq_enc + 8 * half_rows * rows * LANES * hq_enc // HEAD_ENC,
            [((half_rows, width), BF16)],
            [
                pltpu.VMEM((half_rows, width), BF16),
                pltpu.VMEM((half_rows, 2 * hq_enc), BF16),
                pltpu.VMEM((half_rows, 2 * hq_enc), BF16),
                pltpu.VMEM((LANES // HEAD_ENC * half_rows, 2 * LANES), BF16),
                pltpu.VMEM((half_rows, hq_enc), BF16),
            ],
            q_own,
            *win_state,
            halo,
            wkv_enc,
            wkv_x,
            enc_proj,
            wp_x,
        )
        return part

    def key_values(half, part, theirs):
        return call(
            functools.partial(kv_kernel, half),
            2 * half_rows * width * 2 * hq_dec,
            [((half_rows, width), BF16)] + [((half_rows, 2 * LANES), BF16)] * tiles,
            [pltpu.VMEM((half_rows, width), BF16), pltpu.VMEM((half_rows, 2 * hq_dec), BF16)],
            page,
            part,
            theirs,
            wkv_dec,
            dkv_x,
        )

    part_a = window_half(0, above)
    theirs_a = swapped(part_a, "mp")
    part_b = window_half(1, after(below, part_a))
    theirs_b = swapped(part_b, "mp")
    encoded_a, *kv_a = key_values(0, part_a, theirs_a)
    kv_a = [kv_a[0]] + [from_behind(kv_a[s], "tile", s) for s in range(1, tiles)]
    theirs_b, kv_a, q_in = lax.optimization_barrier((theirs_b, kv_a, q_in))
    encoded_b, *kv_b = key_values(1, part_b, theirs_b)
    kv_b = [kv_b[0]] + [from_behind(kv_b[s], "tile", s) for s in range(1, tiles)]
    out_half = after(dec_out, encoded_a)
    do_x = swapped(out_half, "batch")
    do_m = swapped(out_half, "mp")
    do_mx = swapped(do_m, "batch")
    encoded = jnp.concatenate([encoded_a, encoded_b], axis=0)

    cross_scratch = [
        pltpu.VMEM((tiles * half_rows, 3 * LANES), BF16),
        pltpu.VMEM((LANES // HEAD_DEC * tokens, LANES), BF16),
    ]
    arrivals = pltpu.SemaphoreType.DMA((tiles,))
    cross_state = call(
        functools.partial(cross_first_kernel, tiles),
        1,
        [((tiles * tokens, LANES), F32)] * 3,
        cross_scratch + [arrivals],
        *q_in,
        *kv_a,
        specs=[VM] * tiles + [ANY] * tiles,
    )

    def attend(first, queries):
        count = len(queries)
        return call(
            functools.partial(cross_kernel, first, count, tiles),
            1,
            [((count * tokens // 2, LANES), BF16)] * 2,
            cross_scratch + [pltpu.VMEM((tokens, LANES), BF16), arrivals],
            *queries,
            *kv_b,
            *cross_state,
            specs=[VM] * count + [ANY] * tiles + [VM] * 3,
        )

    def joined(keep, other, index):
        span = slice(index * tokens // 2, (index + 1) * tokens // 2)
        return jnp.concatenate([keep[span], other[span]], axis=0)

    near = tiles // 2
    keep_far, send_far = attend(near, q_in[near:])
    other_far = swapped(send_far, "mp")
    keep_near, send_near = attend(0, [after(q_in[0], keep_far), *q_in[1:near]])
    other_near = swapped(send_near, "mp")
    ctx_in = [joined(keep_near, other_near, 0)]
    for s in range(1, near):
        ctx_in.append(from_behind(joined(keep_near, other_near, s), "tile", -s))
    for s in range(near, tiles):
        ctx_in.append(from_behind(joined(keep_far, other_far, s - near), "tile", -s))

    (decoded,) = call(
        functools.partial(out_kernel, tiles),
        2 * tokens * hq_dec * width,
        [((tokens // 2, width), BF16)],
        [pltpu.VMEM((tokens // 2, 2 * hq_dec), BF16)],
        *ctx_in,
        dec_out,
        do_x,
        do_m,
        do_mx,
        text,
    )
    return (
        encoded.reshape(page_cells.shape),
        decoded.reshape(1, tokens // 2, width),
    )


def solution(mesh):
    placed = (
        P(("pages", "batch"), "tile", None, None),
        P(("pages", "batch"), "tile", None),
        P("batch", "mp"),
        P("batch", None, "mp"),
        P("mp", "batch"),
        P("batch", "mp"),
        P("batch", None, "mp"),
        P("mp", "batch"),
    )
    return jax.shard_map(
        body,
        mesh=mesh,
        in_specs=placed,
        out_specs=(
            P(("pages", "batch"), "tile", None, None),
            P(("pages", "batch"), ("tile", "mp"), None),
        ),
        check_vma=False,
    )
```

```python
import functools
import math

import jax
import jax.numpy as jnp
from jax import lax
from jax.experimental import pallas as pl
from jax.experimental.pallas import tpu as pltpu
from jax.sharding import PartitionSpec as P

HEAD_ENC = 32
HEAD_DEC = 64
LANES = 128
VMEM_LIMIT = 48 << 20
F32 = jnp.float32
BF16 = jnp.bfloat16


def from_behind(value, axis, by):
    devices = lax.axis_size(axis)
    return lax.ppermute(value, axis, [(i, (i + by) % devices) for i in range(devices)])


def layer_norm(values):
    center = values - jnp.mean(values, axis=-1, keepdims=True)
    variance = jnp.mean(center * center, axis=-1, keepdims=True)
    return center / jnp.sqrt(variance + 1e-05)


def regions(length, window, offset):
    index_row = jnp.arange(length, dtype=jnp.int32)
    return jnp.where(
        index_row < length - window, 0, jnp.where(index_row < length - offset, 1, 2)
    ).astype(jnp.int32)


def general_body(
    page_cells, text_states, enc_query, enc_keyval, enc_proj, dec_query, dec_keyval, dec_out
):
    wq_enc, wkv_enc, wproj_enc, wq_dec, wkv_dec, wout_dec = (
        lax.all_gather(enc_query, "batch", axis=0, tiled=True),
        lax.all_gather(enc_keyval, "batch", axis=0, tiled=True),
        lax.all_gather(enc_proj, "batch", axis=1, tiled=True),
        lax.all_gather(dec_query, "batch", axis=0, tiled=True),
        lax.all_gather(dec_keyval, "batch", axis=0, tiled=True),
        lax.all_gather(dec_out, "batch", axis=1, tiled=True),
    )
    pages_here, window, columns, width = page_cells.shape
    offset = window // 2
    own_rows = window * columns
    hq_enc = wq_enc.shape[1]
    heads_enc = hq_enc // HEAD_ENC
    joined = jnp.concatenate([wq_enc, wkv_enc.reshape(width, 2 * hq_enc)], axis=1)
    rows_below = from_behind(page_cells[:, :offset], "tile", -1)
    normed = layer_norm(
        jnp.concatenate([page_cells[:, offset:], rows_below], axis=1).astype(F32)
    ).astype(BF16)
    projected = jnp.einsum("prcd,de->prce", normed, joined, preferred_element_type=F32).astype(BF16)
    projected = jnp.roll(projected, -offset, axis=2)
    per_row = columns // window
    shaped = projected.reshape(pages_here, window, per_row, window, 3, heads_enc, HEAD_ENC)
    shaped = jnp.swapaxes(shaped, 1, 2).reshape(
        pages_here, per_row, window * window, 3, heads_enc, HEAD_ENC
    )
    win_q = shaped[:, :, :, 0]
    win_k = shaped[:, :, :, 1]
    win_v = shaped[:, :, :, 2]
    is_last = lax.axis_index("tile") == lax.axis_size("tile") - 1
    local_rows = jnp.arange(window, dtype=jnp.int32)
    row_region = jnp.where(is_last, jnp.where(local_rows < window - offset, 1, 2), 0).astype(
        jnp.int32
    )
    labels = row_region[:, None] * 3 + regions(columns, window, offset)[None, :]
    labels = jnp.swapaxes(labels.reshape(window, per_row, window), 0, 1).reshape(
        per_row, window * window
    )
    allowed = labels[:, :, None] == labels[:, None, :]
    win_scores = jnp.einsum(
        "pnqhd,pnkhd->pnhqk", win_q, win_k, preferred_element_type=F32
    ) / math.sqrt(HEAD_ENC)
    win_scores = jnp.where(allowed[None, :, None], win_scores, -jnp.inf)
    top = jnp.max(win_scores, axis=-1, keepdims=True)
    expd = jnp.exp(win_scores - top)
    win_weights = (expd / jnp.sum(expd, axis=-1, keepdims=True)).astype(BF16)
    win_out = jnp.einsum(
        "pnhqk,pnkhd->pnqhd", win_weights, win_v, preferred_element_type=F32
    ).astype(BF16)
    win_out = win_out.reshape(pages_here, per_row, window, window, hq_enc)
    win_out = jnp.swapaxes(win_out, 1, 2).reshape(pages_here, window, columns, hq_enc)
    win_out = jnp.roll(win_out, offset, axis=2)
    rows_above = from_behind(win_out[:, window - offset :], "tile", 1)
    unrolled = jnp.concatenate([rows_above, win_out[:, : window - offset]], axis=1)
    partial_proj = jnp.einsum("prce,ed->prcd", unrolled, wproj_enc, preferred_element_type=F32)
    summed = lax.psum(partial_proj.astype(BF16), "mp").astype(F32)
    encoded = (page_cells.astype(F32) + summed).astype(BF16)
    hq_dec = wq_dec.shape[1]
    heads_dec = hq_dec // HEAD_DEC
    page_normed = (
        layer_norm(encoded.astype(F32)).astype(BF16).reshape(pages_here, own_rows, width)
    )
    page_kv = jnp.einsum(
        "pnd,de->pne", page_normed, wkv_dec.reshape(width, 2 * hq_dec), preferred_element_type=F32
    ).astype(BF16)
    text_normed = layer_norm(text_states.astype(F32)).astype(BF16)
    queries = jnp.einsum("ptd,de->pte", text_normed, wq_dec, preferred_element_type=F32).astype(
        BF16
    )
    text_len = text_states.shape[1]
    query_heads = queries.reshape(pages_here, text_len, heads_dec, HEAD_DEC)
    carried = (
        jnp.full((pages_here, heads_dec, text_len), -jnp.inf, F32),
        jnp.zeros((pages_here, heads_dec, text_len), F32),
        jnp.zeros((pages_here, heads_dec, text_len, HEAD_DEC), F32),
    )
    shard_rows = lax.all_gather(page_kv, "tile", axis=1, tiled=True)
    count = shard_rows.shape[1] // own_rows
    grouped = max(
        (
            factor
            for factor in range(1, count + 1)
            if count % factor == 0 and factor * own_rows <= 2048
        )
    )
    blocks = jnp.moveaxis(
        shard_rows.reshape(pages_here, count // grouped, grouped * own_rows, 2 * hq_dec), 1, 0
    )

    def advance(running, block_kv):
        maxima, totals, accum = running
        span = block_kv.shape[1]
        block_keys = block_kv[..., :hq_dec].reshape(pages_here, span, heads_dec, HEAD_DEC)
        block_vals = block_kv[..., hq_dec:].reshape(pages_here, span, heads_dec, HEAD_DEC)
        cross_scores = jnp.einsum(
            "pqhd,pkhd->phqk", query_heads, block_keys, preferred_element_type=F32
        ) / math.sqrt(HEAD_DEC)
        newest = jnp.maximum(maxima, jnp.max(cross_scores, axis=-1))
        rescale = jnp.exp(maxima - newest)
        expo = jnp.exp(cross_scores - newest[..., None])
        totals = totals * rescale + jnp.sum(expo, axis=-1)
        accum = accum * rescale[..., None] + jnp.einsum(
            "phqk,pkhd->phqd", expo.astype(BF16), block_vals, preferred_element_type=F32
        )
        return ((newest, totals, accum), None)

    carried, unused = lax.scan(advance, carried, blocks)
    maxima, totals, accum = carried
    context = (
        jnp.transpose(accum / totals[..., None], (0, 2, 1, 3))
        .reshape(pages_here, text_len, hq_dec)
        .astype(BF16)
    )
    share = text_len // lax.axis_size("mp")
    mixed = lax.psum_scatter(
        jnp.einsum("pte,ed->tpd", context, wout_dec, preferred_element_type=F32).astype(BF16),
        "mp",
        scatter_dimension=0,
        tiled=True,
    ).astype(F32)
    own_text = lax.dynamic_slice_in_dim(text_states, lax.axis_index("mp") * share, share, 1)
    decoded = (own_text.astype(F32) + jnp.moveaxis(mixed, 0, 1)).astype(BF16)
    return (encoded, decoded)


def swapped(value, axis):
    return lax.ppermute(value, axis, [(0, 1), (1, 0)])


def norm_rows(ref):
    v = ref[...].astype(F32)
    center = v - jnp.mean(v, axis=-1, keepdims=True)
    variance = jnp.mean(center * center, axis=-1, keepdims=True)
    return (center / jnp.sqrt(variance + 1e-05)).astype(BF16)


def halves(width):
    b = lax.axis_index("batch")
    half = width // 2
    own = pl.multiple_of(b * half, half)
    other = pl.multiple_of((1 - b) * half, half)
    return pl.ds(own, half), pl.ds(other, half)


def dot(a, b):
    return jnp.dot(a, b, preferred_element_type=F32)


def dot_t(a, b):
    return lax.dot_general(a, b, (((1,), (1,)), ((), ())), preferred_element_type=F32)


def lane_head(shape, size):
    return lax.broadcasted_iota(jnp.int32, shape, 1) // size


LOG2E = math.log2(math.e)
EXCLUDED = -1e30


def col_group(col, offset):
    window = 2 * offset
    return jnp.where(col < offset, 0, 1 + jnp.maximum(col - offset, 0) // window)


def attend_part(stacked, keys, values, head_of, scale):
    rows = head_of.shape[0]
    s = dot_t(stacked, keys)
    top = jnp.max(s, axis=-1, keepdims=True)
    o = dot(jnp.exp2((s - top) * scale).astype(BF16), values)
    acc, total, highest = None, None, None
    for h in range(stacked.shape[0] // rows):
        block = slice(h * rows, (h + 1) * rows)
        here = (o[block, :LANES], o[block, LANES:], jnp.broadcast_to(top[block], (rows, LANES)))
        if acc is None:
            acc, total, highest = here
        else:
            acc, total, highest = (
                jnp.where(head_of == h, new, old) for new, old in zip(here, (acc, total, highest))
            )
    return acc, total, highest


def merged(first, second, scale):
    acc_1, total_1, top_1 = first
    acc_2, total_2, top_2 = second
    top = jnp.maximum(top_1, top_2)
    keep_1 = jnp.exp2((top_1 - top) * scale)
    keep_2 = jnp.exp2((top_2 - top) * scale)
    return (acc_1 * keep_1 + acc_2 * keep_2) / (total_1 * keep_1 + total_2 * keep_2)


def stack_heads(stacked, q, head_of):
    rows = head_of.shape[0]
    for h in range(stacked.shape[0] // rows):
        stacked[h * rows : (h + 1) * rows, :LANES] = jnp.where(head_of == h, q, jnp.zeros_like(q))


def window_marks(rows, columns, offset, edge):
    groups = columns // (2 * offset) + 1
    lane = lax.broadcasted_iota(jnp.int32, (rows, LANES), 1)
    group = col_group(lax.broadcasted_iota(jnp.int32, (rows, LANES), 0) % columns, offset)
    out = jnp.logical_and(lane < groups, lane != group)
    if edge is not None:
        out = jnp.logical_or(out, jnp.logical_and(lane == groups, edge))
    k_marks = jnp.where(out, jnp.full((rows, LANES), EXCLUDED, F32), 0.0).astype(BF16)
    q_marks = jnp.where(jnp.logical_or(lane == group, lane == groups), 1.0, 0.0).astype(BF16)
    return q_marks, k_marks


def spread(kx, vx, kv, marks):
    rows = kx.shape[0]
    hq = kv.shape[1] // 2
    ones = jnp.ones((rows, LANES), BF16)
    for g in range(hq // LANES):
        cols = slice(g * LANES, (g + 1) * LANES)
        wide = slice(2 * g * LANES, (2 * g + 1) * LANES)
        extra = slice((2 * g + 1) * LANES, (2 * g + 2) * LANES)
        kx[:, wide] = kv[:, cols]
        kx[:, extra] = marks
        vx[:, wide] = kv[:, hq + g * LANES : hq + (g + 1) * LANES]
        vx[:, extra] = ones


def own_kernel(
    columns, page, wq_o, wq_x, wkv_o, wkv_x, q_out, acc, total, top, xn, kx, vx, ql
):
    rows = page.shape[0]
    half_rows = rows // 2
    hq = q_out.shape[1]
    own, other = halves(page.shape[1])
    xn[...] = norm_rows(page)
    q_out[...] = (dot(xn[:, own], wq_o[...]) + dot(xn[:, other], wq_x[...])).astype(BF16)
    kv = (dot(xn[:, own], wkv_o[...]) + dot(xn[:, other], wkv_x[...])).astype(BF16)
    offset = half_rows // columns
    spread(kx, vx, kv, window_marks(rows, columns, offset, None)[1])
    q_marks = window_marks(half_rows, columns, offset, None)[0]
    head_of = lane_head((half_rows, LANES), HEAD_ENC)
    scale = LOG2E / math.sqrt(HEAD_ENC)
    for h in range(LANES // HEAD_ENC):
        ql[h * half_rows : (h + 1) * half_rows, LANES:] = q_marks
    for half in range(2):
        here = slice(half * half_rows, (half + 1) * half_rows)
        for g in range(hq // LANES):
            cols = slice(g * LANES, (g + 1) * LANES)
            both = slice(2 * g * LANES, (2 * g + 2) * LANES)
            stack_heads(ql, q_out[here, cols], head_of)
            state = attend_part(ql[...], kx[here, both], vx[here, both], head_of, scale)
            acc[here, cols], total[here, cols], top[here, cols] = state


def win_kernel(
    columns, half, q_own, acc, total, top, halo, wkv_o, wkv_x, wp_o, wp_x, part, xn, kx, vx, ql, wo
):
    rows, width = halo.shape
    hq = q_own.shape[1]
    own, other = halves(width)
    xn[...] = norm_rows(halo)
    kv = (dot(xn[:, own], wkv_o[...]) + dot(xn[:, other], wkv_x[...])).astype(BF16)
    tile = lax.axis_index("tile")
    edge = tile == (0 if half == 0 else lax.axis_size("tile") - 1)
    q_marks, k_marks = window_marks(rows, columns, rows // columns, edge)
    spread(kx, vx, kv, k_marks)
    head_of = lane_head((rows, LANES), HEAD_ENC)
    scale = LOG2E / math.sqrt(HEAD_ENC)
    for h in range(LANES // HEAD_ENC):
        ql[h * rows : (h + 1) * rows, LANES:] = q_marks
    here = slice(half * rows, (half + 1) * rows)
    for g in range(hq // LANES):
        cols = slice(g * LANES, (g + 1) * LANES)
        both = slice(2 * g * LANES, (2 * g + 2) * LANES)
        stack_heads(ql, q_own[here, cols], head_of)
        state = attend_part(ql[...], kx[:, both], vx[:, both], head_of, scale)
        first = (acc[here, cols], total[here, cols], top[here, cols])
        wo[:, cols] = merged(first, state, scale).astype(BF16)
    part[:, own] = dot(wo[...], wp_o[...]).astype(BF16)
    part[:, other] = dot(wo[...], wp_x[...]).astype(BF16)


def pieces(scratch, first_col, outs, out_col):
    tiles = len(outs)
    tile = lax.axis_index("tile")
    for s in range(tiles):
        dest = lax.rem(tile + s, tiles)
        start = pl.multiple_of(dest * LANES + first_col, LANES)
        outs[s][:, out_col : out_col + LANES] = scratch[:, pl.ds(start, LANES)]


def kv_kernel(half, page, mine, theirs, wkv_o, wkv_x, encoded, *rest):
    outs, (xn, kvs) = rest[:-2], rest[-2:]
    rows, width = mine.shape
    own, other = halves(width)
    total = mine[...].astype(F32) + theirs[...].astype(F32)
    here = page[half * rows : (half + 1) * rows, :]
    encoded[...] = (here.astype(F32) + total).astype(BF16)
    xn[...] = norm_rows(encoded)
    kvs[...] = (dot(xn[:, own], wkv_o[...]) + dot(xn[:, other], wkv_x[...])).astype(BF16)
    pieces(kvs, 0, outs, 0)
    pieces(kvs, kvs.shape[1] // 2, outs, LANES)


def query_kernel(text, wq_o, wq_x, *rest):
    outs, (xn, qs) = rest[:-2], rest[-2:]
    own, other = halves(text.shape[1])
    xn[...] = norm_rows(text)
    qs[...] = (dot(xn[:, own], wq_o[...]) + dot(xn[:, other], wq_x[...])).astype(BF16)
    pieces(qs, 0, outs, 0)


def load_strips(kv_in, kv, sem):
    rows = kv_in[0].shape[0]
    copies = [
        pltpu.make_async_copy(
            strip, kv.at[pl.ds(s * rows, rows), pl.ds(0, 2 * LANES)], sem.at[s]
        )
        for s, strip in enumerate(kv_in)
    ]
    for copy in copies:
        copy.start()
    kv[:, 2 * LANES :] = jnp.ones((kv.shape[0], LANES), BF16)
    for copy in copies:
        copy.wait()


def cross_first_kernel(tiles, *refs):
    q_in = refs[:tiles]
    kv_in = refs[tiles : 2 * tiles]
    acc, total, top, kv, ql, sem = refs[2 * tiles :]
    load_strips(kv_in, kv, sem)
    tokens = q_in[0].shape[0]
    head_of = lane_head(q_in[0].shape, HEAD_DEC)
    scale = LOG2E / math.sqrt(HEAD_DEC)
    for s in range(tiles):
        here = slice(s * tokens, (s + 1) * tokens)
        stack_heads(ql, q_in[s][...], head_of)
        state = attend_part(ql[...], kv[:, :LANES], kv[:, LANES:], head_of, scale)
        acc[here], total[here], top[here] = state


def cross_kernel(first, count, tiles, *refs):
    q_in = refs[:count]
    kv_in = refs[count : count + tiles]
    acc, total, top, keep, send, kv, ql, ctx, sem = refs[count + tiles :]
    load_strips(kv_in, kv, sem)
    tokens = q_in[0].shape[0]
    head_of = lane_head(q_in[0].shape, HEAD_DEC)
    scale = LOG2E / math.sqrt(HEAD_DEC)
    half = tokens // 2
    m = lax.axis_index("mp")
    own_rows = pl.ds(pl.multiple_of(m * half, half), half)
    send_rows = pl.ds(pl.multiple_of((1 - m) * half, half), half)
    for s in range(count):
        here = slice((first + s) * tokens, (first + s + 1) * tokens)
        stack_heads(ql, q_in[s][...], head_of)
        state = attend_part(ql[...], kv[:, :LANES], kv[:, LANES:], head_of, scale)
        ctx[...] = merged((acc[here], total[here], top[here]), state, scale).astype(BF16)
        keep[s * half : (s + 1) * half] = ctx[own_rows, :]
        send[s * half : (s + 1) * half] = ctx[send_rows, :]


def out_kernel(tiles, *refs):
    ctx_in = refs[:tiles]
    w_own, w_batch, w_mp, w_both, text, decoded, ctx = refs[tiles:]
    half = decoded.shape[0]
    width = decoded.shape[1]
    own, other = halves(width)
    tile = lax.axis_index("tile")
    m = lax.axis_index("mp")
    own_rows = pl.ds(pl.multiple_of(m * half, half), half)
    for s in range(tiles):
        start = lax.rem(tile + s, tiles) * LANES
        here = pl.ds(pl.multiple_of(start, LANES), LANES)
        there = pl.ds(pl.multiple_of(tiles * LANES + start, LANES), LANES)
        ctx[:, here] = ctx_in[s][:half]
        ctx[:, there] = ctx_in[s][half:]
    mine = ctx[:, : tiles * LANES]
    theirs = ctx[:, tiles * LANES :]
    for cols, first, second in ((own, w_own, w_mp), (other, w_batch, w_both)):
        mixed = dot(mine, first[...]) + dot(theirs, second[...])
        decoded[:, cols] = (text[own_rows, cols].astype(F32) + mixed).astype(BF16)


VM = pl.BlockSpec(memory_space=pltpu.VMEM)
ANY = pl.BlockSpec(memory_space=pl.ANY)


def call(kernel, flops, outs, scratch, *args, specs=None):
    moved = sum(math.prod(a.shape) * 2 for a in args) + sum(math.prod(s) * 2 for s, _ in outs)
    return pl.pallas_call(
        kernel,
        out_shape=[jax.ShapeDtypeStruct(shape, dtype) for shape, dtype in outs],
        in_specs=specs or [VM] * len(args),
        out_specs=[VM] * len(outs),
        scratch_shapes=scratch,
        cost_estimate=pl.CostEstimate(flops=flops, transcendentals=0, bytes_accessed=moved)
        if flops
        else None,
        compiler_params=pltpu.CompilerParams(vmem_limit_bytes=VMEM_LIMIT),
    )(*args)


def after(value, *earlier):
    return lax.optimization_barrier((value,) + earlier)[0]


def body(page_cells, text_states, enc_query, enc_keyval, enc_proj, dec_query, dec_keyval, dec_out):
    tiles = lax.axis_size("tile")
    pages_here, window, columns, width = page_cells.shape
    hq_enc = enc_query.shape[1]
    hq_dec = dec_query.shape[1]
    if (
        pages_here != 1
        or lax.axis_size("batch") != 2
        or lax.axis_size("mp") != 2
        or hq_dec != tiles * LANES
        or hq_enc % LANES
    ):
        return general_body(
            page_cells, text_states, enc_query, enc_keyval, enc_proj, dec_query, dec_keyval, dec_out
        )
    rows = window * columns
    half_rows = rows // 2
    page = page_cells.reshape(rows, width)
    text = text_states.reshape(-1, width)
    tokens = text.shape[0]
    up = [(i, i + 1) for i in range(tiles - 1)]
    down = [(i + 1, i) for i in range(tiles - 1)]
    upper, lower = page[:half_rows], page[half_rows:]
    above = lax.ppermute(lower, "tile", up)
    below = lax.ppermute(upper, "tile", down)
    wkv_x = swapped(enc_keyval, "batch").reshape(width // 2, 2 * hq_enc)
    wkv_enc = enc_keyval.reshape(width // 2, 2 * hq_enc)
    wq_x = swapped(enc_query, "batch")
    dkv_x = swapped(dec_keyval, "batch").reshape(width // 2, 2 * hq_dec)
    wkv_dec = dec_keyval.reshape(width // 2, 2 * hq_dec)

    q_own, *win_state = call(
        functools.partial(own_kernel, columns),
        1,
        [((rows, hq_enc), BF16)] + [((rows, hq_enc), F32)] * 3,
        [
            pltpu.VMEM((rows, width), BF16),
            pltpu.VMEM((rows, 2 * hq_enc), BF16),
            pltpu.VMEM((rows, 2 * hq_enc), BF16),
            pltpu.VMEM((LANES // HEAD_ENC * half_rows, 2 * LANES), BF16),
        ],
        page,
        enc_query,
        wq_x,
        wkv_enc,
        wkv_x,
    )
    dq_x = swapped(after(dec_query, q_own), "batch")
    q_out = call(
        query_kernel,
        1,
        [((tokens, LANES), BF16)] * tiles,
        [pltpu.VMEM((tokens, width), BF16), pltpu.VMEM((tokens, hq_dec), BF16)],
        after(text, q_own),
        dec_query,
        dq_x,
    )
    q_in = [q_out[0]] + [from_behind(q_out[s], "tile", s) for s in range(1, tiles)]

    wp_x = swapped(enc_proj, "batch")

    def window_half(half, halo):
        (part,) = call(
            functools.partial(win_kernel, columns, half),
            2 * half_rows * width * 3 * hq_enc + 8 * half_rows * rows * LANES * hq_enc // HEAD_ENC,
            [((half_rows, width), BF16)],
            [
                pltpu.VMEM((half_rows, width), BF16),
                pltpu.VMEM((half_rows, 2 * hq_enc), BF16),
                pltpu.VMEM((half_rows, 2 * hq_enc), BF16),
                pltpu.VMEM((LANES // HEAD_ENC * half_rows, 2 * LANES), BF16),
                pltpu.VMEM((half_rows, hq_enc), BF16),
            ],
            q_own,
            *win_state,
            halo,
            wkv_enc,
            wkv_x,
            enc_proj,
            wp_x,
        )
        return part

    def key_values(half, part, theirs):
        return call(
            functools.partial(kv_kernel, half),
            2 * half_rows * width * 2 * hq_dec,
            [((half_rows, width), BF16)] + [((half_rows, 2 * LANES), BF16)] * tiles,
            [pltpu.VMEM((half_rows, width), BF16), pltpu.VMEM((half_rows, 2 * hq_dec), BF16)],
            page,
            part,
            theirs,
            wkv_dec,
            dkv_x,
        )

    part_a = window_half(0, above)
    theirs_a = swapped(part_a, "mp")
    part_b = window_half(1, after(below, part_a))
    theirs_b = swapped(part_b, "mp")
    encoded_a, *kv_a = key_values(0, part_a, after(theirs_a, *q_out))
    kv_a = [kv_a[0]] + [from_behind(kv_a[s], "tile", s) for s in range(1, tiles)]
    theirs_b, kv_a, q_in = lax.optimization_barrier((theirs_b, kv_a, q_in))
    encoded_b, *kv_b = key_values(1, part_b, theirs_b)
    kv_b = [kv_b[0]] + [from_behind(kv_b[s], "tile", s) for s in range(1, tiles)]
    out_half = after(dec_out, encoded_a)
    do_x = swapped(out_half, "batch")
    do_m = swapped(out_half, "mp")
    do_mx = swapped(do_m, "batch")
    encoded = jnp.concatenate([encoded_a, encoded_b], axis=0)

    cross_scratch = [
        pltpu.VMEM((tiles * half_rows, 3 * LANES), BF16),
        pltpu.VMEM((LANES // HEAD_DEC * tokens, LANES), BF16),
    ]
    arrivals = pltpu.SemaphoreType.DMA((tiles,))
    cross_state = call(
        functools.partial(cross_first_kernel, tiles),
        1,
        [((tiles * tokens, LANES), F32)] * 3,
        cross_scratch + [arrivals],
        *q_in,
        *kv_a,
        specs=[VM] * tiles + [ANY] * tiles,
    )

    def attend(first, queries):
        count = len(queries)
        return call(
            functools.partial(cross_kernel, first, count, tiles),
            1,
            [((count * tokens // 2, LANES), BF16)] * 2,
            cross_scratch + [pltpu.VMEM((tokens, LANES), BF16), arrivals],
            *queries,
            *kv_b,
            *cross_state,
            specs=[VM] * count + [ANY] * tiles + [VM] * 3,
        )

    def joined(keep, other, index):
        span = slice(index * tokens // 2, (index + 1) * tokens // 2)
        return jnp.concatenate([keep[span], other[span]], axis=0)

    near = tiles // 2
    keep_far, send_far = attend(near, q_in[near:])
    other_far = swapped(send_far, "mp")
    keep_near, send_near = attend(0, [after(q_in[0], keep_far), *q_in[1:near]])
    other_near = swapped(send_near, "mp")
    ctx_in = [joined(keep_near, other_near, 0)]
    for s in range(1, near):
        ctx_in.append(from_behind(joined(keep_near, other_near, s), "tile", -s))
    for s in range(near, tiles):
        ctx_in.append(from_behind(joined(keep_far, other_far, s - near), "tile", -s))

    (decoded,) = call(
        functools.partial(out_kernel, tiles),
        2 * tokens * hq_dec * width,
        [((tokens // 2, width), BF16)],
        [pltpu.VMEM((tokens // 2, 2 * hq_dec), BF16)],
        *ctx_in,
        dec_out,
        do_x,
        do_m,
        do_mx,
        text,
    )
    return (
        encoded.reshape(page_cells.shape),
        decoded.reshape(1, tokens // 2, width),
    )


def solution(mesh):
    placed = (
        P(("pages", "batch"), "tile", None, None),
        P(("pages", "batch"), "tile", None),
        P("batch", "mp"),
        P("batch", None, "mp"),
        P("mp", "batch"),
        P("batch", "mp"),
        P("batch", None, "mp"),
        P("mp", "batch"),
    )
    return jax.shard_map(
        body,
        mesh=mesh,
        in_specs=placed,
        out_specs=(
            P(("pages", "batch"), "tile", None, None),
            P(("pages", "batch"), ("tile", "mp"), None),
        ),
        check_vma=False,
    )
```
